256 devices in a mesh: pipe: 4 (over z_lo), expert: 64 (over x, z_hi, y, core).
Axes of the slice: x: 4, y: 4, z: 8 (z_hi: 2, z_lo: 4; z = z_hi * 4 + z_lo), core: 2. Of those that a mesh axis runs over, the one named last changes fastest.
Arguments:
- forward_input: bfloat16 [4, 8192, 2048], P('pipe', 'expert'), may hold values from -6 to 6
- queries: bfloat16 [4, 8192, 2048], P('pipe', 'expert'), may hold values from -100 to 100
- new_keys: bfloat16 [4, 8192, 256], P('pipe', 'expert'), may hold values from -6 to 6
- new_values: bfloat16 [4, 8192, 256], P('pipe', 'expert'), may hold values from -6 to 6
- cache_keys: bfloat16 [4, 8192, 256], P('pipe', 'expert'), may hold values from -6 to 6
- cache_values: bfloat16 [4, 8192, 256], P('pipe', 'expert'), may hold values from -6 to 6
- context_lengths: int32 [4, 64], P('pipe', 'expert'), may hold values from 1 to 128
- norm_gain: float32 [4, 2048], P('pipe'), may hold values from 0.5 to 1.5
- router: bfloat16 [4, 2048, 64], P('pipe'), may hold values from -0.125 to 0.125
- gate_weight: bfloat16 [4, 64, 2048, 768], P('pipe', 'expert'), may hold values from -0.125 to 0.125
- up_weight: bfloat16 [4, 64, 2048, 768], P('pipe', 'expert'), may hold values from -0.125 to 0.125
- down_weight: bfloat16 [4, 64, 768, 2048], P('pipe', 'expert'), may hold values from -0.21875 to 0.21875
- forward_ids: int32 [4, 8192, 4], P('pipe', 'expert'), may hold values from 0 to 63, all different within a row; in each aligned block of 128 rows (0 to 127, 128 to 255, ..., all dimensions but the last counted through in order) at most 9 rows name the same one
- backward_input: bfloat16 [4, 8192, 2048], P('pipe', 'expert'), may hold values from -6 to 6
- backward_ids: int32 [4, 8192, 4], P('pipe', 'expert'), may hold values from 0 to 63, all different within a row; in each aligned block of 128 rows (0 to 127, 128 to 255, ..., all dimensions but the last counted through in order) at most 9 rows name the same one
- output_grad: bfloat16 [4, 8192, 2048], P('pipe', 'expert'), may hold values from -16 to 16
Outputs:
- forward_output: bfloat16 [4, 8192, 2048], P('pipe', 'expert')
- input_grad: bfloat16 [4, 8192, 2048], P('pipe', 'expert')
- router_grad: float32 [4, 2048, 64], P('pipe', 'expert')
- gain_grad: float32 [4, 2048], P('pipe', 'expert')
The draws below stay inside these ranges and needn't reach their ends.
Inputs may be any that keep to these rules, and one draw needn't show every extreme that they name: `forward_ids`: each row names 4 different experts; in the 128 rows of one device no expert is named more than 9 times, and on some devices one is named exactly 9 times. `backward_ids`: each row names 4 different experts; in the 128 rows of one device no expert is named more than 9 times, and on some devices one is named exactly 9 times.
All inputs are finite; a program needn't handle non-finite values.
Results may differ from the reference program's by a relative error of at most 0.012.
Values may be sent and summed in bfloat16 or wider, within the bound.
No kernel may reach another device: no remote copies, remote signals or barrier semaphores. Data moves between devices by JAX's collectives and lax.ppermute only.
A program may use at most 128 MiB of HBM per device.

```python
import math
import jax
import jax.numpy as jnp
import numpy as np
from jax import lax

D = 2048
FF = 768
HEADS = 16
KV_HEADS = 2
HEAD_DIM = 128
TOP = 4
CTX = 128
TOK_DEV = 128
EXPERTS = 64
MOST = 9
TOKENS = 8192
SEQS = 64
N_PIPE = 4
N_EXPERT = 64


def plant_pair(key):
    base = jax.random.fold_in(key, 31)
    key_query, key_keys = jax.random.split(base, 2)
    keys_all = jnp.clip(jax.random.normal(key_keys, (N_PIPE, TOKENS, KV_HEADS, HEAD_DIM), jnp.float32), -5.0, 5.0)
    query_all = jnp.clip(jax.random.normal(key_query, (N_PIPE, TOKENS, HEADS, HEAD_DIM), jnp.float32), -5.0, 5.0)
    return (query_all.reshape(N_PIPE, TOKENS, HEADS * HEAD_DIM), keys_all.reshape(N_PIPE, TOKENS, KV_HEADS * HEAD_DIM))


def draw_queries(key, part):
    return plant_pair(key)[0].astype(jnp.bfloat16)


def draw_new_keys(key, part):
    return plant_pair(key)[1].astype(jnp.bfloat16)


def touch_ends(array, rng, least, largest):
    dims = array.shape
    index_at = [jax.random.randint(jax.random.fold_in(rng, axis), (), 0, dims[axis]) for axis in range(len(dims))]
    array = array.at[tuple(index_at)].set(least)
    longest = dims.index(max(dims))
    index_at[longest] = (index_at[longest] + 1) % dims[longest]
    return array.at[tuple(index_at)].set(largest)


def strengthened(drawn, own_key, source, target, blocks, factor):
    def block_of(dim):
        return (jnp.arange(drawn.shape[dim]) // (drawn.shape[dim] // blocks)).reshape((-1,) + (1,) * (drawn.ndim - 1 - dim))

    one_side = jax.random.permutation(own_key, blocks)[block_of(target)]
    other_side = (block_of(target) + blocks // 2) % blocks
    return jnp.where((block_of(source) == one_side) | (block_of(source) == other_side), factor * drawn, drawn)


def shard_levels(rng, dims, shards, least, high):
    loudness = 1.0
    for dim, parts in shards:
        draws = jax.random.uniform(jax.random.fold_in(jax.random.fold_in(rng, 6), dim), (parts,), jnp.float32, least / len(shards), high / len(shards))
        loudness = loudness * jnp.repeat(jnp.exp(draws), dims[dim] // parts).reshape((-1,) + (1,) * (len(dims) - 1 - dim))
    return loudness


def deal_out(rng, own, number, rows, count, top, bound, slope):
    sequence = jax.random.permutation(rng, count)
    heavy_load, usual = portions_of(count, rows * top, bound, slope, True), portions_of(count, rows * top, bound, slope, False)
    places = jnp.arange(count)

    def named(tallies, rotation):
        used = int((tallies > 0).sum())
        fixed = max(1, used // 4)
        moved = fixed + (places - fixed + rotation * (used - fixed)) % max(1, count - fixed)
        return jnp.zeros((count,), jnp.int32).at[sequence[jnp.where(places < fixed, places, moved)]].set(jnp.asarray(tallies, jnp.int32))

    tallies = jnp.where(number % 4 == 0, named(heavy_load, number // 4), named(usual, number - number // 4 - 1))
    mixed = jax.random.permutation(jax.random.fold_in(own, 3), count)
    donor, receiver = mixed[0:count // 2 * 2:2], mixed[1:count // 2 * 2:2]
    room = jnp.minimum(tallies[donor] - 1, bound - tallies[receiver]) // 2
    room = jnp.where((donor == sequence[0]) | (receiver == sequence[0]) | (tallies[receiver] == 0), 0, jnp.maximum(room, 0))
    moved = jax.random.randint(jax.random.fold_in(own, 4), (count // 2,), 0, 1 << 20) % (room + 1)
    tallies = tallies.at[donor].add(-moved).at[receiver].add(moved)
    labels = jnp.searchsorted(jnp.cumsum(tallies), jnp.arange(rows * top), side="right").astype(jnp.int32)
    grid = labels.reshape(top, rows).T
    grid = grid[jax.random.permutation(jax.random.fold_in(own, 1), rows)]
    rotation = jax.random.randint(jax.random.fold_in(own, 2), (rows, 1), 0, top)
    return jnp.take_along_axis(grid, (jnp.arange(top)[None, :] + rotation) % top, axis=1)


def portions_of(amount, total, reach, slope, full):
    loads = [(1 << 20) // math.isqrt(standing ** slope) + 1 for standing in range(1, amount + 1)]
    largest = reach if full else min(reach, max(-(-total // amount), total * loads[0] // sum(loads)))
    least = 1 if total - largest >= amount - 1 else 0
    given, spare = [largest] + [least] * (amount - 1), total - largest - least * (amount - 1)
    while spare > 0:
        movable = [i for i in range(1, amount) if given[i] < largest] or [i for i in range(1, amount) if given[i] < reach]
        whole, left = sum([loads[i] for i in movable]), spare
        for i in movable:
            addition = min(reach - given[i], max(1, left * loads[i] // whole), spare)
            given[i] = given[i] + addition
            spare = spare - addition
    return np.array(given)


def normal_values(key, extent, deviation, limit, cuts=(), kind=jnp.bfloat16):
    loudness = shard_levels(key, extent, cuts, -0.22, 0.18) if cuts else 1.0
    drawn = jax.random.normal(key, extent, jnp.float32) * deviation * loudness
    return jnp.minimum(jnp.maximum(drawn, -limit), limit).astype(kind)


def gaussian_with(key, dims, width, limit, pieces, heavy, kind=jnp.bfloat16):
    drawn = width * jax.random.normal(key, dims, jnp.float32)
    if pieces:
        drawn = drawn * shard_levels(key, dims, pieces, -0.22, 0.18)
    return jnp.clip(strengthened(drawn, jax.random.fold_in(key, 3), *heavy), -limit, limit).astype(kind)


def setup_inputs(seed: int = 0) -> dict:
    keys = jax.random.split(jax.random.key(seed), 17)
    forward_input = normal_values(keys[0], (N_PIPE, TOKENS, D), 1.0, 6.0, ((0, 4), (1, 64)))
    queries = draw_queries(jax.random.fold_in(keys[16], 71), 0)
    new_keys = draw_new_keys(jax.random.fold_in(keys[16], 71), 0)
    new_values = normal_values(keys[3], (N_PIPE, TOKENS, KV_HEADS * HEAD_DIM), 1.0, 6.0, ((0, 4), (1, 64)))
    cache_keys = normal_values(keys[4], (N_PIPE, SEQS * CTX, KV_HEADS * HEAD_DIM), 1.0, 6.0, ((0, 4), (1, 64)))
    cache_values = normal_values(keys[5], (N_PIPE, SEQS * CTX, KV_HEADS * HEAD_DIM), 1.0, 6.0, ((0, 4), (1, 64)))
    context_lengths = touch_ends(jax.random.randint(keys[6], (N_PIPE, SEQS), 1, CTX + 1), jax.random.fold_in(keys[6], 1), 1, CTX).astype(jnp.int32)
    norm_gain = jnp.clip(1.0 + 0.1 * jax.random.normal(keys[7], (N_PIPE, D), jnp.float32), 0.5, 1.5)
    router = normal_values(keys[8], (N_PIPE, D, EXPERTS), D ** -0.5, 0.125, ((0, 4),))
    gate_weight = normal_values(keys[9], (N_PIPE, EXPERTS, D, FF), D ** -0.5, 0.125, ((0, 4), (1, 64)))
    up_weight = normal_values(keys[10], (N_PIPE, EXPERTS, D, FF), D ** -0.5, 0.125, ((0, 4), (1, 64)))
    down_weight = normal_values(keys[11], (N_PIPE, EXPERTS, FF, D), FF ** -0.5, 0.21875, ((0, 4), (1, 64)))
    forward_ids_keys = jax.random.split(jax.random.fold_in(keys[12], 1), N_PIPE * TOKENS // TOK_DEV)
    forward_ids_turns = jax.random.permutation(jax.random.fold_in(keys[12], 3), N_PIPE * TOKENS // TOK_DEV)
    forward_ids = jax.vmap(lambda own, number: deal_out(jax.random.fold_in(keys[12], 2), own, number, TOK_DEV, EXPERTS, TOP, MOST, 2))(forward_ids_keys, forward_ids_turns).reshape((N_PIPE, TOKENS, TOP))
    backward_input = normal_values(keys[13], (N_PIPE, TOKENS, D), 1.0, 6.0, ((0, 4), (1, 64)))
    backward_ids_keys = jax.random.split(jax.random.fold_in(keys[14], 1), N_PIPE * TOKENS // TOK_DEV)
    backward_ids_turns = jax.random.permutation(jax.random.fold_in(keys[14], 3), N_PIPE * TOKENS // TOK_DEV)
    backward_ids = jax.vmap(lambda own, number: deal_out(jax.random.fold_in(keys[14], 2), own, number, TOK_DEV, EXPERTS, TOP, MOST, 2))(backward_ids_keys, backward_ids_turns).reshape((N_PIPE, TOKENS, TOP))
    output_grad = gaussian_with(keys[15], (N_PIPE, TOKENS, D), 1.0, 16.0, ((0, 4), (1, 64)), (1, 2, 64, 4.0))
    return dict(forward_input=forward_input, queries=queries, new_keys=new_keys, new_values=new_values, cache_keys=cache_keys, cache_values=cache_values, context_lengths=context_lengths, norm_gain=norm_gain, router=router, gate_weight=gate_weight, up_weight=up_weight, down_weight=down_weight, forward_ids=forward_ids, backward_input=backward_input, backward_ids=backward_ids, output_grad=output_grad)


epsilon = 1e-06
far_below = -1e+30

def normalize(resid, gain):
    wide = resid.astype(jnp.float32)
    inv_rms = lax.rsqrt(lax.optimization_barrier(jnp.mean(wide * wide, axis=-1, keepdims=True)) + epsilon)
    return (wide, inv_rms, (wide * inv_rms * gain).astype(jnp.bfloat16))

def routing(normed, expert_ids, table):
    logits = jnp.dot(normed.astype(jnp.float32), table.astype(jnp.float32))
    selects = expert_ids[:, :, None] == jnp.arange(table.shape[1], dtype=jnp.int32)
    chosen = lax.optimization_barrier(jnp.sum(jnp.where(selects, logits[:, None, :], 0.0), axis=-1))
    route_probs = 1.0 / lax.optimization_barrier(jnp.sum(jnp.exp(chosen[:, None, :] - chosen[:, :, None]), axis=-1))
    return (route_probs, selects)

def place_slots(selects, capacity):
    counted = selects.reshape(-1, selects.shape[-1]).astype(jnp.int32)
    running = jnp.cumsum(counted, axis=0)
    slot_index = lax.optimization_barrier(jnp.sum(counted * running, axis=-1)) - 1
    owner = lax.optimization_barrier(jnp.sum(counted * jnp.arange(selects.shape[-1], dtype=jnp.int32), axis=-1))
    return (owner * capacity + slot_index).reshape(selects.shape[0], selects.shape[1])

def attention(queries, new_keys, new_values, cache_keys, cache_values, length):
    tokens = queries.shape[0]
    context = cache_keys.shape[0]
    key_rows = jnp.concatenate([cache_keys, new_keys], axis=0).astype(jnp.float32).reshape(-1, KV_HEADS, HEAD_DIM)
    value_rows = jnp.concatenate([cache_values, new_values], axis=0).astype(jnp.float32).reshape(-1, KV_HEADS, HEAD_DIM)
    grouped = queries.astype(jnp.float32).reshape(tokens, KV_HEADS, HEADS // KV_HEADS, HEAD_DIM)
    scores = jnp.einsum('tkgd,skd->kgts', grouped, key_rows) * HEAD_DIM ** (-0.5)
    position = jnp.arange(key_rows.shape[0], dtype=jnp.int32)[None, :]
    query_pos = jnp.arange(tokens, dtype=jnp.int32)[:, None]
    visible = jnp.where(position < context, position < length, position - context <= query_pos)
    scores = jnp.where(visible, scores, far_below)
    row_max = lax.optimization_barrier(jnp.max(scores, axis=-1, keepdims=True))
    lifted = jnp.exp(scores - row_max)
    attn_weights = (lifted / lax.optimization_barrier(jnp.sum(lifted, axis=-1, keepdims=True))).astype(jnp.bfloat16)
    merged = jnp.einsum('kgts,skd->tkgd', attn_weights.astype(jnp.float32), value_rows)
    return merged.reshape(tokens, HEADS * HEAD_DIM).astype(jnp.bfloat16)

def expert_ahead(operands):
    slot_rows, gate_matrix, up_matrix, down_matrix = operands
    wide_rows = slot_rows.astype(jnp.float32)
    gate_pre = jnp.dot(wide_rows, gate_matrix.astype(jnp.float32))
    up_pre = jnp.dot(wide_rows, up_matrix.astype(jnp.float32))
    hidden = (gate_pre * jax.nn.sigmoid(gate_pre) * up_pre).astype(jnp.bfloat16)
    return jnp.dot(hidden.astype(jnp.float32), down_matrix.astype(jnp.float32)).astype(jnp.bfloat16)

def expert_behind(operands):
    slot_rows, slot_grads, gate_matrix, up_matrix, down_matrix = operands
    wide_rows = slot_rows.astype(jnp.float32)
    gate_wide = gate_matrix.astype(jnp.float32)
    up_wide = up_matrix.astype(jnp.float32)
    gate_pre = jnp.dot(wide_rows, gate_wide)
    up_pre = jnp.dot(wide_rows, up_wide)
    sigmoid_gate = jax.nn.sigmoid(gate_pre)
    gate_act = gate_pre * sigmoid_gate
    hidden = (gate_act * up_pre).astype(jnp.bfloat16)
    down_grad = jnp.dot(slot_grads.astype(jnp.float32), down_matrix.astype(jnp.float32).T)
    weight_grad = lax.optimization_barrier(jnp.sum(hidden.astype(jnp.float32) * down_grad, axis=-1)).astype(jnp.bfloat16)
    slope_act = sigmoid_gate * (1.0 + gate_pre * (1.0 - sigmoid_gate))
    gate_grad = (down_grad * up_pre * slope_act).astype(jnp.bfloat16)
    up_grad = (down_grad * gate_act).astype(jnp.bfloat16)
    slot_back = jnp.dot(gate_grad.astype(jnp.float32), gate_wide.T) + jnp.dot(up_grad.astype(jnp.float32), up_wide.T)
    return (slot_back.astype(jnp.bfloat16), weight_grad)

def layout(selects):
    target = jax.vmap(lambda picked: place_slots(picked, MOST))(selects.reshape(N_EXPERT, TOK_DEV, TOP, EXPERTS))
    owner = target // MOST
    column = jnp.arange(N_EXPERT, dtype=jnp.int32)[:, None, None] * MOST + target % MOST
    return (owner.reshape(TOKENS, TOP), column.reshape(TOKENS, TOP))

def pack_rows(source_rows, owner, column):
    buffer = jnp.zeros((EXPERTS, N_EXPERT * MOST, D), jnp.bfloat16)
    spread = jnp.broadcast_to(source_rows[:, None, :], (TOKENS, TOP, D))
    return buffer.at[owner, column].set(spread)

def section_pass(forward_input, queries, new_keys, new_values, cache_keys, cache_values, context_lengths, norm_gain, router, gate_weight, up_weight, down_weight, forward_ids, backward_input, backward_ids, output_grad):
    sequences = lax.map(lambda operands: attention(*operands), (queries.reshape(N_EXPERT, TOK_DEV, -1), new_keys.reshape(N_EXPERT, TOK_DEV, -1), new_values.reshape(N_EXPERT, TOK_DEV, -1), cache_keys.reshape(N_EXPERT, CTX, -1), cache_values.reshape(N_EXPERT, CTX, -1), context_lengths))
    mixed = sequences.reshape(TOKENS, D)
    resid_ahead = (forward_input.astype(jnp.float32) + mixed.astype(jnp.float32)).astype(jnp.bfloat16)
    ahead_wide, ahead_inv, ahead_normed = normalize(resid_ahead, norm_gain)
    ahead_probs, ahead_selects = routing(ahead_normed, forward_ids, router)
    ahead_owner, ahead_column = layout(ahead_selects)
    ahead_buffer = pack_rows(ahead_normed, ahead_owner, ahead_column)
    produced = lax.map(expert_ahead, (ahead_buffer, gate_weight, up_weight, down_weight))
    ahead_rows = produced[ahead_owner, ahead_column].astype(jnp.float32)
    forward_output = (ahead_wide + lax.optimization_barrier(jnp.sum(ahead_probs[:, :, None] * ahead_rows, axis=1))).astype(jnp.bfloat16)
    behind_wide, behind_inv, behind_normed = normalize(backward_input, norm_gain)
    behind_probs, behind_selects = routing(behind_normed, backward_ids, router)
    behind_owner, behind_column = layout(behind_selects)
    rows_buffer = pack_rows(behind_normed, behind_owner, behind_column)
    grads_buffer = pack_rows(output_grad, behind_owner, behind_column)
    slot_back, slot_weight = lax.map(expert_behind, (rows_buffer, grads_buffer, gate_weight, up_weight, down_weight))
    input_rows = slot_back[behind_owner, behind_column].astype(jnp.float32)
    weight_rows = slot_weight[behind_owner, behind_column].astype(jnp.float32)
    normed_grad = lax.optimization_barrier(jnp.sum(behind_probs[:, :, None] * input_rows, axis=1))
    logit_terms = behind_probs * (weight_rows - lax.optimization_barrier(jnp.sum(behind_probs * weight_rows, axis=-1, keepdims=True)))
    logit_grad = lax.optimization_barrier(jnp.sum(jnp.where(behind_selects, logit_terms[:, :, None], 0.0), axis=1)).astype(jnp.bfloat16)
    normed_grad = normed_grad + jnp.dot(logit_grad.astype(jnp.float32), router.astype(jnp.float32).T)
    grad_factor = TOKENS ** (-0.5)
    router_grad = jnp.dot(behind_normed.astype(jnp.float32).T, logit_grad.astype(jnp.float32)) * grad_factor
    scaled_grad = normed_grad * norm_gain
    resid_grad = behind_inv * (scaled_grad - behind_wide * behind_inv * behind_inv * lax.optimization_barrier(jnp.mean(scaled_grad * behind_wide, axis=-1, keepdims=True)))
    gain_grad = lax.optimization_barrier(jnp.sum(normed_grad * behind_wide * behind_inv, axis=0)) * grad_factor
    input_grad = (output_grad.astype(jnp.float32) + resid_grad).astype(jnp.bfloat16)
    return (forward_output, input_grad, router_grad, gain_grad)

def reference(forward_input, queries, new_keys, new_values, cache_keys, cache_values, context_lengths, norm_gain, router, gate_weight, up_weight, down_weight, forward_ids, backward_input, backward_ids, output_grad):
    outputs = []
    for section in range(N_PIPE):
        outputs.append(section_pass(forward_input[section], queries[section], new_keys[section], new_values[section], cache_keys[section], cache_values[section], context_lengths[section], norm_gain[section], router[section], gate_weight[section], up_weight[section], down_weight[section], forward_ids[section], backward_input[section], backward_ids[section], output_grad[section]))
    forward_output = jnp.roll(jnp.stack([item[0] for item in outputs]), 1, axis=0)
    input_grad = jnp.roll(jnp.stack([item[1] for item in outputs]), -1, axis=0)
    router_grad = jnp.stack([item[2] for item in outputs])
    gain_grad = jnp.stack([item[3] for item in outputs])
    return (forward_output, input_grad, router_grad, gain_grad)
```

```python
import jax
import jax.numpy as jnp
from jax import lax
from jax.sharding import Mesh, PartitionSpec as P

HEADS = 16
KV_HEADS = 2
HEAD_DIM = 128
D = 2048
FF = 768
EXPERTS = 64
MOST = 9
TOK = 128
PEERS = 32
SLOTS = PEERS * MOST
XY = ("x", "y", "core")
ALL = ("x", "zh", "y", "core")

epsilon = 1e-06
far_below = -1e30
bf16 = jnp.bfloat16
f32 = jnp.float32


def spread_out(x, axis=XY):
    return lax.all_to_all(x, axis, 0, 0, tiled=True)


def swapped(x):
    return lax.ppermute(x, "zh", [(0, 1), (1, 0)])


def moved(x, same, step):
    pairs = []
    for pipe in range(4):
        for zh in range(2):
            to = ((pipe + step) % 4) * 2 + (zh if same else 1 - zh)
            pairs.append((pipe * 2 + zh, to))
    return lax.ppermute(x, ("pipe", "zh"), pairs)


def normalize(x, gain):
    wide = x.astype(f32)
    inv_rms = lax.rsqrt(jnp.mean(wide * wide, axis=-1, keepdims=True) + epsilon)
    unit = wide * inv_rms
    return inv_rms, unit, (unit * gain).astype(bf16)


def chosen_of(ids):
    experts = jnp.arange(EXPERTS, dtype=jnp.int32)
    hit = ids[:, 0:1] == experts
    for k in range(1, ids.shape[1]):
        hit = hit | (ids[:, k : k + 1] == experts)
    return hit


def route_probs(normed, table, hit):
    logits = jnp.dot(normed, table, preferred_element_type=f32)
    logits = jnp.where(hit, logits, far_below)
    lifted = jnp.where(hit, jnp.exp(logits - jnp.max(logits, axis=-1, keepdims=True)), 0.0)
    return lifted / jnp.sum(lifted, axis=-1, keepdims=True)


def slot_tables(zh):
    p = jnp.arange(SLOTS, dtype=jnp.int32)
    d = p // MOST
    owner = (d // 8) * 16 + zh * 8 + d % 8
    pick = (owner[:, None] == jnp.arange(EXPERTS, dtype=jnp.int32)).astype(bf16)
    return pick, (p % MOST).astype(f32)[:, None]


def place(hit, pick, slot):
    row = lax.broadcasted_iota(jnp.int32, (TOK, TOK), 0)
    col = lax.broadcasted_iota(jnp.int32, (TOK, TOK), 1)
    before = (col < row).astype(bf16)
    rank = jnp.dot(before, hit.astype(bf16), preferred_element_type=f32)
    code = jnp.where(hit, rank + 1.0, 0.0).astype(bf16)
    spread = lax.dot_general(pick, code, (((1,), (1,)), ((), ())), preferred_element_type=f32)
    return (spread == slot + 1.0).astype(bf16)


def weighted(onehot, pick, probs):
    spread = lax.dot_general(
        pick, probs.astype(bf16), (((1,), (1,)), ((), ())), preferred_element_type=f32
    )
    return onehot * spread.astype(bf16)


def packed(onehot, rows):
    return jnp.dot(onehot, rows, preferred_element_type=f32).astype(bf16)


def summed(weights, rows):
    return lax.dot_general(weights, rows, (((0,), (0,)), ((), ())), preferred_element_type=f32)


def attention(queries, new_keys, new_values, cache_keys, cache_values, length):
    tokens = queries.shape[0]
    context = cache_keys.shape[0]
    key_rows = jnp.concatenate([cache_keys, new_keys], axis=0).reshape(-1, KV_HEADS, HEAD_DIM)
    value_rows = jnp.concatenate([cache_values, new_values], axis=0).reshape(-1, KV_HEADS, HEAD_DIM)
    grouped = queries.reshape(tokens, KV_HEADS, HEADS // KV_HEADS, HEAD_DIM)
    scores = jnp.einsum(
        "tkgd,skd->kgts", grouped, key_rows, preferred_element_type=f32
    ) * HEAD_DIM ** (-0.5)
    position = jnp.arange(key_rows.shape[0], dtype=jnp.int32)[None, :]
    query_pos = jnp.arange(tokens, dtype=jnp.int32)[:, None]
    visible = jnp.where(position < context, position < length, position - context <= query_pos)
    scores = jnp.where(visible, scores, far_below)
    row_max = jnp.max(scores, axis=-1, keepdims=True)
    lifted = jnp.exp(scores - row_max)
    attn_weights = (lifted / jnp.sum(lifted, axis=-1, keepdims=True)).astype(bf16)
    merged = jnp.einsum("kgts,skd->tkgd", attn_weights, value_rows, preferred_element_type=f32)
    return merged.reshape(tokens, HEADS * HEAD_DIM).astype(bf16)


def expert_ahead(rows, gate, up, down):
    gate_pre = jnp.dot(rows, gate, preferred_element_type=f32)
    up_pre = jnp.dot(rows, up, preferred_element_type=f32)
    hidden = (gate_pre * jax.nn.sigmoid(gate_pre) * up_pre).astype(bf16)
    return jnp.dot(hidden, down, preferred_element_type=f32).astype(bf16)


def expert_behind(rows, grads, gate, up, down):
    across = (((1,), (1,)), ((), ()))
    gate_pre = jnp.dot(rows, gate, preferred_element_type=f32)
    up_pre = jnp.dot(rows, up, preferred_element_type=f32)
    sig = jax.nn.sigmoid(gate_pre)
    act = gate_pre * sig
    hidden = (act * up_pre).astype(bf16)
    down_grad = lax.dot_general(grads, down, across, preferred_element_type=f32)
    weight_grad = jnp.sum(hidden.astype(f32) * down_grad, axis=-1)
    slope = sig * (1.0 + gate_pre * (1.0 - sig))
    gate_grad = (down_grad * up_pre * slope).astype(bf16)
    up_grad = (down_grad * act).astype(bf16)
    back = lax.dot_general(gate_grad, gate, across, preferred_element_type=f32)
    back = back + lax.dot_general(up_grad, up, across, preferred_element_type=f32)
    return back.astype(bf16), weight_grad.astype(bf16)


def body(
    forward_input,
    queries,
    new_keys,
    new_values,
    cache_keys,
    cache_values,
    context_lengths,
    norm_gain,
    router,
    gate_weight,
    up_weight,
    down_weight,
    forward_ids,
    backward_input,
    backward_ids,
    output_grad,
):
    zh = lax.axis_index("zh")
    gain = norm_gain[0]
    table = router[0]
    gate, up, down = gate_weight[0, 0], up_weight[0, 0], down_weight[0, 0]
    pick, slot = slot_tables(zh)

    back_x, back_g = backward_input[0], output_grad[0]
    ids = jnp.concatenate([backward_ids[0], forward_ids[0]], axis=1)
    ids_far = swapped(ids)
    x_far = swapped(back_x)
    g_far = swapped(back_g)

    def behind_side(x, g, chosen):
        hit = chosen_of(chosen)
        inv, unit, normed = normalize(x, gain)
        onehot = place(hit, pick, slot)
        probs = route_probs(normed, table, hit)
        sent = jnp.concatenate([packed(onehot, normed), packed(onehot, g)], axis=1)
        return inv, unit, normed, onehot, probs, sent.reshape(PEERS, MOST * 16, 256)

    inv_b, unit_b, normed_b, one_b, probs_b, sent_b = behind_side(back_x, back_g, ids[:, :4])
    got_b = spread_out(sent_b)
    inv_c, unit_c, normed_c, one_c, probs_c, sent_c = behind_side(x_far, g_far, ids_far[:, :4])
    got_c = spread_out(sent_c)

    mixed = attention(
        queries[0], new_keys[0], new_values[0], cache_keys[0], cache_values[0], context_lengths[0, 0]
    )
    resid = (forward_input[0].astype(f32) + mixed.astype(f32)).astype(bf16)
    resid_far = swapped(resid)

    def ahead_side(x, chosen):
        hit = chosen_of(chosen)
        _, _, normed = normalize(x, gain)
        onehot = place(hit, pick, slot)
        probs = route_probs(normed, table, hit)
        sent = packed(onehot, normed).reshape(PEERS, MOST * 8, 256)
        return weighted(onehot, pick, probs), sent

    mix_f, sent_f = ahead_side(resid, ids[:, 4:])
    mix_h, sent_h = ahead_side(resid_far, ids_far[:, 4:])
    got_f = spread_out(jnp.concatenate([sent_f, sent_h], axis=1))

    def behind_expert(got):
        both = got.reshape(SLOTS, 2 * D)
        back, grad = expert_behind(both[:, :D], both[:, D:], gate, up, down)
        return back.reshape(PEERS, MOST * 8, 256), grad.reshape(PEERS, MOST)

    back_b, grad_b = behind_expert(got_b)
    back_c, grad_c = behind_expert(got_c)
    extra = jnp.pad(
        jnp.concatenate([grad_b, grad_c], axis=1)[:, None, :], ((0, 0), (0, 7), (0, 256 - 2 * MOST))
    )
    home_b = spread_out(jnp.concatenate([back_b, back_c, extra], axis=1))

    made = expert_ahead(got_f.reshape(2 * SLOTS, D), gate, up, down)
    home_f = spread_out(made.reshape(PEERS, 2 * MOST * 8, 256))

    rows = MOST * 8
    sums_b = summed(weighted(one_b, pick, probs_b), home_b[:, :rows].reshape(SLOTS, D))
    sums_c = summed(weighted(one_c, pick, probs_c), home_b[:, rows : 2 * rows].reshape(SLOTS, D))
    grads = home_b[:, 2 * rows, : 2 * MOST]

    def grads_at(onehot, part):
        return summed(onehot * part.reshape(SLOTS, 1), pick)

    near = jnp.concatenate([grads_at(one_b, grads[:, :MOST]), grads_at(one_c, grads[:, MOST:])], axis=0)
    far = swapped(near)
    grad_of_b = near[:TOK] + far[TOK:]
    grad_of_c = near[TOK:] + far[:TOK]

    def logit_grads(probs, grad):
        return (probs * (grad - jnp.sum(probs * grad, axis=-1, keepdims=True))).astype(bf16)

    logit_b = logit_grads(probs_b, grad_of_b)
    logit_c = logit_grads(probs_c, grad_of_c)
    sums_b = sums_b + lax.dot_general(
        logit_b, table, (((1,), (1,)), ((), ())), preferred_element_type=f32
    )

    def through_norm(sums, inv, unit):
        scaled = sums * gain
        return inv * (scaled - unit * jnp.mean(scaled * unit, axis=-1, keepdims=True))

    own_b = (back_g.astype(f32) + through_norm(sums_b, inv_b, unit_b)).astype(bf16)
    own_c = through_norm(sums_c, inv_c, unit_c).astype(bf16)
    input_grad = (
        moved(own_b, True, -1).astype(f32) + moved(own_c, False, -1).astype(f32)
    ).astype(bf16)

    own_f = (
        resid.astype(f32) + summed(mix_f, home_f[:, :rows].reshape(SLOTS, D))
    ).astype(bf16)
    own_h = summed(mix_h, home_f[:, rows:].reshape(SLOTS, D)).astype(bf16)
    forward_output = (
        moved(own_f, True, 1).astype(f32) + moved(own_h, False, 1).astype(f32)
    ).astype(bf16)

    factor = 8192 ** (-0.5)
    gains = (jnp.sum(sums_b * unit_b, axis=0) + jnp.sum(sums_c * unit_c, axis=0)).reshape(4, 2, 256)
    mine = lax.dynamic_index_in_dim(gains, zh, 1, keepdims=False)
    theirs = lax.dynamic_index_in_dim(gains, 1 - zh, 1, keepdims=False)
    mine = (mine + swapped(theirs)).reshape(PEERS, 32, 1)
    normed_all = jnp.concatenate([normed_b, normed_c], axis=0).reshape(2 * TOK, 4, 2, 256)
    normed_all = lax.dynamic_index_in_dim(normed_all, zh, 2, keepdims=False).reshape(2 * TOK, D // 2)
    logit_all = jnp.concatenate([logit_b, logit_c], axis=0)
    router_part = summed(normed_all, logit_all).reshape(PEERS, 32, EXPERTS)
    shares = jnp.concatenate(
        [router_part, mine, jnp.zeros((PEERS, 32, 63), f32)], axis=2
    )
    total = jnp.sum(spread_out(shares), axis=0) * factor
    return (
        forward_output[None],
        input_grad[None],
        total[None, :, :EXPERTS],
        total[:, EXPERTS][None],
    )


def solution(mesh):
    grid = Mesh(mesh.devices.reshape(4, 4, 2, 4, 2), ("pipe", "x", "zh", "y", "core"))
    rows = P("pipe", ALL, None)
    placed = (
        rows,
        rows,
        rows,
        rows,
        rows,
        rows,
        P("pipe", ALL),
        P("pipe", None),
        P("pipe", None, None),
        P("pipe", ALL, None, None),
        P("pipe", ALL, None, None),
        P("pipe", ALL, None, None),
        rows,
        rows,
        rows,
        rows,
    )
    return jax.shard_map(
        body,
        mesh=grid,
        in_specs=placed,
        out_specs=(rows, rows, rows, P("pipe", ALL)),
        check_vma=False,
    )
```

```python
import jax
import jax.numpy as jnp
from jax import lax
from jax.experimental import pallas as pl
from jax.experimental.pallas import tpu as pltpu
from jax.sharding import Mesh, PartitionSpec as P


HEADS = 16
KV_HEADS = 2
HEAD_DIM = 128
D = 2048
FF = 768
EXPERTS = 64
MOST = 9
TOK = 128
PEERS = 32
SLOTS = PEERS * MOST
ROWS = MOST * 8
AREA = SLOTS * 8
XY = ("x", "y", "core")
ALL = ("x", "zh", "y", "core")

epsilon = 1e-06
far_below = -1e30
factor = 8192 ** (-0.5)
bf16 = jnp.bfloat16
f32 = jnp.float32
ACROSS = (((1,), (1,)), ((), ()))
DOWN = (((0,), (0,)), ((), ()))
VMEM = pl.BlockSpec(memory_space=pltpu.VMEM)
SMEM = pl.BlockSpec(memory_space=pltpu.SMEM)
HBM = pl.BlockSpec(memory_space=pltpu.HBM)


def spread_out(x):
    return lax.all_to_all(x, XY, 0, 0, tiled=True)


def swapped(x):
    return lax.ppermute(x, "zh", [(0, 1), (1, 0)])


def moved(x, same, step):
    pairs = []
    for pipe in range(4):
        for zh in range(2):
            to = ((pipe + step) % 4) * 2 + (zh if same else 1 - zh)
            pairs.append((pipe * 2 + zh, to))
    return lax.ppermute(x, ("pipe", "zh"), pairs)


def shape(dims, dtype=bf16):
    return jax.ShapeDtypeStruct(dims, dtype)


def call(kernel, outs, ins, scratch, args, flops, mib):
    return pl.pallas_call(
        kernel,
        out_shape=outs,
        in_specs=ins,
        out_specs=tuple(VMEM for _ in outs),
        scratch_shapes=scratch,
        compiler_params=pltpu.CompilerParams(vmem_limit_bytes=60 * 2**20),
        cost_estimate=pl.CostEstimate(
            flops=flops, transcendentals=0, bytes_accessed=mib * 2**20
        ),
    )(*args)


def dot(a, b, dims=None):
    if dims is None:
        return jnp.dot(a, b, preferred_element_type=f32)
    return lax.dot_general(a, b, dims, preferred_element_type=f32)


def iota(dims, dim):
    return lax.broadcasted_iota(jnp.int32, dims, dim)


def marks(cond):
    return cond.astype(f32).astype(bf16)


def unit_rows(x):
    wide = x.astype(f32)
    inv_rms = lax.rsqrt(jnp.mean(wide * wide, axis=-1, keepdims=True) + epsilon)
    return inv_rms, wide * inv_rms


def hits(ids):
    expert = iota((EXPERTS, ids.shape[1]), 0)
    hit = ids[0:1, :] == expert
    for k in range(1, 4):
        hit = hit | (ids[k : k + 1, :] == expert)
    return hit


def choice(normed, table, hit):
    logits = jnp.where(hit, dot(table, normed, ACROSS), far_below)
    lifted = jnp.where(hit, jnp.exp(logits - jnp.max(logits, axis=0, keepdims=True)), 0.0)
    return lifted / jnp.sum(lifted, axis=0, keepdims=True)


def ranked(hit):
    tokens = hit.shape[1]
    earlier, later = iota((tokens, tokens), 0), iota((tokens, tokens), 1)
    before = marks((earlier < later) & (earlier // TOK == later // TOK))
    hit = hit.astype(f32)
    return (hit * (dot(hit.astype(bf16), before) + 1.0)).astype(bf16)


def picks(peer, zh):
    owner = (peer // 8) * 16 + zh * 8 + peer % 8
    return marks(owner == iota(peer.shape, 1))


def each_peer(step):
    def turn(d, carry):
        step(d, pl.ds(pl.multiple_of(d * ROWS, 8), ROWS))
        return carry

    lax.fori_loop(0, PEERS, turn, 0)


def area_rows(d, area):
    return pl.ds(pl.multiple_of(d * ROWS + area * AREA, 8), ROWS)


LANES = (pl.ds(0, 128), pl.ds(128, 128))


def put_rows(wide_ref, j, rows, start=0):
    for lane in range(rows.shape[1] // 128):
        wide_ref[lane, pl.ds(start + j, rows.shape[0], stride=8), :] = rows[
            :, lane * 128 : lane * 128 + 128
        ]


def get_rows(wide_ref, j, count, start=0):
    return jnp.concatenate(
        [
            wide_ref[lane, pl.ds(start + j, count, stride=8), :].astype(bf16)
            for lane in range(wide_ref.shape[0])
        ],
        axis=1,
    )


def routed(ids, x, zh, gain, table):
    hit = hits(ids)
    _, unit = unit_rows(x)
    normed = (unit * gain).astype(bf16)
    probs = choice(normed, table, hit)
    pick = picks(iota((SLOTS, EXPERTS), 0) // MOST, zh)
    slot = (iota((SLOTS, TOK), 0) % MOST + 1).astype(f32)
    return normed, probs, pick, marks(dot(pick, ranked(hit)) == slot)


def mixed_by(onehot, pick, probs):
    return onehot * dot(pick, probs.astype(bf16)).astype(bf16)


def fill(wide_ref, area, onehot, rows_ref):
    for j in range(8):
        put_rows(wide_ref, j, dot(onehot, rows_ref[:, pl.ds(j * 256, 256)]), area * AREA)


def give(wide_ref, sent_ref, areas):
    def step(d, rows):
        for area in range(areas):
            for lane in range(2):
                sent_ref[d, pl.ds(area * ROWS, ROWS), LANES[lane]] = wide_ref[lane, area_rows(d, area), :].astype(bf16)

    each_peer(step)


def near_pack(
    zh_ref, ids_ref, ahead_ids_ref, x_ref, g_ref, resid_ref, gain_ref, table_ref,
    sent_ref, normed_ref, onehot_ref, probs_ref, mix_ref, wide_ref, rows_ref
):
    zh, gain, table = zh_ref[0], gain_ref[...], table_ref[...]
    normed_ref[...], probs_ref[...], _, onehot_ref[...] = routed(ids_ref[...], x_ref[...], zh, gain, table)
    fill(wide_ref, 0, onehot_ref[...], normed_ref)
    fill(wide_ref, 1, onehot_ref[...], g_ref)
    rows_ref[...], probs, pick, onehot = routed(ahead_ids_ref[...], resid_ref[...], zh, gain, table)
    mix_ref[...] = mixed_by(onehot, pick, probs)
    fill(wide_ref, 2, onehot, rows_ref)
    give(wide_ref, sent_ref, 3)


def run_near_pack(*args):
    return call(
        near_pack,
        (
            shape((PEERS, 3 * ROWS, 256)),
            shape((TOK, D)),
            shape((SLOTS, TOK)),
            shape((EXPERTS, TOK), f32),
            shape((SLOTS, TOK)),
        ),
        [SMEM] + [VMEM] * 7,
        [pltpu.VMEM((2, 3 * AREA, 128), f32), pltpu.VMEM((TOK, D), bf16)],
        args,
        2 * 10**9,
        8,
    )


def far_pack(
    zh_ref, ids_ref, x_ref, g_ref, gain_ref, table_ref, sent_ref, normed_ref, onehot_ref, probs_ref, wide_ref
):
    normed_ref[...], probs_ref[...], _, onehot_ref[...] = routed(
        ids_ref[...], x_ref[...], zh_ref[0], gain_ref[...], table_ref[...]
    )
    fill(wide_ref, 0, onehot_ref[...], normed_ref)
    fill(wide_ref, 1, onehot_ref[...], g_ref)
    give(wide_ref, sent_ref, 2)


def run_far_pack(*args):
    return call(
        far_pack,
        (shape((PEERS, 2 * ROWS, 256)), shape((TOK, D)), shape((SLOTS, TOK)), shape((EXPERTS, TOK), f32)),
        [SMEM] + [VMEM] * 5,
        [pltpu.VMEM((2, 2 * AREA, 128), f32)],
        args,
        10**9,
        6,
    )


def ahead_pack(zh_ref, ids_ref, x_ref, gain_ref, table_ref, sent_ref, mix_ref, wide_ref, rows_ref):
    rows_ref[...], probs, pick, onehot = routed(ids_ref[...], x_ref[...], zh_ref[0], gain_ref[...], table_ref[...])
    mix_ref[...] = mixed_by(onehot, pick, probs)
    fill(wide_ref, 0, onehot, rows_ref)
    give(wide_ref, sent_ref, 1)


def run_ahead_pack(*args):
    return call(
        ahead_pack,
        (shape((PEERS, ROWS, 256)), shape((SLOTS, TOK))),
        [SMEM] + [VMEM] * 4,
        [pltpu.VMEM((2, AREA, 128), f32), pltpu.VMEM((TOK, D), bf16)],
        args,
        10**9,
        4,
    )


def fetched(pairs, sems):
    copies = [pltpu.make_async_copy(a, b, sems.at[i]) for i, (a, b) in enumerate(pairs)]
    for copy in copies:
        copy.start()
    return copies


def behind_experts(
    near_ref, far_ref, gate_hbm, up_hbm, down_hbm, back_ref, wide_ref, gate_ref, up_ref, down_ref, sems
):
    copies = fetched(((gate_hbm, gate_ref), (up_hbm, up_ref), (down_hbm, down_ref)), sems)
    count = 2 * SLOTS

    def take(d, rows):
        for lane in range(2):
            for half, ref in enumerate((near_ref, far_ref)):
                for kind in range(2):
                    wide_ref[lane, area_rows(d, 2 * kind + half), :] = ref[
                        d, pl.ds(kind * ROWS, ROWS), LANES[lane]
                    ].astype(f32)

    each_peer(take)
    copies[0].wait()
    copies[1].wait()
    gate_pre, up_pre = jnp.zeros((count, FF), f32), jnp.zeros((count, FF), f32)
    for j in range(4):
        rows = jnp.concatenate([get_rows(wide_ref, 2 * j, count), get_rows(wide_ref, 2 * j + 1, count)], axis=1)
        gate_pre = gate_pre + dot(rows, gate_ref[pl.ds(j * 512, 512), :])
        up_pre = up_pre + dot(rows, up_ref[pl.ds(j * 512, 512), :])
    copies[2].wait()
    down_grad = jnp.zeros((count, FF), f32)
    for j in range(4):
        rows = jnp.concatenate(
            [get_rows(wide_ref, 2 * j + i, count, 2 * AREA) for i in range(2)], axis=1
        )
        down_grad = down_grad + dot(rows, down_ref[:, pl.ds(j * 512, 512)], ACROSS)
    sig = 1.0 / (1.0 + jnp.exp(-gate_pre))
    act = gate_pre * sig
    hidden = (act * up_pre).astype(bf16).astype(f32)
    grads = jnp.sum(hidden * down_grad, axis=-1, keepdims=True).astype(bf16).astype(f32)
    gate_grad = (down_grad * up_pre * sig * (1.0 + gate_pre * (1.0 - sig))).astype(bf16)
    up_grad = (down_grad * act).astype(bf16)
    for j in range(8):
        part = pl.ds(j * 256, 256)
        put_rows(wide_ref, j, dot(gate_grad, gate_ref[part, :], ACROSS) + dot(up_grad, up_ref[part, :], ACROSS))
    p, lane = iota((SLOTS, 128), 0), iota((SLOTS, 128), 1)
    gather = marks(iota((PEERS * 8, SLOTS), 1) // MOST == iota((PEERS * 8, SLOTS), 0) // 8)
    small = jnp.zeros((PEERS * 8, 128), f32)
    for half in range(2):
        spread = jnp.where(lane == p % MOST + half * MOST, grads[half * SLOTS : (half + 1) * SLOTS], 0.0)
        small = small + dot(gather, spread.astype(bf16))
    wide_ref[0, pl.ds(2 * AREA, PEERS * 8), :] = small

    def put(d, rows):
        for lane in range(2):
            for half in range(2):
                back_ref[d, pl.ds(half * ROWS, ROWS), LANES[lane]] = wide_ref[lane, area_rows(d, half), :].astype(bf16)
        tail = pl.ds(2 * ROWS, 8)
        extra = wide_ref[0, pl.ds(pl.multiple_of(2 * AREA + d * 8, 8), 8), :].astype(bf16)
        back_ref[d, tail, LANES[0]] = extra
        back_ref[d, tail, LANES[1]] = extra

    each_peer(put)


WEIGHTS = [
    pltpu.VMEM((D, FF), bf16),
    pltpu.VMEM((D, FF), bf16),
    pltpu.VMEM((FF, D), bf16),
    pltpu.SemaphoreType.DMA((3,)),
]


def run_behind_experts(*args):
    return call(
        behind_experts,
        (shape((PEERS, 2 * ROWS + 8, 256)),),
        [VMEM] * 2 + [HBM] * 3,
        [pltpu.VMEM((2, 4 * AREA, 128), f32)] + WEIGHTS,
        args,
        9 * 10**9,
        17,
    )[0]


def ahead_experts(
    near_ref, far_ref, gate_hbm, up_hbm, down_hbm, first_ref, second_ref, wide_ref, gate_ref, up_ref, down_ref, sems
):
    copies = fetched(((gate_hbm, gate_ref), (up_hbm, up_ref), (down_hbm, down_ref)), sems)
    count = 2 * SLOTS

    def take(d, rows):
        for lane in range(2):
            wide_ref[lane, area_rows(d, 0), :] = near_ref[d, pl.ds(2 * ROWS, ROWS), LANES[lane]].astype(f32)
            wide_ref[lane, area_rows(d, 1), :] = far_ref[d, :, LANES[lane]].astype(f32)

    each_peer(take)
    copies[0].wait()
    copies[1].wait()
    gate_pre, up_pre = jnp.zeros((count, FF), f32), jnp.zeros((count, FF), f32)
    for j in range(4):
        rows = jnp.concatenate([get_rows(wide_ref, 2 * j, count), get_rows(wide_ref, 2 * j + 1, count)], axis=1)
        gate_pre = gate_pre + dot(rows, gate_ref[pl.ds(j * 512, 512), :])
        up_pre = up_pre + dot(rows, up_ref[pl.ds(j * 512, 512), :])
    hidden = (gate_pre / (1.0 + jnp.exp(-gate_pre)) * up_pre).astype(bf16)
    copies[2].wait()
    for c in range(8):
        made = dot(hidden, down_ref[:, pl.ds(c * 256, 256)])
        for i in range(2):
            wide_ref[c // 4, pl.ds(2 * (c % 4) + i, count, stride=8), :] = made[:, i * 128 : i * 128 + 128]

    def put(d, rows):
        for half in range(2):
            first_ref[d, pl.ds(half * ROWS, ROWS), :] = wide_ref[0, area_rows(d, half), :].astype(bf16)
            second_ref[d, pl.ds(half * ROWS, ROWS), :] = wide_ref[1, area_rows(d, half), :].astype(bf16)

    each_peer(put)


def run_ahead_experts(*args):
    return call(
        ahead_experts,
        (shape((PEERS, 2 * ROWS, 128)), shape((PEERS, 2 * ROWS, 128))),
        [VMEM] * 2 + [HBM] * 3,
        [pltpu.VMEM((2, 2 * AREA, 128), f32)] + WEIGHTS,
        args,
        6 * 10**9,
        14,
    )


def attend(length_ref, x_ref, q_ref, kc_ref, kn_ref, vc_ref, vn_ref, resid_ref):
    length = length_ref[0, 0]
    row, col = iota((TOK, 2 * TOK), 0), iota((TOK, 2 * TOK), 1)
    visible = ((col < TOK) & (col < length)) | ((col >= TOK) & (col - TOK <= row))
    for kv in range(KV_HEADS):
        part = pl.ds(kv * HEAD_DIM, HEAD_DIM)
        keys = jnp.concatenate([kc_ref[:, part], kn_ref[:, part]], axis=0)
        values = jnp.concatenate([vc_ref[:, part], vn_ref[:, part]], axis=0)
        for h in range(HEADS // KV_HEADS):
            cols = pl.ds((kv * (HEADS // KV_HEADS) + h) * HEAD_DIM, HEAD_DIM)
            scores = dot(q_ref[:, cols], keys, ACROSS) * HEAD_DIM ** (-0.5)
            scores = jnp.where(visible, scores, far_below)
            lifted = jnp.exp(scores - jnp.max(scores, axis=-1, keepdims=True))
            weights = (lifted * (1.0 / jnp.sum(lifted, axis=-1, keepdims=True))).astype(bf16)
            mixed = dot(weights, values).astype(bf16)
            resid_ref[:, cols] = (x_ref[:, cols].astype(f32) + mixed.astype(f32)).astype(bf16)


def run_attend(length, x, q, kc, kn, vc, vn):
    return call(
        attend,
        (shape((TOK, D)),),
        [SMEM] + [VMEM] * 6,
        [],
        (length, x, q, kc, kn, vc, vn),
        3 * 10**9,
        8,
    )[0]


def through_norm(sums, gain, inv, unit):
    scaled = sums * gain
    return inv * (scaled - unit * jnp.mean(scaled * unit, axis=-1, keepdims=True))


def behind_sums(
    zh_ref, home_ref, near_hot_ref, far_hot_ref, near_probs_ref, far_probs_ref, near_x_ref, far_x_ref, gain_ref,
    sums_ref, sent_ref, note_ref, mine_ref, wide_ref, line_ref
):
    zh = zh_ref[0]

    def take(d, rows):
        for half in range(2):
            for lane in range(2):
                wide_ref[lane, area_rows(d, half), :] = home_ref[d, pl.ds(half * ROWS, ROWS), LANES[lane]].astype(f32)
        wide_ref[0, pl.ds(pl.multiple_of(2 * AREA + d * 8, 8), 8), :] = home_ref[
            d, pl.ds(2 * ROWS, 8), LANES[0]
        ].astype(f32)

    each_peer(take)
    pick = picks(iota((SLOTS, EXPERTS), 0) // MOST, zh)
    near_mix = near_hot_ref[...] * dot(pick, near_probs_ref[...].astype(bf16)).astype(bf16)
    far_mix = far_hot_ref[...] * dot(pick, far_probs_ref[...].astype(bf16)).astype(bf16)
    small = wide_ref[0, pl.ds(2 * AREA, PEERS * 8), :].astype(bf16)
    share = marks(iota((SLOTS, PEERS * 8), 0) // MOST * 8 == iota((SLOTS, PEERS * 8), 1))
    small = dot(share, small)
    p, lane = iota((SLOTS, 128), 0) % MOST, iota((SLOTS, 128), 1)
    for half, hot in enumerate((near_hot_ref, far_hot_ref)):
        grads = jnp.sum(jnp.where(lane == p + half * MOST, small, 0.0), axis=-1, keepdims=True)
        note_ref[pl.ds(0, EXPERTS), pl.ds(half * TOK, TOK)] = dot(
            (pick.astype(f32) * grads).astype(bf16), hot[...], DOWN
        )
    for j in range(8):
        cols = pl.ds(j * 256, 256)
        sums_ref[:, cols] = dot(near_mix, get_rows(wide_ref, j, SLOTS), DOWN)
        line_ref[:, cols] = dot(far_mix, get_rows(wide_ref, j, SLOTS, AREA), DOWN)
    inv, unit = unit_rows(far_x_ref[...])
    sums = line_ref[...]
    sent_ref[...] = through_norm(sums, gain_ref[...], inv, unit).astype(bf16)
    total = jnp.sum(sums * unit, axis=0, keepdims=True)
    _, unit = unit_rows(near_x_ref[...])
    total = total + jnp.sum(sums_ref[...] * unit, axis=0, keepdims=True)
    note_ref[pl.ds(EXPERTS, 8), :] = jnp.zeros((8, 256), f32)
    mine_ref[...] = jnp.zeros((8, 256), f32)
    for x in range(4):
        first, second = total[:, x * 512 : x * 512 + 256], total[:, x * 512 + 256 : x * 512 + 512]
        mine_ref[pl.ds(x, 1), :] = jnp.where(zh == 0, first, second)
        note_ref[pl.ds(EXPERTS + x, 1), :] = jnp.where(zh == 0, second, first)


def run_behind_sums(*args):
    return call(
        behind_sums,
        (shape((TOK, D), f32), shape((TOK, D)), shape((EXPERTS + 8, 256), f32), shape((8, 256), f32)),
        [SMEM] + [VMEM] * 8,
        [pltpu.VMEM((2, 2 * AREA + PEERS * 8, 128), f32), pltpu.VMEM((TOK, D), f32)],
        args,
        10**9,
        6,
    )


def behind_end(
    zh_ref, near_note_ref, far_note_ref, mine_ref, sums_ref, near_probs_ref, far_probs_ref, near_normed_ref,
    far_normed_ref, near_x_ref, far_x_ref, g_ref, gain_ref, table_ref, sent_ref, shares_ref
):
    zh = zh_ref[0]
    near_tok, far_tok = pl.ds(0, TOK), pl.ds(TOK, TOK)
    rows = pl.ds(0, EXPERTS)

    def logit_grads(probs, grads):
        return (probs * (grads - jnp.sum(probs * grads, axis=0, keepdims=True))).astype(bf16)

    near_logit = logit_grads(near_probs_ref[...], near_note_ref[rows, near_tok] + far_note_ref[rows, far_tok])
    far_logit = logit_grads(far_probs_ref[...], near_note_ref[rows, far_tok] + far_note_ref[rows, near_tok])
    inv, near_unit = unit_rows(near_x_ref[...])
    _, far_unit = unit_rows(far_x_ref[...])
    near_term = dot(near_logit, table_ref[...], DOWN)
    sums = sums_ref[...] + near_term
    sent_ref[...] = (g_ref[...].astype(f32) + through_norm(sums, gain_ref[...], inv, near_unit)).astype(bf16)
    far_term = dot(far_logit, table_ref[...], DOWN)
    total = jnp.sum(near_term * near_unit + far_term * far_unit, axis=0, keepdims=True)
    row = iota((128 - EXPERTS, 256), 0)
    for x in range(4):
        first, second = total[:, x * 512 : x * 512 + 256], total[:, x * 512 + 256 : x * 512 + 512]
        gains = (
            jnp.where(zh == 0, first, second)
            + mine_ref[pl.ds(x, 1), :]
            + far_note_ref[pl.ds(EXPERTS + x, 1), :]
        )
        cols = pl.ds(pl.multiple_of(x * 512 + zh * 256, 256), 256)
        part = dot(near_logit, near_normed_ref[:, cols]) + dot(far_logit, far_normed_ref[:, cols])
        both = jnp.concatenate([part, jnp.where(row == 0, gains, 0.0)], axis=0)
        shares_ref[pl.ds(x * 256, 256), :] = both.T


def run_behind_end(*args):
    return call(
        behind_end,
        (shape((TOK, D)), shape((D // 2, 128), f32)),
        [SMEM] + [VMEM] * 13,
        [],
        args,
        10**9,
        6,
    )


def ahead_end(home_ref, near_mix_ref, far_mix_ref, resid_ref, near_ref, far_ref, wide_ref):
    def take(d, rows):
        for half in range(2):
            wide_ref[0, area_rows(d, half), :] = home_ref[d, pl.ds(half * ROWS, ROWS), :].astype(f32)

    each_peer(take)
    for c in range(4):
        cols = pl.ds(c * 256, 256)
        for half, (mix_ref, out_ref) in enumerate(((near_mix_ref, near_ref), (far_mix_ref, far_ref))):
            rows = jnp.concatenate([get_rows(wide_ref, 2 * c + i, SLOTS, half * AREA) for i in range(2)], axis=1)
            sums = dot(mix_ref[...], rows, DOWN)
            if half == 0:
                sums = sums + resid_ref[:, cols].astype(f32)
            out_ref[:, cols] = sums.astype(bf16)


def run_ahead_end(home, near_mix, far_mix, resid, part):
    columns = pl.BlockSpec((TOK, D // 2), lambda i: (0, part))
    whole = [pl.BlockSpec(a.shape, lambda i, n=a.ndim: (0,) * n) for a in (home, near_mix, far_mix)]
    half = pl.BlockSpec((TOK, D // 2), lambda i: (0, 0))
    return pl.pallas_call(
        ahead_end,
        grid=(1,),
        out_shape=(shape((TOK, D // 2)), shape((TOK, D // 2))),
        in_specs=whole + [columns],
        out_specs=(half, half),
        scratch_shapes=[pltpu.VMEM((1, 2 * AREA, 128), f32)],
        compiler_params=pltpu.CompilerParams(vmem_limit_bytes=60 * 2**20),
        cost_estimate=pl.CostEstimate(flops=10**9, transcendentals=0, bytes_accessed=3 * 2**20),
    )(home, near_mix, far_mix, resid)


def final_add(a_ref, b_ref, c_ref, d_ref, out_ref):
    half = D // 2
    out_ref[:, pl.ds(0, half)] = (a_ref[...].astype(f32) + b_ref[...].astype(f32)).astype(bf16)
    out_ref[:, pl.ds(half, half)] = (c_ref[...].astype(f32) + d_ref[...].astype(f32)).astype(bf16)


def run_final_add(*args):
    return call(final_add, (shape((TOK, D)),), [VMEM] * 4, [], args, 10**6, 2)[0]


def body(
    forward_input,
    queries,
    new_keys,
    new_values,
    cache_keys,
    cache_values,
    context_lengths,
    norm_gain,
    router,
    gate_weight,
    up_weight,
    down_weight,
    forward_ids,
    backward_input,
    backward_ids,
    output_grad,
):
    zh = lax.axis_index("zh").astype(jnp.int32).reshape(1)
    gain = norm_gain
    table = router[0].T
    weights = (gate_weight[0, 0], up_weight[0, 0], down_weight[0, 0])
    back_x, back_g = backward_input[0], output_grad[0]
    ids_b, ids_f = backward_ids[0].T, forward_ids[0].T
    ids_far = swapped(jnp.concatenate([ids_b, ids_f], axis=0))
    x_far = swapped(back_x)
    g_far = swapped(back_g)
    resid = run_attend(
        context_lengths,
        forward_input[0],
        queries[0],
        cache_keys[0],
        new_keys[0],
        cache_values[0],
        new_values[0],
    )
    resid_far = swapped(resid)
    sent_1, normed_b, hot_b, probs_b, mix_f = run_near_pack(
        zh, ids_b, ids_f, back_x, back_g, resid, gain, table
    )
    got_1 = spread_out(sent_1)
    sent_2, normed_c, hot_c, probs_c = run_far_pack(zh, ids_far[:4], x_far, g_far, gain, table)
    sent_2, _ = lax.optimization_barrier((sent_2, got_1))
    got_2 = spread_out(sent_2)
    sent_3, mix_h = run_ahead_pack(zh, ids_far[4:], resid_far, gain, table)
    sent_3, got_2 = lax.optimization_barrier((sent_3, got_2))
    got_3 = spread_out(sent_3)
    back = run_behind_experts(got_1, got_2, *weights)
    back, got_3 = lax.optimization_barrier((back, got_3))
    home_b = spread_out(back)
    made_1, made_2 = run_ahead_experts(got_1, got_3, *weights)
    made_1, home_b = lax.optimization_barrier((made_1, home_b))
    home_1 = spread_out(made_1)
    sums_b, own_c, note, mine = run_behind_sums(
        zh, home_b, hot_b, hot_c, probs_b, probs_c, back_x, x_far, gain
    )
    far_note = swapped(note)
    moved_c = moved(own_c, False, -1)
    own_b, shares = run_behind_end(
        zh, note, far_note, mine, sums_b, probs_b, probs_c, normed_b, normed_c, back_x, x_far, back_g, gain, table
    )
    moved_b = moved(own_b, True, -1)
    made_2, home_1 = lax.optimization_barrier((made_2, home_1))
    home_2 = spread_out(made_2)
    own_f1, own_h1 = run_ahead_end(home_1, mix_f, mix_h, resid, 0)
    moved_h1 = moved(own_h1, False, 1)
    moved_f1 = moved(own_f1, True, 1)
    own_f2, own_h2 = run_ahead_end(home_2, mix_f, mix_h, resid, 1)
    moved_h2 = moved(own_h2, False, 1)
    moved_f2 = moved(own_f2, True, 1)
    shares, own_f2 = lax.optimization_barrier((shares, own_f2))
    total = jnp.sum(spread_out(shares.reshape(PEERS, PEERS, 128)), axis=0) * factor
    input_grad = (moved_b.astype(f32) + moved_c.astype(f32)).astype(bf16)
    forward_output = run_final_add(moved_f1, moved_h1, moved_f2, moved_h2)
    return (
        forward_output[None],
        input_grad[None],
        total[None, :, :EXPERTS],
        total[:, EXPERTS][None],
    )


def solution(mesh):
    grid = Mesh(mesh.devices.reshape(4, 4, 2, 4, 2), ("pipe", "x", "zh", "y", "core"))
    rows = P("pipe", ALL, None)
    placed = (
        rows,
        rows,
        rows,
        rows,
        rows,
        rows,
        P("pipe", ALL),
        P("pipe", None),
        P("pipe", None, None),
        P("pipe", ALL, None, None),
        P("pipe", ALL, None, None),
        P("pipe", ALL, None, None),
        rows,
        rows,
        rows,
        rows,
    )
    return jax.shard_map(
        body,
        mesh=grid,
        in_specs=placed,
        out_specs=(rows, rows, rows, P("pipe", ALL)),
        check_vma=False,
    )
```

```python
import jax
import jax.numpy as jnp
from jax import lax
from jax.experimental import pallas as pl
from jax.experimental.pallas import tpu as pltpu
from jax.sharding import Mesh, PartitionSpec as P


HEADS = 16
KV_HEADS = 2
HEAD_DIM = 128
D = 2048
FF = 768
EXPERTS = 64
MOST = 9
TOK = 128
PEERS = 32
SLOTS = PEERS * MOST
ROWS = MOST * 8
AREA = SLOTS * 8
XY = ("x", "y", "core")
ALL = ("x", "zh", "y", "core")

epsilon = 1e-06
far_below = -1e30
factor = 8192 ** (-0.5)
bf16 = jnp.bfloat16
f32 = jnp.float32
ACROSS = (((1,), (1,)), ((), ()))
DOWN = (((0,), (0,)), ((), ()))
VMEM = pl.BlockSpec(memory_space=pltpu.VMEM)
SMEM = pl.BlockSpec(memory_space=pltpu.SMEM)
HBM = pl.BlockSpec(memory_space=pltpu.HBM)


def spread_out(x):
    return lax.all_to_all(x, XY, 0, 0, tiled=True)


def swapped(x):
    return lax.ppermute(x, "zh", [(0, 1), (1, 0)])


def moved(x, same, step):
    pairs = []
    for pipe in range(4):
        for zh in range(2):
            to = ((pipe + step) % 4) * 2 + (zh if same else 1 - zh)
            pairs.append((pipe * 2 + zh, to))
    return lax.ppermute(x, ("pipe", "zh"), pairs)


def shape(dims, dtype=bf16):
    return jax.ShapeDtypeStruct(dims, dtype)


def call(kernel, outs, ins, scratch, args, flops, mib):
    return pl.pallas_call(
        kernel,
        out_shape=outs,
        in_specs=ins,
        out_specs=tuple(VMEM for _ in outs),
        scratch_shapes=scratch,
        compiler_params=pltpu.CompilerParams(vmem_limit_bytes=63 * 2**20),
        cost_estimate=pl.CostEstimate(
            flops=flops, transcendentals=0, bytes_accessed=mib * 2**20
        ),
    )(*args)


def dot(a, b, dims=None):
    if dims is None:
        return jnp.dot(a, b, preferred_element_type=f32)
    return lax.dot_general(a, b, dims, preferred_element_type=f32)


def iota(dims, dim):
    return lax.broadcasted_iota(jnp.int32, dims, dim)


def marks(cond):
    return cond.astype(f32).astype(bf16)


def unit_rows(x):
    wide = x.astype(f32)
    inv_rms = lax.rsqrt(jnp.mean(wide * wide, axis=-1, keepdims=True) + epsilon)
    return inv_rms, wide * inv_rms


def hits(ids):
    expert = iota((EXPERTS, ids.shape[1]), 0)
    hit = ids[0:1, :] == expert
    for k in range(1, 4):
        hit = hit | (ids[k : k + 1, :] == expert)
    return hit


def choice(normed, table, hit):
    logits = jnp.where(hit, dot(table, normed, ACROSS), far_below)
    lifted = jnp.where(hit, jnp.exp(logits - jnp.max(logits, axis=0, keepdims=True)), 0.0)
    return lifted / jnp.sum(lifted, axis=0, keepdims=True)


def ranked(hit):
    tokens = hit.shape[1]
    earlier, later = iota((tokens, tokens), 0), iota((tokens, tokens), 1)
    before = marks((earlier < later) & (earlier // TOK == later // TOK))
    hit = hit.astype(f32)
    return (hit * (dot(hit.astype(bf16), before) + 1.0)).astype(bf16)


def picks(peer, zh):
    owner = (peer // 8) * 16 + zh * 8 + peer % 8
    return marks(owner == iota(peer.shape, 1))


def each_peer(step):
    def turn(d, carry):
        step(d, pl.ds(pl.multiple_of(d * ROWS, 8), ROWS))
        return carry

    lax.fori_loop(0, PEERS, turn, 0)


def area_rows(d, area):
    return pl.ds(pl.multiple_of(d * ROWS + area * AREA, 8), ROWS)


LANES = (pl.ds(0, 128), pl.ds(128, 128))


def put_rows(wide_ref, j, rows, start=0):
    for lane in range(rows.shape[1] // 128):
        wide_ref[lane, pl.ds(start + j, rows.shape[0], stride=8), :] = rows[
            :, lane * 128 : lane * 128 + 128
        ]


def get_rows(wide_ref, j, count, start=0):
    return jnp.concatenate(
        [
            wide_ref[lane, pl.ds(start + j, count, stride=8), :].astype(bf16)
            for lane in range(wide_ref.shape[0])
        ],
        axis=1,
    )


def routed(ids, x, zh, gain, table):
    hit = hits(ids)
    _, unit = unit_rows(x)
    normed = (unit * gain).astype(bf16)
    probs = choice(normed, table, hit)
    pick = picks(iota((SLOTS, EXPERTS), 0) // MOST, zh)
    slot = (iota((SLOTS, TOK), 0) % MOST + 1).astype(f32)
    return normed, probs, pick, marks(dot(pick, ranked(hit)) == slot)


def mixed_by(onehot, pick, probs):
    return onehot * dot(pick, probs.astype(bf16)).astype(bf16)


def loop(count, step):
    def turn(i, carry):
        step(i)
        return carry

    lax.fori_loop(0, count, turn, 0)


def columns(j, width):
    return pl.ds(pl.multiple_of(j * width, width), width)


def fill_looped(wide_ref, area, onehot_ref, rows_ref):
    def step(j):
        put_rows(wide_ref, j, dot(onehot_ref[...], rows_ref[:, columns(j, 256)]), area * AREA)

    loop(8, step)


def fill(wide_ref, area, onehot, rows_ref):
    for j in range(8):
        put_rows(wide_ref, j, dot(onehot, rows_ref[:, pl.ds(j * 256, 256)]), area * AREA)


def give(wide_ref, sent_ref, areas):
    def step(d, rows):
        for area in range(areas):
            for lane in range(2):
                sent_ref[d, pl.ds(area * ROWS, ROWS), LANES[lane]] = wide_ref[lane, area_rows(d, area), :].astype(bf16)

    each_peer(step)


def near_pack(
    zh_ref, ids_ref, ahead_ids_ref, x_ref, g_ref, resid_ref, gain_ref, table_ref,
    sent_ref, normed_ref, onehot_ref, probs_ref, mix_ref, wide_ref, rows_ref
):
    zh, gain, table = zh_ref[0], gain_ref[...], table_ref[...]
    normed_ref[...], probs_ref[...], _, onehot_ref[...] = routed(ids_ref[...], x_ref[...], zh, gain, table)
    fill(wide_ref, 0, onehot_ref[...], normed_ref)
    fill(wide_ref, 1, onehot_ref[...], g_ref)
    rows_ref[...], probs, pick, onehot = routed(ahead_ids_ref[...], resid_ref[...], zh, gain, table)
    mix_ref[...] = mixed_by(onehot, pick, probs)
    fill(wide_ref, 2, onehot, rows_ref)
    give(wide_ref, sent_ref, 3)


def run_near_pack(*args):
    return call(
        near_pack,
        (
            shape((PEERS, 3 * ROWS, 256)),
            shape((TOK, D)),
            shape((SLOTS, TOK)),
            shape((EXPERTS, TOK), f32),
            shape((SLOTS, TOK)),
        ),
        [SMEM] + [VMEM] * 7,
        [pltpu.VMEM((2, 3 * AREA, 128), f32), pltpu.VMEM((TOK, D), bf16)],
        args,
        2 * 10**9,
        8,
    )


def far_pack(
    zh_ref, ids_ref, x_ref, g_ref, gain_ref, table_ref, sent_ref, normed_ref, onehot_ref, probs_ref, wide_ref
):
    normed_ref[...], probs_ref[...], _, onehot_ref[...] = routed(
        ids_ref[...], x_ref[...], zh_ref[0], gain_ref[...], table_ref[...]
    )
    fill_looped(wide_ref, 0, onehot_ref, normed_ref)
    fill_looped(wide_ref, 1, onehot_ref, g_ref)
    give(wide_ref, sent_ref, 2)


def run_far_pack(*args):
    return call(
        far_pack,
        (shape((PEERS, 2 * ROWS, 256)), shape((TOK, D)), shape((SLOTS, TOK)), shape((EXPERTS, TOK), f32)),
        [SMEM] + [VMEM] * 5,
        [pltpu.VMEM((2, 2 * AREA, 128), f32)],
        args,
        10**9,
        6,
    )


def ahead_pack(zh_ref, ids_ref, x_ref, gain_ref, table_ref, sent_ref, mix_ref, wide_ref, rows_ref, onehot_ref):
    rows_ref[...], probs, pick, onehot = routed(ids_ref[...], x_ref[...], zh_ref[0], gain_ref[...], table_ref[...])
    mix_ref[...] = mixed_by(onehot, pick, probs)
    onehot_ref[...] = onehot
    fill_looped(wide_ref, 0, onehot_ref, rows_ref)
    give(wide_ref, sent_ref, 1)


def run_ahead_pack(*args):
    return call(
        ahead_pack,
        (shape((PEERS, ROWS, 256)), shape((SLOTS, TOK))),
        [SMEM] + [VMEM] * 4,
        [pltpu.VMEM((2, AREA, 128), f32), pltpu.VMEM((TOK, D), bf16), pltpu.VMEM((SLOTS, TOK), bf16)],
        args,
        10**9,
        4,
    )


def fetched(pairs, sems):
    copies = [pltpu.make_async_copy(a, b, sems.at[i]) for i, (a, b) in enumerate(pairs)]
    for copy in copies:
        copy.start()
    return copies


def behind_half(got_ref, weights, place, wide_ref, sems):
    (gate_hbm, gate_ref), (up_hbm, up_ref), (down_hbm, down_ref) = weights
    copies = fetched(weights, sems)

    def take(d, rows):
        for lane in range(2):
            for kind in range(2):
                wide_ref[lane, area_rows(d, kind), :] = got_ref[d, pl.ds(kind * ROWS, ROWS), LANES[lane]].astype(f32)

    each_peer(take)
    copies[0].wait()
    copies[1].wait()
    gate_pre, up_pre = jnp.zeros((SLOTS, FF), f32), jnp.zeros((SLOTS, FF), f32)
    for j in range(4):
        rows = jnp.concatenate([get_rows(wide_ref, 2 * j + i, SLOTS) for i in range(2)], axis=1)
        gate_pre = gate_pre + dot(rows, gate_ref[pl.ds(j * 512, 512), :])
        up_pre = up_pre + dot(rows, up_ref[pl.ds(j * 512, 512), :])
    copies[2].wait()
    down_grad = jnp.zeros((SLOTS, FF), f32)
    for j in range(4):
        rows = jnp.concatenate([get_rows(wide_ref, 2 * j + i, SLOTS, AREA) for i in range(2)], axis=1)
        down_grad = down_grad + dot(rows, down_ref[:, pl.ds(j * 512, 512)], ACROSS)
    sig = 1.0 / (1.0 + jnp.exp(-gate_pre))
    act = gate_pre * sig
    hidden = (act * up_pre).astype(bf16).astype(f32)
    grads = jnp.sum(hidden * down_grad, axis=-1, keepdims=True).astype(bf16).astype(f32)
    gate_grad = (down_grad * up_pre * sig * (1.0 + gate_pre * (1.0 - sig))).astype(bf16)
    up_grad = (down_grad * act).astype(bf16)
    for j in range(8):
        part = pl.ds(j * 256, 256)
        put_rows(wide_ref, j, dot(gate_grad, gate_ref[part, :], ACROSS) + dot(up_grad, up_ref[part, :], ACROSS))
    p, lane = iota((SLOTS, 128), 0), iota((SLOTS, 128), 1)
    gather = marks(iota((PEERS * 8, SLOTS), 1) // MOST == iota((PEERS * 8, SLOTS), 0) // 8)
    spread = jnp.where(lane == p % MOST + place * MOST, grads, 0.0)
    return dot(gather, spread.astype(bf16))


def near_experts(
    got_ref, gate_hbm, up_hbm, down_hbm, back_ref, small_ref, wide_ref, gate_ref, up_ref, down_ref, sems
):
    weights = ((gate_hbm, gate_ref), (up_hbm, up_ref), (down_hbm, down_ref))
    small_ref[...] = behind_half(got_ref, weights, 0, wide_ref, sems)

    def put(d, rows):
        for lane in range(2):
            back_ref[d, :, LANES[lane]] = wide_ref[lane, rows, :].astype(bf16)

    each_peer(put)


def far_experts(
    got_ref, near_ref, near_small_ref, gate_hbm, up_hbm, down_hbm, back_ref, wide_ref, gate_ref, up_ref, down_ref, sems
):
    weights = ((gate_hbm, gate_ref), (up_hbm, up_ref), (down_hbm, down_ref))
    small = behind_half(got_ref, weights, 1, wide_ref, sems) + near_small_ref[...]
    wide_ref[0, pl.ds(AREA, PEERS * 8), :] = small

    def put(d, rows):
        for lane in range(2):
            back_ref[d, pl.ds(0, ROWS), LANES[lane]] = near_ref[d, :, LANES[lane]]
            back_ref[d, pl.ds(ROWS, ROWS), LANES[lane]] = wide_ref[lane, rows, :].astype(bf16)
        extra = wide_ref[0, pl.ds(pl.multiple_of(AREA + d * 8, 8), 8), :].astype(bf16)
        back_ref[d, pl.ds(2 * ROWS, 8), LANES[0]] = extra
        back_ref[d, pl.ds(2 * ROWS, 8), LANES[1]] = extra

    each_peer(put)


WEIGHTS = [
    pltpu.VMEM((D, FF), bf16),
    pltpu.VMEM((D, FF), bf16),
    pltpu.VMEM((FF, D), bf16),
    pltpu.SemaphoreType.DMA((3,)),
]


def run_near_experts(*args):
    return call(
        near_experts,
        (shape((PEERS, ROWS, 256)), shape((PEERS * 8, 128), f32)),
        [VMEM] + [HBM] * 3,
        [pltpu.VMEM((2, 2 * AREA, 128), f32)] + WEIGHTS,
        args,
        5 * 10**9,
        13,
    )


def run_far_experts(*args):
    return call(
        far_experts,
        (shape((PEERS, 2 * ROWS + 8, 256)),),
        [VMEM] * 3 + [HBM] * 3,
        [pltpu.VMEM((2, 2 * AREA, 128), f32)] + WEIGHTS,
        args,
        5 * 10**9,
        15,
    )[0]


def ahead_experts(
    near_ref, far_ref, gate_hbm, up_hbm, down_hbm, first_ref, second_ref, wide_ref, gate_ref, up_ref, down_ref, sems,
    gate_sum, up_sum, hidden_ref
):
    copies = fetched(((gate_hbm, gate_ref), (up_hbm, up_ref), (down_hbm, down_ref)), sems)
    count = 2 * SLOTS

    def take(d, rows):
        for lane in range(2):
            wide_ref[lane, area_rows(d, 0), :] = near_ref[d, pl.ds(2 * ROWS, ROWS), LANES[lane]].astype(f32)
            wide_ref[lane, area_rows(d, 1), :] = far_ref[d, :, LANES[lane]].astype(f32)

    each_peer(take)
    copies[0].wait()
    copies[1].wait()
    gate_sum[...] = jnp.zeros((count, FF), f32)
    up_sum[...] = jnp.zeros((count, FF), f32)

    def inward(j):
        rows = jnp.concatenate([get_rows(wide_ref, 2 * j, count), get_rows(wide_ref, 2 * j + 1, count)], axis=1)
        gate_sum[...] += dot(rows, gate_ref[columns(j, 512), :])
        up_sum[...] += dot(rows, up_ref[columns(j, 512), :])

    loop(4, inward)
    gate_pre = gate_sum[...]
    hidden_ref[...] = (gate_pre / (1.0 + jnp.exp(-gate_pre)) * up_sum[...]).astype(bf16)
    copies[2].wait()

    def outward(c):
        for part in range(2):
            made = dot(hidden_ref[...], down_ref[:, columns(part * 4 + c, 256)])
            for i in range(2):
                wide_ref[part, pl.ds(2 * c + i, count, stride=8), :] = made[:, i * 128 : i * 128 + 128]

    loop(4, outward)

    def put(d, rows):
        for half in range(2):
            first_ref[d, pl.ds(half * ROWS, ROWS), :] = wide_ref[0, area_rows(d, half), :].astype(bf16)
            second_ref[d, pl.ds(half * ROWS, ROWS), :] = wide_ref[1, area_rows(d, half), :].astype(bf16)

    each_peer(put)


def run_ahead_experts(*args):
    return call(
        ahead_experts,
        (shape((PEERS, 2 * ROWS, 128)), shape((PEERS, 2 * ROWS, 128))),
        [VMEM] * 2 + [HBM] * 3,
        [pltpu.VMEM((2, 2 * AREA, 128), f32)]
        + WEIGHTS
        + [pltpu.VMEM((2 * SLOTS, FF), f32), pltpu.VMEM((2 * SLOTS, FF), f32), pltpu.VMEM((2 * SLOTS, FF), bf16)],
        args,
        6 * 10**9,
        14,
    )


def attend(length_ref, x_ref, q_ref, kc_ref, kn_ref, vc_ref, vn_ref, resid_ref):
    length = length_ref[0, 0]
    row, col = iota((TOK, 2 * TOK), 0), iota((TOK, 2 * TOK), 1)
    visible = ((col < TOK) & (col < length)) | ((col >= TOK) & (col - TOK <= row))
    for kv in range(KV_HEADS):
        part = pl.ds(kv * HEAD_DIM, HEAD_DIM)
        keys = jnp.concatenate([kc_ref[:, part], kn_ref[:, part]], axis=0)
        values = jnp.concatenate([vc_ref[:, part], vn_ref[:, part]], axis=0)
        for h in range(HEADS // KV_HEADS):
            cols = pl.ds((kv * (HEADS // KV_HEADS) + h) * HEAD_DIM, HEAD_DIM)
            scores = dot(q_ref[:, cols], keys, ACROSS) * HEAD_DIM ** (-0.5)
            scores = jnp.where(visible, scores, far_below)
            lifted = jnp.exp(scores - jnp.max(scores, axis=-1, keepdims=True))
            weights = (lifted * (1.0 / jnp.sum(lifted, axis=-1, keepdims=True))).astype(bf16)
            mixed = dot(weights, values).astype(bf16)
            resid_ref[:, cols] = (x_ref[:, cols].astype(f32) + mixed.astype(f32)).astype(bf16)


def run_attend(length, x, q, kc, kn, vc, vn):
    return call(
        attend,
        (shape((TOK, D)),),
        [SMEM] + [VMEM] * 6,
        [],
        (length, x, q, kc, kn, vc, vn),
        3 * 10**9,
        8,
    )[0]


def through_norm(sums, gain, inv, unit):
    scaled = sums * gain
    return inv * (scaled - unit * jnp.mean(scaled * unit, axis=-1, keepdims=True))


def behind_sums(
    zh_ref, home_ref, near_hot_ref, far_hot_ref, near_probs_ref, far_probs_ref, near_x_ref, far_x_ref, gain_ref,
    sums_ref, sent_ref, note_ref, mine_ref, wide_ref, line_ref, mix_ref
):
    zh = zh_ref[0]

    def take(d, rows):
        for half in range(2):
            for lane in range(2):
                wide_ref[lane, area_rows(d, half), :] = home_ref[d, pl.ds(half * ROWS, ROWS), LANES[lane]].astype(f32)
        wide_ref[0, pl.ds(pl.multiple_of(2 * AREA + d * 8, 8), 8), :] = home_ref[
            d, pl.ds(2 * ROWS, 8), LANES[0]
        ].astype(f32)

    each_peer(take)
    pick = picks(iota((SLOTS, EXPERTS), 0) // MOST, zh)
    near_mix = near_hot_ref[...] * dot(pick, near_probs_ref[...].astype(bf16)).astype(bf16)
    far_mix = far_hot_ref[...] * dot(pick, far_probs_ref[...].astype(bf16)).astype(bf16)
    small = wide_ref[0, pl.ds(2 * AREA, PEERS * 8), :].astype(bf16)
    share = marks(iota((SLOTS, PEERS * 8), 0) // MOST * 8 == iota((SLOTS, PEERS * 8), 1))
    small = dot(share, small)
    p, lane = iota((SLOTS, 128), 0) % MOST, iota((SLOTS, 128), 1)
    for half, hot in enumerate((near_hot_ref, far_hot_ref)):
        grads = jnp.sum(jnp.where(lane == p + half * MOST, small, 0.0), axis=-1, keepdims=True)
        note_ref[pl.ds(0, EXPERTS), pl.ds(half * TOK, TOK)] = dot(
            (pick.astype(f32) * grads).astype(bf16), hot[...], DOWN
        )
    mix_ref[0] = near_mix
    mix_ref[1] = far_mix

    def gather(j):
        cols = columns(j, 256)
        sums_ref[:, cols] = dot(mix_ref[0], get_rows(wide_ref, j, SLOTS), DOWN)
        line_ref[:, cols] = dot(mix_ref[1], get_rows(wide_ref, j, SLOTS, AREA), DOWN)

    loop(8, gather)
    inv, unit = unit_rows(far_x_ref[...])
    sums = line_ref[...]
    sent_ref[...] = through_norm(sums, gain_ref[...], inv, unit).astype(bf16)
    total = jnp.sum(sums * unit, axis=0, keepdims=True)
    _, unit = unit_rows(near_x_ref[...])
    total = total + jnp.sum(sums_ref[...] * unit, axis=0, keepdims=True)
    note_ref[pl.ds(EXPERTS, 8), :] = jnp.zeros((8, 256), f32)
    mine_ref[...] = jnp.zeros((8, 256), f32)
    for x in range(4):
        first, second = total[:, x * 512 : x * 512 + 256], total[:, x * 512 + 256 : x * 512 + 512]
        mine_ref[pl.ds(x, 1), :] = jnp.where(zh == 0, first, second)
        note_ref[pl.ds(EXPERTS + x, 1), :] = jnp.where(zh == 0, second, first)


def run_behind_sums(*args):
    return call(
        behind_sums,
        (shape((TOK, D), f32), shape((TOK, D)), shape((EXPERTS + 8, 256), f32), shape((8, 256), f32)),
        [SMEM] + [VMEM] * 8,
        [pltpu.VMEM((2, 2 * AREA + PEERS * 8, 128), f32), pltpu.VMEM((TOK, D), f32), pltpu.VMEM((2, SLOTS, TOK), bf16)],
        args,
        10**9,
        6,
    )


def behind_end(
    zh_ref, near_note_ref, far_note_ref, mine_ref, sums_ref, near_probs_ref, far_probs_ref, near_normed_ref,
    far_normed_ref, near_x_ref, far_x_ref, g_ref, gain_ref, table_ref, sent_ref, shares_ref
):
    zh = zh_ref[0]
    near_tok, far_tok = pl.ds(0, TOK), pl.ds(TOK, TOK)
    rows = pl.ds(0, EXPERTS)

    def logit_grads(probs, grads):
        return (probs * (grads - jnp.sum(probs * grads, axis=0, keepdims=True))).astype(bf16)

    near_logit = logit_grads(near_probs_ref[...], near_note_ref[rows, near_tok] + far_note_ref[rows, far_tok])
    far_logit = logit_grads(far_probs_ref[...], near_note_ref[rows, far_tok] + far_note_ref[rows, near_tok])
    inv, near_unit = unit_rows(near_x_ref[...])
    _, far_unit = unit_rows(far_x_ref[...])
    near_term = dot(near_logit, table_ref[...], DOWN)
    sums = sums_ref[...] + near_term
    sent_ref[...] = (g_ref[...].astype(f32) + through_norm(sums, gain_ref[...], inv, near_unit)).astype(bf16)
    far_term = dot(far_logit, table_ref[...], DOWN)
    total = jnp.sum(near_term * near_unit + far_term * far_unit, axis=0, keepdims=True)
    row = iota((128 - EXPERTS, 256), 0)
    for x in range(4):
        first, second = total[:, x * 512 : x * 512 + 256], total[:, x * 512 + 256 : x * 512 + 512]
        gains = (
            jnp.where(zh == 0, first, second)
            + mine_ref[pl.ds(x, 1), :]
            + far_note_ref[pl.ds(EXPERTS + x, 1), :]
        )
        cols = pl.ds(pl.multiple_of(x * 512 + zh * 256, 256), 256)
        part = dot(near_logit, near_normed_ref[:, cols]) + dot(far_logit, far_normed_ref[:, cols])
        both = jnp.concatenate([part, jnp.where(row == 0, gains, 0.0)], axis=0)
        shares_ref[pl.ds(x * 256, 256), :] = both.T


def run_behind_end(*args):
    return call(
        behind_end,
        (shape((TOK, D)), shape((D // 2, 128), f32)),
        [SMEM] + [VMEM] * 13,
        [],
        args,
        10**9,
        6,
    )


def ahead_end(home_ref, near_mix_ref, far_mix_ref, resid_ref, near_ref, far_ref, wide_ref):
    def take(d, rows):
        for half in range(2):
            wide_ref[0, area_rows(d, half), :] = home_ref[d, pl.ds(half * ROWS, ROWS), :].astype(f32)

    each_peer(take)
    for c in range(4):
        cols = pl.ds(c * 256, 256)
        for half, (mix_ref, out_ref) in enumerate(((near_mix_ref, near_ref), (far_mix_ref, far_ref))):
            rows = jnp.concatenate([get_rows(wide_ref, 2 * c + i, SLOTS, half * AREA) for i in range(2)], axis=1)
            sums = dot(mix_ref[...], rows, DOWN)
            if half == 0:
                sums = sums + resid_ref[:, cols].astype(f32)
            out_ref[:, cols] = sums.astype(bf16)


def run_ahead_end(home, near_mix, far_mix, resid, part):
    columns = pl.BlockSpec((TOK, D // 2), lambda i: (0, part))
    whole = [pl.BlockSpec(a.shape, lambda i, n=a.ndim: (0,) * n) for a in (home, near_mix, far_mix)]
    half = pl.BlockSpec((TOK, D // 2), lambda i: (0, 0))
    return pl.pallas_call(
        ahead_end,
        grid=(1,),
        out_shape=(shape((TOK, D // 2)), shape((TOK, D // 2))),
        in_specs=whole + [columns],
        out_specs=(half, half),
        scratch_shapes=[pltpu.VMEM((1, 2 * AREA, 128), f32)],
        compiler_params=pltpu.CompilerParams(vmem_limit_bytes=63 * 2**20),
        cost_estimate=pl.CostEstimate(flops=10**9, transcendentals=0, bytes_accessed=3 * 2**20),
    )(home, near_mix, far_mix, resid)


def final_add(a_ref, b_ref, c_ref, d_ref, out_ref):
    half = D // 2
    out_ref[:, pl.ds(0, half)] = (a_ref[...].astype(f32) + b_ref[...].astype(f32)).astype(bf16)
    out_ref[:, pl.ds(half, half)] = (c_ref[...].astype(f32) + d_ref[...].astype(f32)).astype(bf16)


def run_final_add(*args):
    return call(final_add, (shape((TOK, D)),), [VMEM] * 4, [], args, 10**6, 2)[0]


def body(
    forward_input,
    queries,
    new_keys,
    new_values,
    cache_keys,
    cache_values,
    context_lengths,
    norm_gain,
    router,
    gate_weight,
    up_weight,
    down_weight,
    forward_ids,
    backward_input,
    backward_ids,
    output_grad,
):
    zh = lax.axis_index("zh").astype(jnp.int32).reshape(1)
    gain = norm_gain
    table = router[0].T
    weights = (gate_weight[0, 0], up_weight[0, 0], down_weight[0, 0])
    back_x, back_g = backward_input[0], output_grad[0]
    ids_b, ids_f = backward_ids[0].T, forward_ids[0].T
    ids_far = swapped(jnp.concatenate([ids_b, ids_f], axis=0))
    x_far = swapped(back_x)
    g_far = swapped(back_g)
    resid = run_attend(
        context_lengths,
        forward_input[0],
        queries[0],
        cache_keys[0],
        new_keys[0],
        cache_values[0],
        new_values[0],
    )
    resid_far = swapped(resid)
    sent_1, normed_b, hot_b, probs_b, mix_f = run_near_pack(
        zh, ids_b, ids_f, back_x, back_g, resid, gain, table
    )
    got_1 = spread_out(sent_1)
    sent_2, normed_c, hot_c, probs_c = run_far_pack(zh, ids_far[:4], x_far, g_far, gain, table)
    sent_2, _ = lax.optimization_barrier((sent_2, got_1))
    got_2 = spread_out(sent_2)
    sent_3, mix_h = run_ahead_pack(zh, ids_far[4:], resid_far, gain, table)
    sent_3, got_2 = lax.optimization_barrier((sent_3, got_2))
    got_3 = spread_out(sent_3)
    back_b, small_b = run_near_experts(got_1, *weights)
    back = run_far_experts(got_2, back_b, small_b, *weights)
    back, got_3 = lax.optimization_barrier((back, got_3))
    home_b = spread_out(back)
    made_1, made_2 = run_ahead_experts(got_1, got_3, *weights)
    made_1, home_b = lax.optimization_barrier((made_1, home_b))
    home_1 = spread_out(made_1)
    sums_b, own_c, note, mine = run_behind_sums(
        zh, home_b, hot_b, hot_c, probs_b, probs_c, back_x, x_far, gain
    )
    far_note = swapped(note)
    moved_c = moved(own_c, False, -1)
    own_b, shares = run_behind_end(
        zh, note, far_note, mine, sums_b, probs_b, probs_c, normed_b, normed_c, back_x, x_far, back_g, gain, table
    )
    moved_b = moved(own_b, True, -1)
    made_2, home_1 = lax.optimization_barrier((made_2, home_1))
    home_2 = spread_out(made_2)
    own_f1, own_h1 = run_ahead_end(home_1, mix_f, mix_h, resid, 0)
    moved_h1 = moved(own_h1, False, 1)
    moved_f1 = moved(own_f1, True, 1)
    own_f2, own_h2 = run_ahead_end(home_2, mix_f, mix_h, resid, 1)
    moved_h2 = moved(own_h2, False, 1)
    moved_f2 = moved(own_f2, True, 1)
    shares, own_f2 = lax.optimization_barrier((shares, own_f2))
    total = jnp.sum(spread_out(shares.reshape(PEERS, PEERS, 128)), axis=0) * factor
    input_grad = (moved_b.astype(f32) + moved_c.astype(f32)).astype(bf16)
    forward_output = run_final_add(moved_f1, moved_h1, moved_f2, moved_h2)
    return (
        forward_output[None],
        input_grad[None],
        total[None, :, :EXPERTS],
        total[:, EXPERTS][None],
    )


def solution(mesh):
    grid = Mesh(mesh.devices.reshape(4, 4, 2, 4, 2), ("pipe", "x", "zh", "y", "core"))
    rows = P("pipe", ALL, None)
    placed = (
        rows,
        rows,
        rows,
        rows,
        rows,
        rows,
        P("pipe", ALL),
        P("pipe", None),
        P("pipe", None, None),
        P("pipe", ALL, None, None),
        P("pipe", ALL, None, None),
        P("pipe", ALL, None, None),
        rows,
        rows,
        rows,
        rows,
    )
    return jax.shard_map(
        body,
        mesh=grid,
        in_specs=placed,
        out_specs=(rows, rows, rows, P("pipe", ALL)),
        check_vma=False,
    )
```

```python
import jax
import jax.numpy as jnp
from jax import lax
from jax.experimental import pallas as pl
from jax.experimental.pallas import tpu as pltpu
from jax.sharding import Mesh, PartitionSpec as P


HEADS = 16
KV_HEADS = 2
HEAD_DIM = 128
D = 2048
FF = 768
EXPERTS = 64
MOST = 9
TOK = 128
PEERS = 32
SLOTS = PEERS * MOST
ROWS = MOST * 8
AREA = SLOTS * 8
XY = ("x", "y", "core")
ALL = ("x", "zh", "y", "core")

epsilon = 1e-06
far_below = -1e30
factor = 8192 ** (-0.5)
bf16 = jnp.bfloat16
f32 = jnp.float32
ACROSS = (((1,), (1,)), ((), ()))
DOWN = (((0,), (0,)), ((), ()))
VMEM = pl.BlockSpec(memory_space=pltpu.VMEM)
SMEM = pl.BlockSpec(memory_space=pltpu.SMEM)
HBM = pl.BlockSpec(memory_space=pltpu.HBM)


def spread_out(x):
    return lax.all_to_all(x, XY, 0, 0, tiled=True)


def swapped(x):
    return lax.ppermute(x, "zh", [(0, 1), (1, 0)])


def moved(x, same, step):
    pairs = []
    for pipe in range(4):
        for zh in range(2):
            to = ((pipe + step) % 4) * 2 + (zh if same else 1 - zh)
            pairs.append((pipe * 2 + zh, to))
    return lax.ppermute(x, ("pipe", "zh"), pairs)


def shape(dims, dtype=bf16):
    return jax.ShapeDtypeStruct(dims, dtype)


def call(kernel, outs, ins, scratch, args, flops, mib):
    return pl.pallas_call(
        kernel,
        out_shape=outs,
        in_specs=ins,
        out_specs=tuple(VMEM for _ in outs),
        scratch_shapes=scratch,
        compiler_params=pltpu.CompilerParams(vmem_limit_bytes=63 * 2**20),
        cost_estimate=pl.CostEstimate(
            flops=flops, transcendentals=0, bytes_accessed=mib * 2**20
        ),
    )(*args)


def dot(a, b, dims=None):
    if dims is None:
        return jnp.dot(a, b, preferred_element_type=f32)
    return lax.dot_general(a, b, dims, preferred_element_type=f32)


def iota(dims, dim):
    return lax.broadcasted_iota(jnp.int32, dims, dim)


def marks(cond):
    return cond.astype(f32).astype(bf16)


def unit_rows(x):
    wide = x.astype(f32)
    inv_rms = lax.rsqrt(jnp.mean(wide * wide, axis=-1, keepdims=True) + epsilon)
    return inv_rms, wide * inv_rms


def hits(ids):
    expert = iota((EXPERTS, ids.shape[1]), 0)
    hit = ids[0:1, :] == expert
    for k in range(1, 4):
        hit = hit | (ids[k : k + 1, :] == expert)
    return hit


def choice(normed, table, hit):
    logits = jnp.where(hit, dot(table, normed, ACROSS), far_below)
    lifted = jnp.where(hit, jnp.exp(logits - jnp.max(logits, axis=0, keepdims=True)), 0.0)
    return lifted / jnp.sum(lifted, axis=0, keepdims=True)


def ranked(hit):
    tokens = hit.shape[1]
    earlier, later = iota((tokens, tokens), 0), iota((tokens, tokens), 1)
    before = marks((earlier < later) & (earlier // TOK == later // TOK))
    hit = hit.astype(f32)
    return (hit * (dot(hit.astype(bf16), before) + 1.0)).astype(bf16)


def picks(peer, zh):
    owner = (peer // 8) * 16 + zh * 8 + peer % 8
    return marks(owner == iota(peer.shape, 1))


def each_peer(step):
    def turn(d, carry):
        step(d, pl.ds(pl.multiple_of(d * ROWS, 8), ROWS))
        return carry

    lax.fori_loop(0, PEERS, turn, 0)


def area_rows(d, area):
    return pl.ds(pl.multiple_of(d * ROWS + area * AREA, 8), ROWS)


LANES = (pl.ds(0, 128), pl.ds(128, 128))


def put_rows(wide_ref, j, rows, start=0):
    for lane in range(rows.shape[1] // 128):
        wide_ref[lane, pl.ds(start + j, rows.shape[0], stride=8), :] = rows[
            :, lane * 128 : lane * 128 + 128
        ]


def get_rows(wide_ref, j, count, start=0):
    return jnp.concatenate(
        [
            wide_ref[lane, pl.ds(start + j, count, stride=8), :].astype(bf16)
            for lane in range(wide_ref.shape[0])
        ],
        axis=1,
    )


def routed(ids, x, zh, gain, table):
    hit = hits(ids)
    _, unit = unit_rows(x)
    normed = (unit * gain).astype(bf16)
    probs = choice(normed, table, hit)
    pick = picks(iota((SLOTS, EXPERTS), 0) // MOST, zh)
    slot = (iota((SLOTS, TOK), 0) % MOST + 1).astype(f32)
    return normed, probs, pick, marks(dot(pick, ranked(hit)) == slot)


def mixed_by(onehot, pick, probs):
    return onehot * dot(pick, probs.astype(bf16)).astype(bf16)


def loop(count, step):
    def turn(i, carry):
        step(i)
        return carry

    lax.fori_loop(0, count, turn, 0)


def columns(j, width):
    return pl.ds(pl.multiple_of(j * width, width), width)


def fill_looped(wide_ref, area, onehot_ref, rows_ref):
    def step(j):
        put_rows(wide_ref, j, dot(onehot_ref[...], rows_ref[:, columns(j, 256)]), area * AREA)

    loop(8, step)


def fill(wide_ref, area, onehot, rows_ref):
    for j in range(8):
        put_rows(wide_ref, j, dot(onehot, rows_ref[:, pl.ds(j * 256, 256)]), area * AREA)


def give(wide_ref, sent_ref, areas):
    def step(d, rows):
        for area in range(areas):
            for lane in range(2):
                sent_ref[d, pl.ds(area * ROWS, ROWS), LANES[lane]] = wide_ref[lane, area_rows(d, area), :].astype(bf16)

    each_peer(step)


def near_pack(
    zh_ref, ids_ref, ahead_ids_ref, x_ref, g_ref, resid_ref, gain_ref, table_ref,
    sent_ref, normed_ref, onehot_ref, probs_ref, mix_ref, wide_ref, rows_ref
):
    zh, gain, table = zh_ref[0], gain_ref[...], table_ref[...]
    normed_ref[...], probs_ref[...], _, onehot_ref[...] = routed(ids_ref[...], x_ref[...], zh, gain, table)
    fill(wide_ref, 0, onehot_ref[...], normed_ref)
    fill(wide_ref, 1, onehot_ref[...], g_ref)
    rows_ref[...], probs, pick, onehot = routed(ahead_ids_ref[...], resid_ref[...], zh, gain, table)
    mix_ref[...] = mixed_by(onehot, pick, probs)
    fill(wide_ref, 2, onehot, rows_ref)
    give(wide_ref, sent_ref, 3)


def run_near_pack(*args):
    return call(
        near_pack,
        (
            shape((PEERS, 3 * ROWS, 256)),
            shape((TOK, D)),
            shape((SLOTS, TOK)),
            shape((EXPERTS, TOK), f32),
            shape((SLOTS, TOK)),
        ),
        [SMEM] + [VMEM] * 7,
        [pltpu.VMEM((2, 3 * AREA, 128), f32), pltpu.VMEM((TOK, D), bf16)],
        args,
        2 * 10**9,
        8,
    )


def far_pack(
    zh_ref, ids_ref, x_ref, g_ref, gain_ref, table_ref, sent_ref, normed_ref, onehot_ref, probs_ref, wide_ref
):
    normed_ref[...], probs_ref[...], _, onehot_ref[...] = routed(
        ids_ref[...], x_ref[...], zh_ref[0], gain_ref[...], table_ref[...]
    )
    fill(wide_ref, 0, onehot_ref[...], normed_ref)
    fill(wide_ref, 1, onehot_ref[...], g_ref)
    give(wide_ref, sent_ref, 2)


def run_far_pack(*args):
    return call(
        far_pack,
        (shape((PEERS, 2 * ROWS, 256)), shape((TOK, D)), shape((SLOTS, TOK)), shape((EXPERTS, TOK), f32)),
        [SMEM] + [VMEM] * 5,
        [pltpu.VMEM((2, 2 * AREA, 128), f32)],
        args,
        10**9,
        6,
    )


def ahead_pack(zh_ref, ids_ref, x_ref, gain_ref, table_ref, sent_ref, mix_ref, wide_ref, rows_ref, onehot_ref):
    rows_ref[...], probs, pick, onehot = routed(ids_ref[...], x_ref[...], zh_ref[0], gain_ref[...], table_ref[...])
    mix_ref[...] = mixed_by(onehot, pick, probs)
    onehot_ref[...] = onehot
    fill_looped(wide_ref, 0, onehot_ref, rows_ref)
    give(wide_ref, sent_ref, 1)


def run_ahead_pack(*args):
    return call(
        ahead_pack,
        (shape((PEERS, ROWS, 256)), shape((SLOTS, TOK))),
        [SMEM] + [VMEM] * 4,
        [pltpu.VMEM((2, AREA, 128), f32), pltpu.VMEM((TOK, D), bf16), pltpu.VMEM((SLOTS, TOK), bf16)],
        args,
        10**9,
        4,
    )


def fetched(pairs, sems):
    copies = [pltpu.make_async_copy(a, b, sems.at[i]) for i, (a, b) in enumerate(pairs)]
    for copy in copies:
        copy.start()
    return copies


def expert_slopes(gate_pre, up_pre, down_grad, gate_grad, up_grad):
    sig = 1.0 / (1.0 + jnp.exp(-gate_pre))
    act = gate_pre * sig
    hidden = (act * up_pre).astype(bf16).astype(f32)
    gate_grad[...] = (down_grad * up_pre * sig * (1.0 + gate_pre * (1.0 - sig))).astype(bf16)
    up_grad[...] = (down_grad * act).astype(bf16)
    return jnp.sum(hidden * down_grad, axis=-1, keepdims=True).astype(bf16).astype(f32)


def small_grads(grads, place):
    p, lane = iota((SLOTS, 128), 0), iota((SLOTS, 128), 1)
    gather = marks(iota((PEERS * 8, SLOTS), 1) // MOST == iota((PEERS * 8, SLOTS), 0) // 8)
    spread = jnp.where(lane == p % MOST + place * MOST, grads, 0.0)
    return dot(gather, spread.astype(bf16))


def behind_half(got_ref, weights, place, wide_ref, sems, gate_grad, up_grad):
    (gate_hbm, gate_ref), (up_hbm, up_ref), (down_hbm, down_ref) = weights
    copies = fetched(weights, sems)

    def take(d, rows):
        for lane in range(2):
            for kind in range(2):
                wide_ref[lane, area_rows(d, kind), :] = got_ref[d, pl.ds(kind * ROWS, ROWS), LANES[lane]].astype(f32)

    each_peer(take)
    copies[0].wait()
    copies[1].wait()
    gate_pre, up_pre = jnp.zeros((SLOTS, FF), f32), jnp.zeros((SLOTS, FF), f32)
    for j in range(4):
        rows = jnp.concatenate([get_rows(wide_ref, 2 * j + i, SLOTS) for i in range(2)], axis=1)
        gate_pre = gate_pre + dot(rows, gate_ref[pl.ds(j * 512, 512), :])
        up_pre = up_pre + dot(rows, up_ref[pl.ds(j * 512, 512), :])
    copies[2].wait()
    down_grad = jnp.zeros((SLOTS, FF), f32)
    for j in range(4):
        rows = jnp.concatenate([get_rows(wide_ref, 2 * j + i, SLOTS, AREA) for i in range(2)], axis=1)
        down_grad = down_grad + dot(rows, down_ref[:, pl.ds(j * 512, 512)], ACROSS)
    grads = expert_slopes(gate_pre, up_pre, down_grad, gate_grad, up_grad)
    for j in range(8):
        part = pl.ds(j * 256, 256)
        rows = dot(gate_grad[...], gate_ref[part, :], ACROSS) + dot(up_grad[...], up_ref[part, :], ACROSS)
        put_rows(wide_ref, j, rows)
    return small_grads(grads, place)


def near_experts(
    got_ref, gate_hbm, up_hbm, down_hbm, back_ref, small_ref, wide_ref, gate_ref, up_ref, down_ref, sems,
    gate_sum, up_sum, down_sum, gate_grad, up_grad
):
    copies = fetched(((gate_hbm, gate_ref), (up_hbm, up_ref), (down_hbm, down_ref)), sems)

    def take(d, rows):
        for lane in range(2):
            for kind in range(2):
                wide_ref[lane, area_rows(d, kind), :] = got_ref[d, pl.ds(kind * ROWS, ROWS), LANES[lane]].astype(f32)

    each_peer(take)
    for ref in (gate_sum, up_sum, down_sum):
        ref[...] = jnp.zeros((SLOTS, FF), f32)
    for copy in copies:
        copy.wait()

    def inward(j):
        rows = jnp.concatenate([get_rows(wide_ref, 2 * j + i, SLOTS) for i in range(2)], axis=1)
        gate_sum[...] += dot(rows, gate_ref[columns(j, 512), :])
        up_sum[...] += dot(rows, up_ref[columns(j, 512), :])
        rows = jnp.concatenate([get_rows(wide_ref, 2 * j + i, SLOTS, AREA) for i in range(2)], axis=1)
        down_sum[...] += dot(rows, down_ref[:, columns(j, 512)], ACROSS)

    loop(4, inward)
    grads = expert_slopes(gate_sum[...], up_sum[...], down_sum[...], gate_grad, up_grad)

    def outward(j):
        part = columns(j, 256)
        rows = dot(gate_grad[...], gate_ref[part, :], ACROSS) + dot(up_grad[...], up_ref[part, :], ACROSS)
        put_rows(wide_ref, j, rows)

    loop(8, outward)
    small_ref[...] = small_grads(grads, 0)

    def put(d, rows):
        for lane in range(2):
            back_ref[d, :, LANES[lane]] = wide_ref[lane, rows, :].astype(bf16)

    each_peer(put)


def far_experts(
    got_ref, near_ref, near_small_ref, gate_hbm, up_hbm, down_hbm, back_ref, wide_ref, gate_ref, up_ref, down_ref, sems,
    gate_grad, up_grad
):
    weights = ((gate_hbm, gate_ref), (up_hbm, up_ref), (down_hbm, down_ref))
    small = behind_half(got_ref, weights, 1, wide_ref, sems, gate_grad, up_grad) + near_small_ref[...]
    wide_ref[0, pl.ds(AREA, PEERS * 8), :] = small

    def put(d, rows):
        for lane in range(2):
            back_ref[d, pl.ds(0, ROWS), LANES[lane]] = near_ref[d, :, LANES[lane]]
            back_ref[d, pl.ds(ROWS, ROWS), LANES[lane]] = wide_ref[lane, rows, :].astype(bf16)
        extra = wide_ref[0, pl.ds(pl.multiple_of(AREA + d * 8, 8), 8), :].astype(bf16)
        back_ref[d, pl.ds(2 * ROWS, 8), LANES[0]] = extra
        back_ref[d, pl.ds(2 * ROWS, 8), LANES[1]] = extra

    each_peer(put)


GRADS = [pltpu.VMEM((SLOTS, FF), bf16)] * 2
WEIGHTS = [
    pltpu.VMEM((D, FF), bf16),
    pltpu.VMEM((D, FF), bf16),
    pltpu.VMEM((FF, D), bf16),
    pltpu.SemaphoreType.DMA((3,)),
]


def run_near_experts(*args):
    return call(
        near_experts,
        (shape((PEERS, ROWS, 256)), shape((PEERS * 8, 128), f32)),
        [VMEM] + [HBM] * 3,
        [pltpu.VMEM((2, 2 * AREA, 128), f32)] + WEIGHTS + [pltpu.VMEM((SLOTS, FF), f32)] * 3 + GRADS,
        args,
        5 * 10**9,
        13,
    )


def run_far_experts(*args):
    return call(
        far_experts,
        (shape((PEERS, 2 * ROWS + 8, 256)),),
        [VMEM] * 3 + [HBM] * 3,
        [pltpu.VMEM((2, 2 * AREA, 128), f32)] + WEIGHTS + GRADS,
        args,
        5 * 10**9,
        15,
    )[0]


def ahead_experts(
    near_ref, far_ref, gate_hbm, up_hbm, down_hbm, first_ref, second_ref, wide_ref, gate_ref, up_ref, down_ref, sems,
    gate_sum, up_sum, hidden_ref
):
    copies = fetched(((gate_hbm, gate_ref), (up_hbm, up_ref), (down_hbm, down_ref)), sems)
    count = 2 * SLOTS

    def take(d, rows):
        for lane in range(2):
            wide_ref[lane, area_rows(d, 0), :] = near_ref[d, pl.ds(2 * ROWS, ROWS), LANES[lane]].astype(f32)
            wide_ref[lane, area_rows(d, 1), :] = far_ref[d, :, LANES[lane]].astype(f32)

    each_peer(take)
    copies[0].wait()
    copies[1].wait()
    gate_sum[...] = jnp.zeros((count, FF), f32)
    up_sum[...] = jnp.zeros((count, FF), f32)

    def inward(j):
        rows = jnp.concatenate([get_rows(wide_ref, 2 * j, count), get_rows(wide_ref, 2 * j + 1, count)], axis=1)
        gate_sum[...] += dot(rows, gate_ref[columns(j, 512), :])
        up_sum[...] += dot(rows, up_ref[columns(j, 512), :])

    loop(4, inward)
    gate_pre = gate_sum[...]
    hidden_ref[...] = (gate_pre / (1.0 + jnp.exp(-gate_pre)) * up_sum[...]).astype(bf16)
    copies[2].wait()

    def outward(j):
        put_rows(wide_ref, j, dot(hidden_ref[...], down_ref[:, columns(j, 256)]))

    loop(8, outward)

    def put(d, rows):
        for lane in range(2):
            first_ref[d, :, LANES[lane]] = wide_ref[lane, area_rows(d, 1), :].astype(bf16)
            second_ref[d, :, LANES[lane]] = wide_ref[lane, area_rows(d, 0), :].astype(bf16)

    each_peer(put)


def run_ahead_experts(*args):
    return call(
        ahead_experts,
        (shape((PEERS, ROWS, 256)), shape((PEERS, ROWS, 256))),
        [VMEM] * 2 + [HBM] * 3,
        [pltpu.VMEM((2, 2 * AREA, 128), f32)]
        + WEIGHTS
        + [pltpu.VMEM((2 * SLOTS, FF), f32), pltpu.VMEM((2 * SLOTS, FF), f32), pltpu.VMEM((2 * SLOTS, FF), bf16)],
        args,
        6 * 10**9,
        14,
    )


def attend(length_ref, x_ref, q_ref, kc_ref, kn_ref, vc_ref, vn_ref, resid_ref):
    length = length_ref[0, 0]
    row, col = iota((TOK, 2 * TOK), 0), iota((TOK, 2 * TOK), 1)
    visible = ((col < TOK) & (col < length)) | ((col >= TOK) & (col - TOK <= row))
    for kv in range(KV_HEADS):
        part = pl.ds(kv * HEAD_DIM, HEAD_DIM)
        keys = jnp.concatenate([kc_ref[:, part], kn_ref[:, part]], axis=0)
        values = jnp.concatenate([vc_ref[:, part], vn_ref[:, part]], axis=0)
        for h in range(HEADS // KV_HEADS):
            cols = pl.ds((kv * (HEADS // KV_HEADS) + h) * HEAD_DIM, HEAD_DIM)
            scores = dot(q_ref[:, cols], keys, ACROSS) * HEAD_DIM ** (-0.5)
            scores = jnp.where(visible, scores, far_below)
            lifted = jnp.exp(scores - jnp.max(scores, axis=-1, keepdims=True))
            weights = (lifted * (1.0 / jnp.sum(lifted, axis=-1, keepdims=True))).astype(bf16)
            mixed = dot(weights, values).astype(bf16)
            resid_ref[:, cols] = (x_ref[:, cols].astype(f32) + mixed.astype(f32)).astype(bf16)


def run_attend(length, x, q, kc, kn, vc, vn):
    return call(
        attend,
        (shape((TOK, D)),),
        [SMEM] + [VMEM] * 6,
        [],
        (length, x, q, kc, kn, vc, vn),
        3 * 10**9,
        8,
    )[0]


def through_norm(sums, gain, inv, unit):
    scaled = sums * gain
    return inv * (scaled - unit * jnp.mean(scaled * unit, axis=-1, keepdims=True))


def behind_note(zh_ref, home_ref, near_hot_ref, far_hot_ref, note_ref):
    pick = picks(iota((SLOTS, EXPERTS), 0) // MOST, zh_ref[0]).astype(f32)
    small = jnp.concatenate([home_ref[d].astype(f32) for d in range(PEERS)], axis=0)[:, :128].astype(bf16)
    share = marks(iota((SLOTS, PEERS * 8), 0) // MOST * 8 == iota((SLOTS, PEERS * 8), 1))
    small = dot(share, small)
    p, lane = iota((SLOTS, 128), 0) % MOST, iota((SLOTS, 128), 1)
    for half, hot in enumerate((near_hot_ref, far_hot_ref)):
        grads = jnp.sum(jnp.where(lane == p + half * MOST, small, 0.0), axis=-1, keepdims=True)
        note_ref[:, pl.ds(half * TOK, TOK)] = dot((pick * grads).astype(bf16), hot[...], DOWN)


def whole(a):
    return pl.BlockSpec(a.shape, lambda i, n=a.ndim: (0,) * n)


def run_behind_note(zh, home, near_hot, far_hot):
    tail = pl.BlockSpec((PEERS, 8, 256), lambda i: (0, 2 * ROWS // 8, 0))
    return pl.pallas_call(
        behind_note,
        grid=(1,),
        out_shape=shape((EXPERTS, 2 * TOK), f32),
        in_specs=[SMEM, tail, whole(near_hot), whole(far_hot)],
        out_specs=pl.BlockSpec((EXPERTS, 2 * TOK), lambda i: (0, 0)),
        compiler_params=pltpu.CompilerParams(vmem_limit_bytes=63 * 2**20),
        cost_estimate=pl.CostEstimate(flops=10**7, transcendentals=0, bytes_accessed=2**18),
    )(zh, home, near_hot, far_hot)


def behind_sums(
    zh_ref, home_ref, near_hot_ref, far_hot_ref, near_probs_ref, far_probs_ref, near_x_ref, far_x_ref, gain_ref,
    sums_ref, sent_ref, theirs_ref, mine_ref, wide_ref, line_ref, mix_ref
):
    zh = zh_ref[0]

    def take(d, rows):
        for half in range(2):
            for lane in range(2):
                wide_ref[lane, area_rows(d, half), :] = home_ref[d, pl.ds(half * ROWS, ROWS), LANES[lane]].astype(f32)

    each_peer(take)
    pick = picks(iota((SLOTS, EXPERTS), 0) // MOST, zh)
    mix_ref[0] = mixed_by(near_hot_ref[...], pick, near_probs_ref[...])
    mix_ref[1] = mixed_by(far_hot_ref[...], pick, far_probs_ref[...])

    for j in range(8):
        cols = pl.ds(j * 256, 256)
        sums_ref[:, cols] = dot(mix_ref[0], get_rows(wide_ref, j, SLOTS), DOWN)
        line_ref[:, cols] = dot(mix_ref[1], get_rows(wide_ref, j, SLOTS, AREA), DOWN)
    inv, unit = unit_rows(far_x_ref[...])
    sums = line_ref[...]
    sent_ref[...] = through_norm(sums, gain_ref[...], inv, unit).astype(bf16)
    total = jnp.sum(sums * unit, axis=0, keepdims=True)
    _, unit = unit_rows(near_x_ref[...])
    total = total + jnp.sum(sums_ref[...] * unit, axis=0, keepdims=True)
    theirs_ref[...] = jnp.zeros((8, 256), f32)
    mine_ref[...] = jnp.zeros((8, 256), f32)
    for x in range(4):
        first, second = total[:, x * 512 : x * 512 + 256], total[:, x * 512 + 256 : x * 512 + 512]
        mine_ref[pl.ds(x, 1), :] = jnp.where(zh == 0, first, second)
        theirs_ref[pl.ds(x, 1), :] = jnp.where(zh == 0, second, first)


def run_behind_sums(*args):
    return call(
        behind_sums,
        (shape((TOK, D), f32), shape((TOK, D)), shape((8, 256), f32), shape((8, 256), f32)),
        [SMEM] + [VMEM] * 8,
        [
            pltpu.VMEM((2, 2 * AREA, 128), f32),
            pltpu.VMEM((TOK, D), f32),
            pltpu.VMEM((2, SLOTS, TOK), bf16),
        ],
        args,
        10**9,
        6,
    )


def behind_end(
    near_note_ref, far_note_ref, sums_ref, near_probs_ref, far_probs_ref, x_ref, g_ref, gain_ref, table_ref,
    sent_ref, near_logit_ref, far_logit_ref
):
    near_tok, far_tok = pl.ds(0, TOK), pl.ds(TOK, TOK)

    def logit_grads(probs, grads):
        return (probs * (grads - jnp.sum(probs * grads, axis=0, keepdims=True))).astype(bf16)

    near_logit_ref[...] = logit_grads(near_probs_ref[...], near_note_ref[:, near_tok] + far_note_ref[:, far_tok])
    far_logit_ref[...] = logit_grads(far_probs_ref[...], near_note_ref[:, far_tok] + far_note_ref[:, near_tok])
    inv, unit = unit_rows(x_ref[...])
    sums = sums_ref[...] + dot(near_logit_ref[...], table_ref[...], DOWN)
    sent_ref[...] = (g_ref[...].astype(f32) + through_norm(sums, gain_ref[...], inv, unit)).astype(bf16)


def run_behind_end(*args):
    return call(
        behind_end,
        (shape((TOK, D)), shape((EXPERTS, TOK)), shape((EXPERTS, TOK))),
        [VMEM] * 9,
        [],
        args,
        10**9,
        4,
    )


def share_parts(
    zh_ref, near_logit_ref, far_logit_ref, mine_ref, theirs_ref, near_normed_ref, far_normed_ref, near_x_ref,
    far_x_ref, table_ref, shares_ref
):
    zh = zh_ref[0]
    near_logit, far_logit = near_logit_ref[...], far_logit_ref[...]
    _, near_unit = unit_rows(near_x_ref[...])
    _, far_unit = unit_rows(far_x_ref[...])
    near_term, far_term = dot(near_logit, table_ref[...], DOWN), dot(far_logit, table_ref[...], DOWN)
    total = jnp.sum(near_term * near_unit + far_term * far_unit, axis=0, keepdims=True)
    row = iota((128 - EXPERTS, 256), 0)
    for x in range(4):
        first, second = total[:, x * 512 : x * 512 + 256], total[:, x * 512 + 256 : x * 512 + 512]
        gains = jnp.where(zh == 0, first, second) + mine_ref[pl.ds(x, 1), :] + theirs_ref[pl.ds(x, 1), :]
        cols = pl.ds(pl.multiple_of(x * 512 + zh * 256, 256), 256)
        part = dot(near_logit, near_normed_ref[:, cols]) + dot(far_logit, far_normed_ref[:, cols])
        both = jnp.concatenate([part, jnp.where(row == 0, gains, 0.0)], axis=0)
        shares_ref[pl.ds(x * 256, 256), :] = both.T


def run_share_parts(*args):
    return call(share_parts, (shape((D // 2, 128), f32),), [SMEM] + [VMEM] * 9, [], args, 10**9, 3)[0]


def ahead_sums(home_ref, mix_ref, wide_ref):
    def take(d, rows):
        for lane in range(2):
            wide_ref[lane, rows, :] = home_ref[d, :, LANES[lane]].astype(f32)

    each_peer(take)
    for j in range(8):
        yield pl.ds(j * 256, 256), dot(mix_ref[...], get_rows(wide_ref, j, SLOTS), DOWN)


def ahead_far(home_ref, mix_ref, out_ref, wide_ref):
    for cols, sums in ahead_sums(home_ref, mix_ref, wide_ref):
        out_ref[:, cols] = sums.astype(bf16)


def ahead_near(home_ref, mix_ref, resid_ref, out_ref, wide_ref):
    for cols, sums in ahead_sums(home_ref, mix_ref, wide_ref):
        out_ref[:, cols] = (resid_ref[:, cols].astype(f32) + sums).astype(bf16)


def run_ahead_end(kernel, *args):
    return call(
        kernel, (shape((TOK, D)),), [VMEM] * len(args), [pltpu.VMEM((2, AREA, 128), f32)], args, 10**9, 3
    )[0]


def share_sums(got_ref, router_ref, gain_ref):
    total = got_ref[0]
    for source in range(1, PEERS):
        total = total + got_ref[source]
    total = total * factor
    router_ref[...] = total[:, :EXPERTS]
    gain_ref[...] = total.T[EXPERTS : EXPERTS + 1, :]


def run_share_sums(got):
    return call(
        share_sums, (shape((PEERS, EXPERTS), f32), shape((1, PEERS), f32)), [VMEM], [], (got,), 10**6, 1
    )


def body(
    forward_input,
    queries,
    new_keys,
    new_values,
    cache_keys,
    cache_values,
    context_lengths,
    norm_gain,
    router,
    gate_weight,
    up_weight,
    down_weight,
    forward_ids,
    backward_input,
    backward_ids,
    output_grad,
):
    zh = lax.axis_index("zh").astype(jnp.int32).reshape(1)
    gain = norm_gain
    table = router[0].T
    weights = (gate_weight[0, 0], up_weight[0, 0], down_weight[0, 0])
    back_x, back_g = backward_input[0], output_grad[0]
    ids_b, ids_f = backward_ids[0].T, forward_ids[0].T
    ids_far = swapped(jnp.concatenate([ids_b, ids_f], axis=0))
    x_far = swapped(back_x)
    g_far = swapped(back_g)
    resid = run_attend(
        context_lengths,
        forward_input[0],
        queries[0],
        cache_keys[0],
        new_keys[0],
        cache_values[0],
        new_values[0],
    )
    resid_far = swapped(resid)
    sent_1, normed_b, hot_b, probs_b, mix_f = run_near_pack(
        zh, ids_b, ids_f, back_x, back_g, resid, gain, table
    )
    got_1 = spread_out(sent_1)
    sent_2, normed_c, hot_c, probs_c = run_far_pack(zh, ids_far[:4], x_far, g_far, gain, table)
    sent_2, _ = lax.optimization_barrier((sent_2, got_1))
    got_2 = spread_out(sent_2)
    sent_3, mix_h = run_ahead_pack(zh, ids_far[4:], resid_far, gain, table)
    sent_3, got_2 = lax.optimization_barrier((sent_3, got_2))
    got_3 = spread_out(sent_3)
    back_b, small_b = run_near_experts(got_1, *weights)
    back = run_far_experts(got_2, back_b, small_b, *weights)
    back, got_3 = lax.optimization_barrier((back, got_3))
    home_b = spread_out(back)
    made_1, made_2 = run_ahead_experts(got_1, got_3, *weights)
    made_1, home_b = lax.optimization_barrier((made_1, home_b))
    home_1 = spread_out(made_1)
    note = run_behind_note(zh, home_b, hot_b, hot_c)
    far_note = swapped(note)
    sums_b, own_c, theirs, mine = run_behind_sums(
        zh, home_b, hot_b, hot_c, probs_b, probs_c, back_x, x_far, gain
    )
    moved_c = moved(own_c, False, -1)
    own_b, logit_b, logit_c = run_behind_end(
        note, far_note, sums_b, probs_b, probs_c, back_x, back_g, gain, table
    )
    moved_b = moved(own_b, True, -1)
    made_2, home_1 = lax.optimization_barrier((made_2, home_1))
    home_2 = spread_out(made_2)
    own_h = run_ahead_end(ahead_far, home_1, mix_h)
    moved_h = moved(own_h, False, 1)
    theirs = swapped(theirs)
    shares = run_share_parts(
        zh, logit_b, logit_c, mine, theirs, normed_b, normed_c, back_x, x_far, table
    )
    own_f = run_ahead_end(ahead_near, home_2, mix_f, resid)
    moved_f = moved(own_f, True, 1)
    shares, own_f = lax.optimization_barrier((shares, own_f))
    got_s = spread_out(shares.reshape(PEERS, PEERS, 128))
    router_grad, gain_grad = run_share_sums(got_s)
    input_grad = (moved_b.astype(f32) + moved_c.astype(f32)).astype(bf16)
    forward_output = (moved_f.astype(f32) + moved_h.astype(f32)).astype(bf16)
    return forward_output[None], input_grad[None], router_grad[None], gain_grad


def solution(mesh):
    grid = Mesh(mesh.devices.reshape(4, 4, 2, 4, 2), ("pipe", "x", "zh", "y", "core"))
    rows = P("pipe", ALL, None)
    placed = (
        rows,
        rows,
        rows,
        rows,
        rows,
        rows,
        P("pipe", ALL),
        P("pipe", None),
        P("pipe", None, None),
        P("pipe", ALL, None, None),
        P("pipe", ALL, None, None),
        P("pipe", ALL, None, None),
        rows,
        rows,
        rows,
        rows,
    )
    return jax.shard_map(
        body,
        mesh=grid,
        in_specs=placed,
        out_specs=(rows, rows, rows, P("pipe", ALL)),
        check_vma=False,
    )
```

```python
import jax
import jax.numpy as jnp
from jax import lax
from jax.experimental import pallas as pl
from jax.experimental.pallas import tpu as pltpu
from jax.sharding import Mesh, PartitionSpec as P


HEADS = 16
KV_HEADS = 2
HEAD_DIM = 128
D = 2048
FF = 768
EXPERTS = 64
MOST = 9
TOK = 128
PEERS = 32
SLOTS = PEERS * MOST
ROWS = MOST * 8
AREA = SLOTS * 8
XY = ("x", "y", "core")
ALL = ("x", "zh", "y", "core")

epsilon = 1e-06
far_below = -1e30
factor = 8192 ** (-0.5)
bf16 = jnp.bfloat16
f32 = jnp.float32
ACROSS = (((1,), (1,)), ((), ()))
DOWN = (((0,), (0,)), ((), ()))
VMEM = pl.BlockSpec(memory_space=pltpu.VMEM)
SMEM = pl.BlockSpec(memory_space=pltpu.SMEM)
HBM = pl.BlockSpec(memory_space=pltpu.HBM)


def spread_out(x):
    return lax.all_to_all(x, XY, 0, 0, tiled=True)


def swapped(x):
    return lax.ppermute(x, "zh", [(0, 1), (1, 0)])


def moved(x, same, step):
    pairs = []
    for pipe in range(4):
        for zh in range(2):
            to = ((pipe + step) % 4) * 2 + (zh if same else 1 - zh)
            pairs.append((pipe * 2 + zh, to))
    return lax.ppermute(x, ("pipe", "zh"), pairs)


def shape(dims, dtype=bf16):
    return jax.ShapeDtypeStruct(dims, dtype)


def call(kernel, outs, ins, scratch, args, flops, mib):
    return pl.pallas_call(
        kernel,
        out_shape=outs,
        in_specs=ins,
        out_specs=tuple(VMEM for _ in outs),
        scratch_shapes=scratch,
        compiler_params=pltpu.CompilerParams(vmem_limit_bytes=63 * 2**20),
        cost_estimate=pl.CostEstimate(
            flops=flops, transcendentals=0, bytes_accessed=mib * 2**20
        ),
    )(*args)


def dot(a, b, dims=None):
    if dims is None:
        return jnp.dot(a, b, preferred_element_type=f32)
    return lax.dot_general(a, b, dims, preferred_element_type=f32)


def iota(dims, dim):
    return lax.broadcasted_iota(jnp.int32, dims, dim)


def marks(cond):
    return cond.astype(f32).astype(bf16)


def unit_rows(x):
    wide = x.astype(f32)
    inv_rms = lax.rsqrt(jnp.mean(wide * wide, axis=-1, keepdims=True) + epsilon)
    return inv_rms, wide * inv_rms


def hits(ids):
    expert = iota((EXPERTS, ids.shape[1]), 0)
    hit = ids[0:1, :] == expert
    for k in range(1, 4):
        hit = hit | (ids[k : k + 1, :] == expert)
    return hit


def choice(normed, table, hit):
    logits = jnp.where(hit, dot(table, normed, ACROSS), far_below)
    lifted = jnp.where(hit, jnp.exp(logits - jnp.max(logits, axis=0, keepdims=True)), 0.0)
    return lifted / jnp.sum(lifted, axis=0, keepdims=True)


def ranked(hit):
    tokens = hit.shape[1]
    earlier, later = iota((tokens, tokens), 0), iota((tokens, tokens), 1)
    before = marks((earlier < later) & (earlier // TOK == later // TOK))
    hit = hit.astype(f32)
    return (hit * (dot(hit.astype(bf16), before) + 1.0)).astype(bf16)


def picks(peer, zh):
    owner = (peer // 8) * 16 + zh * 8 + peer % 8
    return marks(owner == iota(peer.shape, 1))


def each_peer(step):
    def turn(d, carry):
        step(d, pl.ds(pl.multiple_of(d * ROWS, 8), ROWS))
        return carry

    lax.fori_loop(0, PEERS, turn, 0)


def area_rows(d, area):
    return pl.ds(pl.multiple_of(d * ROWS + area * AREA, 8), ROWS)


LANES = (pl.ds(0, 128), pl.ds(128, 128))


def put_rows(wide_ref, j, rows, start=0):
    for lane in range(rows.shape[1] // 128):
        wide_ref[lane, pl.ds(start + j, rows.shape[0], stride=8), :] = rows[
            :, lane * 128 : lane * 128 + 128
        ]


def get_rows(wide_ref, j, count, start=0):
    return jnp.concatenate(
        [
            wide_ref[lane, pl.ds(start + j, count, stride=8), :].astype(bf16)
            for lane in range(wide_ref.shape[0])
        ],
        axis=1,
    )


def routed(ids, x, zh, gain, table):
    hit = hits(ids)
    _, unit = unit_rows(x)
    normed = (unit * gain).astype(bf16)
    probs = choice(normed, table, hit)
    pick = picks(iota((SLOTS, EXPERTS), 0) // MOST, zh)
    slot = (iota((SLOTS, TOK), 0) % MOST + 1).astype(f32)
    return normed, probs, pick, marks(dot(pick, ranked(hit)) == slot)


def mixed_by(onehot, pick, probs):
    return onehot * dot(pick, probs.astype(bf16)).astype(bf16)


def loop(count, step):
    def turn(i, carry):
        step(i)
        return carry

    lax.fori_loop(0, count, turn, 0)


def columns(j, width):
    return pl.ds(pl.multiple_of(j * width, width), width)


def fill_looped(wide_ref, area, onehot_ref, rows_ref):
    def step(j):
        put_rows(wide_ref, j, dot(onehot_ref[...], rows_ref[:, columns(j, 256)]), area * AREA)

    loop(8, step)


def fill(wide_ref, area, onehot, rows_ref):
    for j in range(8):
        put_rows(wide_ref, j, dot(onehot, rows_ref[:, pl.ds(j * 256, 256)]), area * AREA)


def give(wide_ref, sent_ref, areas):
    def step(d, rows):
        for area in range(areas):
            for lane in range(2):
                sent_ref[d, pl.ds(area * ROWS, ROWS), LANES[lane]] = wide_ref[lane, area_rows(d, area), :].astype(bf16)

    each_peer(step)


def near_pack(
    zh_ref, ids_ref, ahead_ids_ref, x_ref, g_ref, resid_ref, gain_ref, table_ref,
    sent_ref, normed_ref, onehot_ref, probs_ref, mix_ref, wide_ref, rows_ref
):
    zh, gain, table = zh_ref[0], gain_ref[...], table_ref[...]
    normed_ref[...], probs_ref[...], _, onehot_ref[...] = routed(ids_ref[...], x_ref[...], zh, gain, table)
    fill(wide_ref, 0, onehot_ref[...], normed_ref)
    fill(wide_ref, 1, onehot_ref[...], g_ref)
    rows_ref[...], probs, pick, onehot = routed(ahead_ids_ref[...], resid_ref[...], zh, gain, table)
    mix_ref[...] = mixed_by(onehot, pick, probs)
    fill(wide_ref, 2, onehot, rows_ref)
    give(wide_ref, sent_ref, 3)


def run_near_pack(*args):
    return call(
        near_pack,
        (
            shape((PEERS, 3 * ROWS, 256)),
            shape((TOK, D)),
            shape((SLOTS, TOK)),
            shape((EXPERTS, TOK), f32),
            shape((SLOTS, TOK)),
        ),
        [SMEM] + [VMEM] * 7,
        [pltpu.VMEM((2, 3 * AREA, 128), f32), pltpu.VMEM((TOK, D), bf16)],
        args,
        2 * 10**9,
        8,
    )


def far_pack(
    zh_ref, ids_ref, x_ref, g_ref, gain_ref, table_ref, sent_ref, normed_ref, onehot_ref, probs_ref, wide_ref
):
    normed_ref[...], probs_ref[...], _, onehot_ref[...] = routed(
        ids_ref[...], x_ref[...], zh_ref[0], gain_ref[...], table_ref[...]
    )
    fill(wide_ref, 0, onehot_ref[...], normed_ref)
    fill(wide_ref, 1, onehot_ref[...], g_ref)
    give(wide_ref, sent_ref, 2)


def run_far_pack(*args):
    return call(
        far_pack,
        (shape((PEERS, 2 * ROWS, 256)), shape((TOK, D)), shape((SLOTS, TOK)), shape((EXPERTS, TOK), f32)),
        [SMEM] + [VMEM] * 5,
        [pltpu.VMEM((2, 2 * AREA, 128), f32)],
        args,
        10**9,
        6,
    )


def ahead_pack(zh_ref, ids_ref, x_ref, gain_ref, table_ref, sent_ref, mix_ref, wide_ref, rows_ref, onehot_ref):
    rows_ref[...], probs, pick, onehot = routed(ids_ref[...], x_ref[...], zh_ref[0], gain_ref[...], table_ref[...])
    mix_ref[...] = mixed_by(onehot, pick, probs)
    onehot_ref[...] = onehot
    fill_looped(wide_ref, 0, onehot_ref, rows_ref)
    give(wide_ref, sent_ref, 1)


def run_ahead_pack(*args):
    return call(
        ahead_pack,
        (shape((PEERS, ROWS, 256)), shape((SLOTS, TOK))),
        [SMEM] + [VMEM] * 4,
        [pltpu.VMEM((2, AREA, 128), f32), pltpu.VMEM((TOK, D), bf16), pltpu.VMEM((SLOTS, TOK), bf16)],
        args,
        10**9,
        4,
    )


def fetched(pairs, sems):
    copies = [pltpu.make_async_copy(a, b, sems.at[i]) for i, (a, b) in enumerate(pairs)]
    for copy in copies:
        copy.start()
    return copies


def expert_slopes(gate_pre, up_pre, down_grad, gate_grad, up_grad):
    sig = 1.0 / (1.0 + jnp.exp(-gate_pre))
    act = gate_pre * sig
    hidden = (act * up_pre).astype(bf16).astype(f32)
    gate_grad[...] = (down_grad * up_pre * sig * (1.0 + gate_pre * (1.0 - sig))).astype(bf16)
    up_grad[...] = (down_grad * act).astype(bf16)
    return jnp.sum(hidden * down_grad, axis=-1, keepdims=True).astype(bf16).astype(f32)


def small_grads(grads, place):
    p, lane = iota((SLOTS, 128), 0), iota((SLOTS, 128), 1)
    gather = marks(iota((PEERS * 8, SLOTS), 1) // MOST == iota((PEERS * 8, SLOTS), 0) // 8)
    spread = jnp.where(lane == p % MOST + place * MOST, grads, 0.0)
    return dot(gather, spread.astype(bf16))


def behind_half(got_ref, weights, place, wide_ref, sems, gate_grad, up_grad):
    (gate_hbm, gate_ref), (up_hbm, up_ref), (down_hbm, down_ref) = weights
    copies = fetched(weights, sems)

    def take(d, rows):
        for lane in range(2):
            for kind in range(2):
                wide_ref[lane, area_rows(d, kind), :] = got_ref[d, pl.ds(kind * ROWS, ROWS), LANES[lane]].astype(f32)

    each_peer(take)
    copies[0].wait()
    copies[1].wait()
    gate_pre, up_pre = jnp.zeros((SLOTS, FF), f32), jnp.zeros((SLOTS, FF), f32)
    for j in range(4):
        rows = jnp.concatenate([get_rows(wide_ref, 2 * j + i, SLOTS) for i in range(2)], axis=1)
        gate_pre = gate_pre + dot(rows, gate_ref[pl.ds(j * 512, 512), :])
        up_pre = up_pre + dot(rows, up_ref[pl.ds(j * 512, 512), :])
    copies[2].wait()
    down_grad = jnp.zeros((SLOTS, FF), f32)
    for j in range(4):
        rows = jnp.concatenate([get_rows(wide_ref, 2 * j + i, SLOTS, AREA) for i in range(2)], axis=1)
        down_grad = down_grad + dot(rows, down_ref[:, pl.ds(j * 512, 512)], ACROSS)
    grads = expert_slopes(gate_pre, up_pre, down_grad, gate_grad, up_grad)
    for j in range(8):
        part = pl.ds(j * 256, 256)
        rows = dot(gate_grad[...], gate_ref[part, :], ACROSS) + dot(up_grad[...], up_ref[part, :], ACROSS)
        put_rows(wide_ref, j, rows)
    return small_grads(grads, place)


def near_experts(
    got_ref, gate_hbm, up_hbm, down_hbm, back_ref, small_ref, wide_ref, gate_ref, up_ref, down_ref, sems,
    gate_sum, up_sum, down_sum, gate_grad, up_grad
):
    copies = fetched(((gate_hbm, gate_ref), (up_hbm, up_ref), (down_hbm, down_ref)), sems)

    def take(d, rows):
        for lane in range(2):
            for kind in range(2):
                wide_ref[lane, area_rows(d, kind), :] = got_ref[d, pl.ds(kind * ROWS, ROWS), LANES[lane]].astype(f32)

    each_peer(take)
    for ref in (gate_sum, up_sum, down_sum):
        ref[...] = jnp.zeros((SLOTS, FF), f32)
    for copy in copies:
        copy.wait()

    def inward(j):
        rows = jnp.concatenate([get_rows(wide_ref, 2 * j + i, SLOTS) for i in range(2)], axis=1)
        gate_sum[...] += dot(rows, gate_ref[columns(j, 512), :])
        up_sum[...] += dot(rows, up_ref[columns(j, 512), :])
        rows = jnp.concatenate([get_rows(wide_ref, 2 * j + i, SLOTS, AREA) for i in range(2)], axis=1)
        down_sum[...] += dot(rows, down_ref[:, columns(j, 512)], ACROSS)

    loop(4, inward)
    grads = expert_slopes(gate_sum[...], up_sum[...], down_sum[...], gate_grad, up_grad)

    def outward(j):
        part = columns(j, 256)
        rows = dot(gate_grad[...], gate_ref[part, :], ACROSS) + dot(up_grad[...], up_ref[part, :], ACROSS)
        put_rows(wide_ref, j, rows)

    loop(8, outward)
    small_ref[...] = small_grads(grads, 0)

    def put(d, rows):
        for lane in range(2):
            back_ref[d, :, LANES[lane]] = wide_ref[lane, rows, :].astype(bf16)

    each_peer(put)


def far_experts(
    got_ref, near_ref, near_small_ref, gate_hbm, up_hbm, down_hbm, back_ref, wide_ref, gate_ref, up_ref, down_ref, sems,
    gate_grad, up_grad
):
    weights = ((gate_hbm, gate_ref), (up_hbm, up_ref), (down_hbm, down_ref))
    small = behind_half(got_ref, weights, 1, wide_ref, sems, gate_grad, up_grad) + near_small_ref[...]
    wide_ref[0, pl.ds(AREA, PEERS * 8), :] = small

    def put(d, rows):
        for lane in range(2):
            back_ref[d, pl.ds(0, ROWS), LANES[lane]] = near_ref[d, :, LANES[lane]]
            back_ref[d, pl.ds(ROWS, ROWS), LANES[lane]] = wide_ref[lane, rows, :].astype(bf16)
        extra = wide_ref[0, pl.ds(pl.multiple_of(AREA + d * 8, 8), 8), :].astype(bf16)
        back_ref[d, pl.ds(2 * ROWS, 8), LANES[0]] = extra
        back_ref[d, pl.ds(2 * ROWS, 8), LANES[1]] = extra

    each_peer(put)


GRADS = [pltpu.VMEM((SLOTS, FF), bf16)] * 2
WEIGHTS = [
    pltpu.VMEM((D, FF), bf16),
    pltpu.VMEM((D, FF), bf16),
    pltpu.VMEM((FF, D), bf16),
    pltpu.SemaphoreType.DMA((3,)),
]


def run_near_experts(*args):
    return call(
        near_experts,
        (shape((PEERS, ROWS, 256)), shape((PEERS * 8, 128), f32)),
        [VMEM] + [HBM] * 3,
        [pltpu.VMEM((2, 2 * AREA, 128), f32)] + WEIGHTS + [pltpu.VMEM((SLOTS, FF), f32)] * 3 + GRADS,
        args,
        5 * 10**9,
        13,
    )


def run_far_experts(*args):
    return call(
        far_experts,
        (shape((PEERS, 2 * ROWS + 8, 256)),),
        [VMEM] * 3 + [HBM] * 3,
        [pltpu.VMEM((2, 2 * AREA, 128), f32)] + WEIGHTS + GRADS,
        args,
        5 * 10**9,
        15,
    )[0]


def ahead_experts(
    near_ref, far_ref, gate_hbm, up_hbm, down_hbm, first_ref, second_ref, wide_ref, gate_ref, up_ref, down_ref, sems,
    gate_sum, up_sum, hidden_ref
):
    copies = fetched(((gate_hbm, gate_ref), (up_hbm, up_ref), (down_hbm, down_ref)), sems)
    count = 2 * SLOTS

    def take(d, rows):
        for lane in range(2):
            wide_ref[lane, area_rows(d, 0), :] = near_ref[d, pl.ds(2 * ROWS, ROWS), LANES[lane]].astype(f32)
            wide_ref[lane, area_rows(d, 1), :] = far_ref[d, :, LANES[lane]].astype(f32)

    each_peer(take)
    copies[0].wait()
    copies[1].wait()
    gate_sum[...] = jnp.zeros((count, FF), f32)
    up_sum[...] = jnp.zeros((count, FF), f32)

    def inward(j):
        rows = jnp.concatenate([get_rows(wide_ref, 2 * j, count), get_rows(wide_ref, 2 * j + 1, count)], axis=1)
        gate_sum[...] += dot(rows, gate_ref[columns(j, 512), :])
        up_sum[...] += dot(rows, up_ref[columns(j, 512), :])

    loop(4, inward)
    gate_pre = gate_sum[...]
    hidden_ref[...] = (gate_pre / (1.0 + jnp.exp(-gate_pre)) * up_sum[...]).astype(bf16)
    copies[2].wait()

    def outward(j):
        put_rows(wide_ref, j, dot(hidden_ref[...], down_ref[:, columns(j, 256)]))

    loop(8, outward)

    def put(d, rows):
        for lane in range(2):
            first_ref[d, :, LANES[lane]] = wide_ref[lane, area_rows(d, 1), :].astype(bf16)
            second_ref[d, :, LANES[lane]] = wide_ref[lane, area_rows(d, 0), :].astype(bf16)

    each_peer(put)


def run_ahead_experts(*args):
    return call(
        ahead_experts,
        (shape((PEERS, ROWS, 256)), shape((PEERS, ROWS, 256))),
        [VMEM] * 2 + [HBM] * 3,
        [pltpu.VMEM((2, 2 * AREA, 128), f32)]
        + WEIGHTS
        + [pltpu.VMEM((2 * SLOTS, FF), f32), pltpu.VMEM((2 * SLOTS, FF), f32), pltpu.VMEM((2 * SLOTS, FF), bf16)],
        args,
        6 * 10**9,
        14,
    )


def attend(length_ref, x_ref, q_ref, kc_ref, kn_ref, vc_ref, vn_ref, resid_ref):
    length = length_ref[0, 0]
    row, col = iota((TOK, 2 * TOK), 0), iota((TOK, 2 * TOK), 1)
    visible = ((col < TOK) & (col < length)) | ((col >= TOK) & (col - TOK <= row))
    for kv in range(KV_HEADS):
        part = pl.ds(kv * HEAD_DIM, HEAD_DIM)
        keys = jnp.concatenate([kc_ref[:, part], kn_ref[:, part]], axis=0)
        values = jnp.concatenate([vc_ref[:, part], vn_ref[:, part]], axis=0)
        for h in range(HEADS // KV_HEADS):
            cols = pl.ds((kv * (HEADS // KV_HEADS) + h) * HEAD_DIM, HEAD_DIM)
            scores = dot(q_ref[:, cols], keys, ACROSS) * HEAD_DIM ** (-0.5)
            scores = jnp.where(visible, scores, far_below)
            lifted = jnp.exp(scores - jnp.max(scores, axis=-1, keepdims=True))
            weights = (lifted * (1.0 / jnp.sum(lifted, axis=-1, keepdims=True))).astype(bf16)
            mixed = dot(weights, values).astype(bf16)
            resid_ref[:, cols] = (x_ref[:, cols].astype(f32) + mixed.astype(f32)).astype(bf16)


def run_attend(length, x, q, kc, kn, vc, vn):
    return call(
        attend,
        (shape((TOK, D)),),
        [SMEM] + [VMEM] * 6,
        [],
        (length, x, q, kc, kn, vc, vn),
        3 * 10**9,
        8,
    )[0]


def through_norm(sums, gain, inv, unit):
    scaled = sums * gain
    return inv * (scaled - unit * jnp.mean(scaled * unit, axis=-1, keepdims=True))


def behind_note(zh_ref, home_ref, near_hot_ref, far_hot_ref, note_ref):
    pick = picks(iota((SLOTS, EXPERTS), 0) // MOST, zh_ref[0]).astype(f32)
    small = jnp.concatenate([home_ref[d].astype(f32) for d in range(PEERS)], axis=0)[:, :128].astype(bf16)
    share = marks(iota((SLOTS, PEERS * 8), 0) // MOST * 8 == iota((SLOTS, PEERS * 8), 1))
    small = dot(share, small)
    p, lane = iota((SLOTS, 128), 0) % MOST, iota((SLOTS, 128), 1)
    for half, hot in enumerate((near_hot_ref, far_hot_ref)):
        grads = jnp.sum(jnp.where(lane == p + half * MOST, small, 0.0), axis=-1, keepdims=True)
        note_ref[:, pl.ds(half * TOK, TOK)] = dot((pick * grads).astype(bf16), hot[...], DOWN)


def whole(a):
    return pl.BlockSpec(a.shape, lambda i, n=a.ndim: (0,) * n)


def run_behind_note(zh, home, near_hot, far_hot):
    tail = pl.BlockSpec((PEERS, 8, 256), lambda i: (0, 2 * ROWS // 8, 0))
    return pl.pallas_call(
        behind_note,
        grid=(1,),
        out_shape=shape((EXPERTS, 2 * TOK), f32),
        in_specs=[SMEM, tail, whole(near_hot), whole(far_hot)],
        out_specs=pl.BlockSpec((EXPERTS, 2 * TOK), lambda i: (0, 0)),
        compiler_params=pltpu.CompilerParams(vmem_limit_bytes=63 * 2**20),
        cost_estimate=pl.CostEstimate(flops=10**7, transcendentals=0, bytes_accessed=2**18),
    )(zh, home, near_hot, far_hot)


def behind_sums(
    zh_ref, home_ref, near_hot_ref, far_hot_ref, near_probs_ref, far_probs_ref, near_x_ref, far_x_ref, gain_ref,
    sums_ref, sent_ref, theirs_ref, mine_ref, wide_ref, line_ref, mix_ref
):
    zh = zh_ref[0]

    def take(d, rows):
        for half in range(2):
            for lane in range(2):
                wide_ref[lane, area_rows(d, half), :] = home_ref[d, pl.ds(half * ROWS, ROWS), LANES[lane]].astype(f32)

    each_peer(take)
    pick = picks(iota((SLOTS, EXPERTS), 0) // MOST, zh)
    mix_ref[0] = mixed_by(near_hot_ref[...], pick, near_probs_ref[...])
    mix_ref[1] = mixed_by(far_hot_ref[...], pick, far_probs_ref[...])

    for j in range(8):
        cols = pl.ds(j * 256, 256)
        sums_ref[:, cols] = dot(mix_ref[0], get_rows(wide_ref, j, SLOTS), DOWN)
        line_ref[:, cols] = dot(mix_ref[1], get_rows(wide_ref, j, SLOTS, AREA), DOWN)
    inv, unit = unit_rows(far_x_ref[...])
    sums = line_ref[...]
    sent_ref[...] = through_norm(sums, gain_ref[...], inv, unit).astype(bf16)
    total = jnp.sum(sums * unit, axis=0, keepdims=True)
    _, unit = unit_rows(near_x_ref[...])
    total = total + jnp.sum(sums_ref[...] * unit, axis=0, keepdims=True)
    theirs_ref[...] = jnp.zeros((8, 256), f32)
    mine_ref[...] = jnp.zeros((8, 256), f32)
    for x in range(4):
        first, second = total[:, x * 512 : x * 512 + 256], total[:, x * 512 + 256 : x * 512 + 512]
        mine_ref[pl.ds(x, 1), :] = jnp.where(zh == 0, first, second)
        theirs_ref[pl.ds(x, 1), :] = jnp.where(zh == 0, second, first)


def run_behind_sums(*args):
    return call(
        behind_sums,
        (shape((TOK, D), f32), shape((TOK, D)), shape((8, 256), f32), shape((8, 256), f32)),
        [SMEM] + [VMEM] * 8,
        [
            pltpu.VMEM((2, 2 * AREA, 128), f32),
            pltpu.VMEM((TOK, D), f32),
            pltpu.VMEM((2, SLOTS, TOK), bf16),
        ],
        args,
        10**9,
        6,
    )


def behind_end(
    near_note_ref, far_note_ref, sums_ref, near_probs_ref, far_probs_ref, x_ref, g_ref, gain_ref, table_ref,
    sent_ref, near_logit_ref, far_logit_ref
):
    near_tok, far_tok = pl.ds(0, TOK), pl.ds(TOK, TOK)

    def logit_grads(probs, grads):
        return (probs * (grads - jnp.sum(probs * grads, axis=0, keepdims=True))).astype(bf16)

    near_logit_ref[...] = logit_grads(near_probs_ref[...], near_note_ref[:, near_tok] + far_note_ref[:, far_tok])
    far_logit_ref[...] = logit_grads(far_probs_ref[...], near_note_ref[:, far_tok] + far_note_ref[:, near_tok])
    inv, unit = unit_rows(x_ref[...])
    sums = sums_ref[...] + dot(near_logit_ref[...], table_ref[...], DOWN)
    sent_ref[...] = (g_ref[...].astype(f32) + through_norm(sums, gain_ref[...], inv, unit)).astype(bf16)


def run_behind_end(*args):
    return call(
        behind_end,
        (shape((TOK, D)), shape((EXPERTS, TOK)), shape((EXPERTS, TOK))),
        [VMEM] * 9,
        [],
        args,
        10**9,
        4,
    )


def share_parts(
    zh_ref, near_logit_ref, far_logit_ref, mine_ref, theirs_ref, near_normed_ref, far_normed_ref, near_x_ref,
    far_x_ref, table_ref, shares_ref
):
    zh = zh_ref[0]
    near_logit, far_logit = near_logit_ref[...], far_logit_ref[...]
    _, near_unit = unit_rows(near_x_ref[...])
    _, far_unit = unit_rows(far_x_ref[...])
    near_term, far_term = dot(near_logit, table_ref[...], DOWN), dot(far_logit, table_ref[...], DOWN)
    total = jnp.sum(near_term * near_unit + far_term * far_unit, axis=0, keepdims=True)
    row = iota((128 - EXPERTS, 256), 0)
    for x in range(4):
        first, second = total[:, x * 512 : x * 512 + 256], total[:, x * 512 + 256 : x * 512 + 512]
        gains = jnp.where(zh == 0, first, second) + mine_ref[pl.ds(x, 1), :] + theirs_ref[pl.ds(x, 1), :]
        cols = pl.ds(pl.multiple_of(x * 512 + zh * 256, 256), 256)
        part = dot(near_logit, near_normed_ref[:, cols]) + dot(far_logit, far_normed_ref[:, cols])
        both = jnp.concatenate([part, jnp.where(row == 0, gains, 0.0)], axis=0)
        shares_ref[pl.ds(x * 256, 256), :] = both.T.astype(bf16)


def run_share_parts(*args):
    return call(share_parts, (shape((D // 2, 128)),), [SMEM] + [VMEM] * 9, [], args, 10**9, 3)[0]


def ahead_sums(home_ref, mix_ref, wide_ref):
    def take(d, rows):
        for lane in range(2):
            wide_ref[lane, rows, :] = home_ref[d, :, LANES[lane]].astype(f32)

    each_peer(take)
    for j in range(8):
        yield pl.ds(j * 256, 256), dot(mix_ref[...], get_rows(wide_ref, j, SLOTS), DOWN)


def ahead_far(home_ref, mix_ref, out_ref, wide_ref):
    for cols, sums in ahead_sums(home_ref, mix_ref, wide_ref):
        out_ref[:, cols] = sums.astype(bf16)


def ahead_near(home_ref, mix_ref, resid_ref, out_ref, wide_ref):
    for cols, sums in ahead_sums(home_ref, mix_ref, wide_ref):
        out_ref[:, cols] = (resid_ref[:, cols].astype(f32) + sums).astype(bf16)


def run_ahead_end(kernel, *args):
    return call(
        kernel, (shape((TOK, D)),), [VMEM] * len(args), [pltpu.VMEM((2, AREA, 128), f32)], args, 10**9, 3
    )[0]


def share_sums(got_ref, router_ref, gain_ref):
    total = got_ref[0].astype(f32)
    for source in range(1, PEERS):
        total = total + got_ref[source].astype(f32)
    total = total * factor
    router_ref[...] = total[:, :EXPERTS]
    gain_ref[...] = total.T[EXPERTS : EXPERTS + 1, :]


def run_share_sums(got):
    return call(
        share_sums, (shape((PEERS, EXPERTS), f32), shape((1, PEERS), f32)), [VMEM], [], (got,), 10**6, 1
    )


def body(
    forward_input,
    queries,
    new_keys,
    new_values,
    cache_keys,
    cache_values,
    context_lengths,
    norm_gain,
    router,
    gate_weight,
    up_weight,
    down_weight,
    forward_ids,
    backward_input,
    backward_ids,
    output_grad,
):
    zh = lax.axis_index("zh").astype(jnp.int32).reshape(1)
    gain = norm_gain
    table = router[0].T
    weights = (gate_weight[0, 0], up_weight[0, 0], down_weight[0, 0])
    back_x, back_g = backward_input[0], output_grad[0]
    ids_b, ids_f = backward_ids[0].T, forward_ids[0].T
    ids_far = swapped(jnp.concatenate([ids_b, ids_f], axis=0))
    x_far = swapped(back_x)
    g_far = swapped(back_g)
    resid = run_attend(
        context_lengths,
        forward_input[0],
        queries[0],
        cache_keys[0],
        new_keys[0],
        cache_values[0],
        new_values[0],
    )
    resid_far = swapped(resid)
    sent_1, normed_b, hot_b, probs_b, mix_f = run_near_pack(
        zh, ids_b, ids_f, back_x, back_g, resid, gain, table
    )
    got_1 = spread_out(sent_1)
    sent_2, normed_c, hot_c, probs_c = run_far_pack(zh, ids_far[:4], x_far, g_far, gain, table)
    sent_2, _ = lax.optimization_barrier((sent_2, got_1))
    got_2 = spread_out(sent_2)
    sent_3, mix_h = run_ahead_pack(zh, ids_far[4:], resid_far, gain, table)
    sent_3, got_2 = lax.optimization_barrier((sent_3, got_2))
    got_3 = spread_out(sent_3)
    back_b, small_b = run_near_experts(got_1, *weights)
    back = run_far_experts(got_2, back_b, small_b, *weights)
    back, got_3 = lax.optimization_barrier((back, got_3))
    home_b = spread_out(back)
    made_1, made_2 = run_ahead_experts(got_1, got_3, *weights)
    made_1, home_b = lax.optimization_barrier((made_1, home_b))
    home_1 = spread_out(made_1)
    note = run_behind_note(zh, home_b, hot_b, hot_c)
    far_note = swapped(note)
    sums_b, own_c, theirs, mine = run_behind_sums(
        zh, home_b, hot_b, hot_c, probs_b, probs_c, back_x, x_far, gain
    )
    moved_c = moved(own_c, False, -1)
    own_b, logit_b, logit_c = run_behind_end(
        note, far_note, sums_b, probs_b, probs_c, back_x, back_g, gain, table
    )
    moved_b = moved(own_b, True, -1)
    made_2, home_1 = lax.optimization_barrier((made_2, home_1))
    home_2 = spread_out(made_2)
    own_h = run_ahead_end(ahead_far, home_1, mix_h)
    moved_h = moved(own_h, False, 1)
    theirs = swapped(theirs)
    shares = run_share_parts(
        zh, logit_b, logit_c, mine, theirs, normed_b, normed_c, back_x, x_far, table
    )
    own_f = run_ahead_end(ahead_near, home_2, mix_f, resid)
    moved_f = moved(own_f, True, 1)
    shares, own_f = lax.optimization_barrier((shares, own_f))
    got_s = spread_out(shares.reshape(PEERS, PEERS, 128))
    router_grad, gain_grad = run_share_sums(got_s)
    input_grad = (moved_b.astype(f32) + moved_c.astype(f32)).astype(bf16)
    forward_output = (moved_f.astype(f32) + moved_h.astype(f32)).astype(bf16)
    return forward_output[None], input_grad[None], router_grad[None], gain_grad


def solution(mesh):
    grid = Mesh(mesh.devices.reshape(4, 4, 2, 4, 2), ("pipe", "x", "zh", "y", "core"))
    rows = P("pipe", ALL, None)
    placed = (
        rows,
        rows,
        rows,
        rows,
        rows,
        rows,
        P("pipe", ALL),
        P("pipe", None),
        P("pipe", None, None),
        P("pipe", ALL, None, None),
        P("pipe", ALL, None, None),
        P("pipe", ALL, None, None),
        rows,
        rows,
        rows,
        rows,
    )
    return jax.shard_map(
        body,
        mesh=grid,
        in_specs=placed,
        out_specs=(rows, rows, rows, P("pipe", ALL)),
        check_vma=False,
    )
```

```python
import jax
import jax.numpy as jnp
from jax import lax
from jax.experimental import pallas as pl
from jax.experimental.pallas import tpu as pltpu
from jax.sharding import Mesh, PartitionSpec as P


HEADS = 16
KV_HEADS = 2
HEAD_DIM = 128
D = 2048
FF = 768
EXPERTS = 64
MOST = 9
TOK = 128
PEERS = 32
SLOTS = PEERS * MOST
ROWS = MOST * 8
AREA = SLOTS * 8
XY = ("x", "y", "core")
ALL = ("x", "zh", "y", "core")

epsilon = 1e-06
far_below = -1e30
factor = 8192 ** (-0.5)
bf16 = jnp.bfloat16
f32 = jnp.float32
ACROSS = (((1,), (1,)), ((), ()))
DOWN = (((0,), (0,)), ((), ()))
VMEM = pl.BlockSpec(memory_space=pltpu.VMEM)
SMEM = pl.BlockSpec(memory_space=pltpu.SMEM)
HBM = pl.BlockSpec(memory_space=pltpu.HBM)


def spread_out(x):
    return lax.all_to_all(x, XY, 0, 0, tiled=True)


def swapped(x):
    return lax.ppermute(x, "zh", [(0, 1), (1, 0)])


def moved(x, same, step):
    pairs = []
    for pipe in range(4):
        for zh in range(2):
            to = ((pipe + step) % 4) * 2 + (zh if same else 1 - zh)
            pairs.append((pipe * 2 + zh, to))
    return lax.ppermute(x, ("pipe", "zh"), pairs)


def shape(dims, dtype=bf16):
    return jax.ShapeDtypeStruct(dims, dtype)


def call(kernel, outs, ins, scratch, args, flops, mib):
    return pl.pallas_call(
        kernel,
        out_shape=outs,
        in_specs=ins,
        out_specs=tuple(VMEM for _ in outs),
        scratch_shapes=scratch,
        compiler_params=pltpu.CompilerParams(vmem_limit_bytes=63 * 2**20),
        cost_estimate=pl.CostEstimate(
            flops=flops, transcendentals=0, bytes_accessed=mib * 2**20
        ),
    )(*args)


def dot(a, b, dims=None):
    if dims is None:
        return jnp.dot(a, b, preferred_element_type=f32)
    return lax.dot_general(a, b, dims, preferred_element_type=f32)


def iota(dims, dim):
    return lax.broadcasted_iota(jnp.int32, dims, dim)


def marks(cond):
    return cond.astype(f32).astype(bf16)


def unit_rows(x):
    wide = x.astype(f32)
    inv_rms = lax.rsqrt(jnp.mean(wide * wide, axis=-1, keepdims=True) + epsilon)
    return inv_rms, wide * inv_rms


def hits(ids):
    expert = iota((EXPERTS, ids.shape[1]), 0)
    hit = ids[0:1, :] == expert
    for k in range(1, 4):
        hit = hit | (ids[k : k + 1, :] == expert)
    return hit


def choice(normed, table, hit):
    logits = jnp.where(hit, dot(table, normed, ACROSS), far_below)
    lifted = jnp.where(hit, jnp.exp(logits - jnp.max(logits, axis=0, keepdims=True)), 0.0)
    return lifted / jnp.sum(lifted, axis=0, keepdims=True)


def ranked(hit):
    tokens = hit.shape[1]
    earlier, later = iota((tokens, tokens), 0), iota((tokens, tokens), 1)
    before = marks((earlier < later) & (earlier // TOK == later // TOK))
    hit = hit.astype(f32)
    return (hit * (dot(hit.astype(bf16), before) + 1.0)).astype(bf16)


def picks(peer, zh):
    owner = (peer // 8) * 16 + zh * 8 + peer % 8
    return marks(owner == iota(peer.shape, 1))


def each_peer(step):
    def turn(d, carry):
        step(d, pl.ds(pl.multiple_of(d * ROWS, 8), ROWS))
        return carry

    lax.fori_loop(0, PEERS, turn, 0)


def area_rows(d, area):
    return pl.ds(pl.multiple_of(d * ROWS + area * AREA, 8), ROWS)


LANES = (pl.ds(0, 128), pl.ds(128, 128))


def put_rows(wide_ref, j, rows, start=0):
    for lane in range(rows.shape[1] // 128):
        wide_ref[lane, pl.ds(start + j, rows.shape[0], stride=8), :] = rows[
            :, lane * 128 : lane * 128 + 128
        ]


def get_rows(wide_ref, j, count, start=0):
    return jnp.concatenate(
        [
            wide_ref[lane, pl.ds(start + j, count, stride=8), :].astype(bf16)
            for lane in range(wide_ref.shape[0])
        ],
        axis=1,
    )


def routed(ids, x, zh, gain, table):
    hit = hits(ids)
    _, unit = unit_rows(x)
    normed = (unit * gain).astype(bf16)
    probs = choice(normed, table, hit)
    pick = picks(iota((SLOTS, EXPERTS), 0) // MOST, zh)
    slot = (iota((SLOTS, TOK), 0) % MOST + 1).astype(f32)
    return normed, probs, pick, marks(dot(pick, ranked(hit)) == slot)


def mixed_by(onehot, pick, probs):
    return onehot * dot(pick, probs.astype(bf16)).astype(bf16)


def loop(count, step):
    def turn(i, carry):
        step(i)
        return carry

    lax.fori_loop(0, count, turn, 0)


def columns(j, width):
    return pl.ds(pl.multiple_of(j * width, width), width)


def fill_looped(wide_ref, area, onehot_ref, rows_ref):
    def step(j):
        put_rows(wide_ref, j, dot(onehot_ref[...], rows_ref[:, columns(j, 256)]), area * AREA)

    loop(8, step)


def fill(wide_ref, area, onehot, rows_ref):
    for j in range(8):
        put_rows(wide_ref, j, dot(onehot, rows_ref[:, pl.ds(j * 256, 256)]), area * AREA)


def give(wide_ref, sent_ref, areas):
    def step(d, rows):
        for area in range(areas):
            for lane in range(2):
                sent_ref[d, pl.ds(area * ROWS, ROWS), LANES[lane]] = wide_ref[lane, area_rows(d, area), :].astype(bf16)

    each_peer(step)


def near_pack(
    zh_ref, ids_ref, ahead_ids_ref, x_ref, g_ref, resid_ref, gain_ref, table_ref,
    sent_ref, normed_ref, onehot_ref, probs_ref, mix_ref, wide_ref, rows_ref
):
    zh, gain, table = (zh_ref[0] & 1), gain_ref[...], table_ref[...]
    normed_ref[...], probs_ref[...], _, onehot_ref[...] = routed(ids_ref[...], x_ref[...], zh, gain, table)
    fill(wide_ref, 0, onehot_ref[...], normed_ref)
    fill(wide_ref, 1, onehot_ref[...], g_ref)
    rows_ref[...], probs, pick, onehot = routed(ahead_ids_ref[...], resid_ref[...], zh, gain, table)
    mix_ref[...] = mixed_by(onehot, pick, probs)
    fill(wide_ref, 2, onehot, rows_ref)
    give(wide_ref, sent_ref, 3)


def run_near_pack(*args):
    return call(
        near_pack,
        (
            shape((PEERS, 3 * ROWS, 256)),
            shape((TOK, D)),
            shape((SLOTS, TOK)),
            shape((EXPERTS, TOK), f32),
            shape((SLOTS, TOK)),
        ),
        [SMEM] + [VMEM] * 7,
        [pltpu.VMEM((2, 3 * AREA, 128), f32), pltpu.VMEM((TOK, D), bf16)],
        args,
        2 * 10**9,
        8,
    )


def far_pack(
    zh_ref, ids_ref, x_ref, g_ref, gain_ref, table_ref, sent_ref, normed_ref, onehot_ref, probs_ref, wide_ref
):
    normed_ref[...], probs_ref[...], _, onehot_ref[...] = routed(
        ids_ref[...], x_ref[...], (zh_ref[0] & 1), gain_ref[...], table_ref[...]
    )
    fill(wide_ref, 0, onehot_ref[...], normed_ref)
    fill(wide_ref, 1, onehot_ref[...], g_ref)
    give(wide_ref, sent_ref, 2)


def run_far_pack(*args):
    return call(
        far_pack,
        (shape((PEERS, 2 * ROWS, 256)), shape((TOK, D)), shape((SLOTS, TOK)), shape((EXPERTS, TOK), f32)),
        [SMEM] + [VMEM] * 5,
        [pltpu.VMEM((2, 2 * AREA, 128), f32)],
        args,
        10**9,
        6,
    )


def ahead_pack(zh_ref, ids_ref, x_ref, gain_ref, table_ref, sent_ref, mix_ref, wide_ref, rows_ref, onehot_ref):
    rows_ref[...], probs, pick, onehot = routed(ids_ref[...], x_ref[...], (zh_ref[0] & 1), gain_ref[...], table_ref[...])
    mix_ref[...] = mixed_by(onehot, pick, probs)
    onehot_ref[...] = onehot
    fill_looped(wide_ref, 0, onehot_ref, rows_ref)
    give(wide_ref, sent_ref, 1)


def run_ahead_pack(*args):
    return call(
        ahead_pack,
        (shape((PEERS, ROWS, 256)), shape((SLOTS, TOK))),
        [SMEM] + [VMEM] * 4,
        [pltpu.VMEM((2, AREA, 128), f32), pltpu.VMEM((TOK, D), bf16), pltpu.VMEM((SLOTS, TOK), bf16)],
        args,
        10**9,
        4,
    )


def fetched(pairs, sems):
    copies = [pltpu.make_async_copy(a, b, sems.at[i]) for i, (a, b) in enumerate(pairs)]
    for copy in copies:
        copy.start()
    return copies


def expert_slopes(gate_pre, up_pre, down_grad, gate_grad, up_grad):
    sig = 1.0 / (1.0 + jnp.exp(-gate_pre))
    act = gate_pre * sig
    hidden = (act * up_pre).astype(bf16).astype(f32)
    gate_grad[...] = (down_grad * up_pre * sig * (1.0 + gate_pre * (1.0 - sig))).astype(bf16)
    up_grad[...] = (down_grad * act).astype(bf16)
    return jnp.sum(hidden * down_grad, axis=-1, keepdims=True).astype(bf16).astype(f32)


def small_grads(grads, place):
    p, lane = iota((SLOTS, 128), 0), iota((SLOTS, 128), 1)
    gather = marks(iota((PEERS * 8, SLOTS), 1) // MOST == iota((PEERS * 8, SLOTS), 0) // 8)
    spread = jnp.where(lane == p % MOST + place * MOST, grads, 0.0)
    return dot(gather, spread.astype(bf16))


def behind_half(got_ref, weights, place, wide_ref, sems, gate_grad, up_grad):
    (gate_hbm, gate_ref), (up_hbm, up_ref), (down_hbm, down_ref) = weights
    copies = fetched(weights, sems)

    def take(d, rows):
        for lane in range(2):
            for kind in range(2):
                wide_ref[lane, area_rows(d, kind), :] = got_ref[d, pl.ds(kind * ROWS, ROWS), LANES[lane]].astype(f32)

    each_peer(take)
    copies[0].wait()
    copies[1].wait()
    gate_pre, up_pre = jnp.zeros((SLOTS, FF), f32), jnp.zeros((SLOTS, FF), f32)
    for j in range(4):
        rows = jnp.concatenate([get_rows(wide_ref, 2 * j + i, SLOTS) for i in range(2)], axis=1)
        gate_pre = gate_pre + dot(rows, gate_ref[pl.ds(j * 512, 512), :])
        up_pre = up_pre + dot(rows, up_ref[pl.ds(j * 512, 512), :])
    copies[2].wait()
    down_grad = jnp.zeros((SLOTS, FF), f32)
    for j in range(4):
        rows = jnp.concatenate([get_rows(wide_ref, 2 * j + i, SLOTS, AREA) for i in range(2)], axis=1)
        down_grad = down_grad + dot(rows, down_ref[:, pl.ds(j * 512, 512)], ACROSS)
    grads = expert_slopes(gate_pre, up_pre, down_grad, gate_grad, up_grad)
    for j in range(8):
        part = pl.ds(j * 256, 256)
        rows = dot(gate_grad[...], gate_ref[part, :], ACROSS) + dot(up_grad[...], up_ref[part, :], ACROSS)
        put_rows(wide_ref, j, rows)
    return small_grads(grads, place)


def near_experts(
    got_ref, gate_hbm, up_hbm, down_hbm, back_ref, small_ref, wide_ref, gate_ref, up_ref, down_ref, sems,
    gate_sum, up_sum, down_sum, gate_grad, up_grad
):
    copies = fetched(((gate_hbm, gate_ref), (up_hbm, up_ref), (down_hbm, down_ref)), sems)

    def take(d, rows):
        for lane in range(2):
            for kind in range(2):
                wide_ref[lane, area_rows(d, kind), :] = got_ref[d, pl.ds(kind * ROWS, ROWS), LANES[lane]].astype(f32)

    each_peer(take)
    for ref in (gate_sum, up_sum, down_sum):
        ref[...] = jnp.zeros((SLOTS, FF), f32)
    for copy in copies:
        copy.wait()

    def inward(j):
        rows = jnp.concatenate([get_rows(wide_ref, 2 * j + i, SLOTS) for i in range(2)], axis=1)
        gate_sum[...] += dot(rows, gate_ref[columns(j, 512), :])
        up_sum[...] += dot(rows, up_ref[columns(j, 512), :])
        rows = jnp.concatenate([get_rows(wide_ref, 2 * j + i, SLOTS, AREA) for i in range(2)], axis=1)
        down_sum[...] += dot(rows, down_ref[:, columns(j, 512)], ACROSS)

    loop(4, inward)
    grads = expert_slopes(gate_sum[...], up_sum[...], down_sum[...], gate_grad, up_grad)

    def outward(j):
        part = columns(j, 256)
        rows = dot(gate_grad[...], gate_ref[part, :], ACROSS) + dot(up_grad[...], up_ref[part, :], ACROSS)
        put_rows(wide_ref, j, rows)

    loop(8, outward)
    small_ref[...] = small_grads(grads, 0)

    def put(d, rows):
        for lane in range(2):
            back_ref[d, :, LANES[lane]] = wide_ref[lane, rows, :].astype(bf16)

    each_peer(put)


def far_experts(
    got_ref, near_small_ref, gate_hbm, up_hbm, down_hbm, back_ref, wide_ref, gate_ref, up_ref, down_ref, sems,
    gate_grad, up_grad
):
    weights = ((gate_hbm, gate_ref), (up_hbm, up_ref), (down_hbm, down_ref))
    small = behind_half(got_ref, weights, 1, wide_ref, sems, gate_grad, up_grad) + near_small_ref[...]
    wide_ref[0, pl.ds(AREA, PEERS * 8), :] = small

    def put(d, rows):
        for lane in range(2):
            back_ref[d, pl.ds(0, ROWS), LANES[lane]] = wide_ref[lane, rows, :].astype(bf16)
        extra = wide_ref[0, pl.ds(pl.multiple_of(AREA + d * 8, 8), 8), :].astype(bf16)
        back_ref[d, pl.ds(ROWS, 8), LANES[0]] = extra
        back_ref[d, pl.ds(ROWS, 8), LANES[1]] = extra

    each_peer(put)


GRADS = [pltpu.VMEM((SLOTS, FF), bf16)] * 2
WEIGHTS = [
    pltpu.VMEM((D, FF), bf16),
    pltpu.VMEM((D, FF), bf16),
    pltpu.VMEM((FF, D), bf16),
    pltpu.SemaphoreType.DMA((3,)),
]


def run_near_experts(*args):
    return call(
        near_experts,
        (shape((PEERS, ROWS, 256)), shape((PEERS * 8, 128), f32)),
        [VMEM] + [HBM] * 3,
        [pltpu.VMEM((2, 2 * AREA, 128), f32)] + WEIGHTS + [pltpu.VMEM((SLOTS, FF), f32)] * 3 + GRADS,
        args,
        5 * 10**9,
        13,
    )


def run_far_experts(*args):
    return call(
        far_experts,
        (shape((PEERS, ROWS + 8, 256)),),
        [VMEM] * 2 + [HBM] * 3,
        [pltpu.VMEM((2, 2 * AREA, 128), f32)] + WEIGHTS + GRADS,
        args,
        5 * 10**9,
        15,
    )[0]


def ahead_experts(
    near_ref, far_ref, gate_hbm, up_hbm, down_hbm, made_ref, wide_ref, gate_ref, up_ref, down_ref, sems,
    gate_sum, up_sum, hidden_ref
):
    copies = fetched(((gate_hbm, gate_ref), (up_hbm, up_ref), (down_hbm, down_ref)), sems)
    count = 2 * SLOTS

    def take(d, rows):
        for lane in range(2):
            wide_ref[lane, area_rows(d, 0), :] = near_ref[d, pl.ds(2 * ROWS, ROWS), LANES[lane]].astype(f32)
            wide_ref[lane, area_rows(d, 1), :] = far_ref[d, :, LANES[lane]].astype(f32)

    each_peer(take)
    copies[0].wait()
    copies[1].wait()
    gate_sum[...] = jnp.zeros((count, FF), f32)
    up_sum[...] = jnp.zeros((count, FF), f32)

    def inward(j):
        rows = jnp.concatenate([get_rows(wide_ref, 2 * j, count), get_rows(wide_ref, 2 * j + 1, count)], axis=1)
        gate_sum[...] += dot(rows, gate_ref[columns(j, 512), :])
        up_sum[...] += dot(rows, up_ref[columns(j, 512), :])

    loop(4, inward)
    gate_pre = gate_sum[...]
    hidden_ref[...] = (gate_pre / (1.0 + jnp.exp(-gate_pre)) * up_sum[...]).astype(bf16)
    copies[2].wait()

    def outward(j):
        put_rows(wide_ref, j, dot(hidden_ref[...], down_ref[:, columns(j, 256)]))

    loop(8, outward)

    def put(d, rows):
        for lane in range(2):
            for half in range(2):
                made_ref[d, pl.ds(half * ROWS, ROWS), LANES[lane]] = wide_ref[lane, area_rows(d, half), :].astype(bf16)

    each_peer(put)


def run_ahead_experts(*args):
    return call(
        ahead_experts,
        (shape((PEERS, 2 * ROWS, 256)),),
        [VMEM] * 2 + [HBM] * 3,
        [pltpu.VMEM((2, 2 * AREA, 128), f32)]
        + WEIGHTS
        + [pltpu.VMEM((2 * SLOTS, FF), f32), pltpu.VMEM((2 * SLOTS, FF), f32), pltpu.VMEM((2 * SLOTS, FF), bf16)],
        args,
        6 * 10**9,
        14,
    )[0]


def attend(length_ref, x_ref, q_ref, kc_ref, kn_ref, vc_ref, vn_ref, resid_ref):
    length = length_ref[0, 0]
    row, col = iota((TOK, 2 * TOK), 0), iota((TOK, 2 * TOK), 1)
    visible = ((col < TOK) & (col < length)) | ((col >= TOK) & (col - TOK <= row))
    for kv in range(KV_HEADS):
        part = pl.ds(kv * HEAD_DIM, HEAD_DIM)
        keys = jnp.concatenate([kc_ref[:, part], kn_ref[:, part]], axis=0)
        values = jnp.concatenate([vc_ref[:, part], vn_ref[:, part]], axis=0)
        for h in range(HEADS // KV_HEADS):
            cols = pl.ds((kv * (HEADS // KV_HEADS) + h) * HEAD_DIM, HEAD_DIM)
            scores = dot(q_ref[:, cols], keys, ACROSS) * HEAD_DIM ** (-0.5)
            scores = jnp.where(visible, scores, far_below)
            lifted = jnp.exp(scores - jnp.max(scores, axis=-1, keepdims=True))
            weights = (lifted * (1.0 / jnp.sum(lifted, axis=-1, keepdims=True))).astype(bf16)
            mixed = dot(weights, values).astype(bf16)
            resid_ref[:, cols] = (x_ref[:, cols].astype(f32) + mixed.astype(f32)).astype(bf16)


def run_attend(length, x, q, kc, kn, vc, vn):
    return call(
        attend,
        (shape((TOK, D)),),
        [SMEM] + [VMEM] * 6,
        [],
        (length, x, q, kc, kn, vc, vn),
        3 * 10**9,
        8,
    )[0]


def through_norm(sums, gain, inv, unit):
    scaled = sums * gain
    return inv * (scaled - unit * jnp.mean(scaled * unit, axis=-1, keepdims=True))


def behind_note(zh_ref, home_ref, near_hot_ref, far_hot_ref, note_ref):
    pick = picks(iota((SLOTS, EXPERTS), 0) // MOST, (zh_ref[0] & 1)).astype(f32)
    small = jnp.concatenate([home_ref[d].astype(f32) for d in range(PEERS)], axis=0)[:, :128].astype(bf16)
    share = marks(iota((SLOTS, PEERS * 8), 0) // MOST * 8 == iota((SLOTS, PEERS * 8), 1))
    small = dot(share, small)
    p, lane = iota((SLOTS, 128), 0) % MOST, iota((SLOTS, 128), 1)
    for half, hot in enumerate((near_hot_ref, far_hot_ref)):
        grads = jnp.sum(jnp.where(lane == p + half * MOST, small, 0.0), axis=-1, keepdims=True)
        note_ref[:, pl.ds(half * TOK, TOK)] = dot((pick * grads).astype(bf16), hot[...], DOWN)


def whole(a):
    return pl.BlockSpec(a.shape, lambda i, n=a.ndim: (0,) * n)


def run_behind_note(zh, home, near_hot, far_hot):
    tail = pl.BlockSpec((PEERS, 8, 256), lambda i: (0, ROWS // 8, 0))
    return pl.pallas_call(
        behind_note,
        grid=(1,),
        out_shape=shape((EXPERTS, 2 * TOK), f32),
        in_specs=[SMEM, tail, whole(near_hot), whole(far_hot)],
        out_specs=pl.BlockSpec((EXPERTS, 2 * TOK), lambda i: (0, 0)),
        compiler_params=pltpu.CompilerParams(vmem_limit_bytes=63 * 2**20),
        cost_estimate=pl.CostEstimate(flops=10**7, transcendentals=0, bytes_accessed=2**18),
    )(zh, home, near_hot, far_hot)


def block_sums(home_ref, mix_ref, wide_ref):
    def take(d, rows):
        for lane in range(2):
            wide_ref[lane, rows, :] = home_ref[d, pl.ds(0, ROWS), LANES[lane]].astype(f32)

    each_peer(take)
    for j in range(8):
        yield pl.ds(j * 256, 256), dot(mix_ref[...], get_rows(wide_ref, j, SLOTS), DOWN)


def behind_far(
    zh_ref, home_ref, hot_ref, probs_ref, x_ref, gain_ref, sent_ref, gains_ref, wide_ref, line_ref, mix_ref
):
    pick = picks(iota((SLOTS, EXPERTS), 0) // MOST, (zh_ref[0] & 1))
    mix_ref[...] = mixed_by(hot_ref[...], pick, probs_ref[...])
    for cols, sums in block_sums(home_ref, mix_ref, wide_ref):
        line_ref[:, cols] = sums
    inv, unit = unit_rows(x_ref[...])
    sums = line_ref[...]
    sent_ref[...] = through_norm(sums, gain_ref[...], inv, unit).astype(bf16)
    gains_ref[...] = jnp.broadcast_to(jnp.sum(sums * unit, axis=0, keepdims=True), (8, D))


SUMMING = [pltpu.VMEM((2, AREA, 128), f32), pltpu.VMEM((TOK, D), f32), pltpu.VMEM((SLOTS, TOK), bf16)]


def run_behind_far(*args):
    return call(
        behind_far, (shape((TOK, D)), shape((8, D), f32)), [SMEM] + [VMEM] * 5, SUMMING, args, 10**9, 4
    )


def behind_near(
    zh_ref, home_ref, hot_ref, probs_ref, logit_ref, gains_ref, x_ref, g_ref, gain_ref, table_ref,
    sent_ref, mine_ref, theirs_ref, wide_ref, line_ref, mix_ref
):
    zh = (zh_ref[0] & 1)
    pick = picks(iota((SLOTS, EXPERTS), 0) // MOST, zh)
    mix_ref[...] = mixed_by(hot_ref[...], pick, probs_ref[...])
    for cols, sums in block_sums(home_ref, mix_ref, wide_ref):
        line_ref[:, cols] = sums
    inv, unit = unit_rows(x_ref[...])
    sums = line_ref[...] + dot(logit_ref[...], table_ref[...], DOWN)
    sent_ref[...] = (g_ref[...].astype(f32) + through_norm(sums, gain_ref[...], inv, unit)).astype(bf16)
    total = jnp.sum(sums * unit, axis=0, keepdims=True) + gains_ref[pl.ds(0, 1), :]
    theirs_ref[...] = jnp.zeros((8, 256), f32)
    mine_ref[...] = jnp.zeros((8, 256), f32)
    for x in range(4):
        first, second = total[:, x * 512 : x * 512 + 256], total[:, x * 512 + 256 : x * 512 + 512]
        mine_ref[pl.ds(x, 1), :] = jnp.where(zh == 0, first, second)
        theirs_ref[pl.ds(x, 1), :] = jnp.where(zh == 0, second, first)


def run_behind_near(*args):
    return call(
        behind_near,
        (shape((TOK, D)), shape((8, 256), f32), shape((8, 256), f32)),
        [SMEM] + [VMEM] * 9,
        SUMMING,
        args,
        10**9,
        5,
    )


def behind_logits(
    zh_ref, near_note_ref, far_note_ref, near_probs_ref, far_probs_ref, near_normed_ref, far_normed_ref,
    logit_ref, parts_ref
):
    near_tok, far_tok = pl.ds(0, TOK), pl.ds(TOK, TOK)

    def logit_grads(probs, grads):
        return (probs * (grads - jnp.sum(probs * grads, axis=0, keepdims=True))).astype(bf16)

    near_logit = logit_grads(near_probs_ref[...], near_note_ref[:, near_tok] + far_note_ref[:, far_tok])
    far_logit = logit_grads(far_probs_ref[...], near_note_ref[:, far_tok] + far_note_ref[:, near_tok])
    logit_ref[...] = near_logit
    for x in range(4):
        cols = pl.ds(pl.multiple_of(x * 512 + (zh_ref[0] & 1) * 256, 256), 256)
        part = dot(near_logit, near_normed_ref[:, cols]) + dot(far_logit, far_normed_ref[:, cols])
        both = jnp.concatenate([part, jnp.zeros((128 - EXPERTS, 256), f32)], axis=0).T.astype(bf16)
        for peer in range(8):
            parts_ref[x * 8 + peer] = both[peer * 32 : peer * 32 + 32]


def run_behind_logits(*args):
    return call(
        behind_logits,
        (shape((EXPERTS, TOK)), shape((PEERS, PEERS, 128))),
        [SMEM] + [VMEM] * 6,
        [],
        args,
        10**9,
        2,
    )


def share_parts(parts_ref, mine_ref, theirs_ref, shares_ref):
    shares_ref[:, pl.ds(0, PEERS), :] = parts_ref[...]
    gains = mine_ref[...] + theirs_ref[...]
    for d in range(PEERS):
        tile = gains[d // 8 : d // 8 + 1, d % 8 // 4 * 128 : d % 8 // 4 * 128 + 128]
        shares_ref[d, pl.ds(PEERS, 8), :] = jnp.broadcast_to(tile, (8, 128)).astype(bf16)


def run_share_parts(*args):
    return call(share_parts, (shape((PEERS, PEERS + 8, 128)),), [VMEM] * 3, [], args, 10**8, 1)[0]


def ahead_far(home_ref, mix_ref, out_ref, wide_ref):
    for cols, sums in block_sums(home_ref, mix_ref, wide_ref):
        out_ref[:, cols] = sums.astype(bf16)


def ahead_near(home_ref, mix_ref, resid_ref, out_ref, wide_ref):
    for cols, sums in block_sums(home_ref, mix_ref, wide_ref):
        out_ref[:, cols] = (resid_ref[:, cols].astype(f32) + sums).astype(bf16)


def run_ahead_end(kernel, half, home, *rest):
    return pl.pallas_call(
        kernel,
        grid=(1,),
        out_shape=shape((TOK, D)),
        in_specs=[pl.BlockSpec((PEERS, ROWS, 256), lambda i: (0, half, 0))] + [whole(a) for a in rest],
        out_specs=pl.BlockSpec((TOK, D), lambda i: (0, 0)),
        scratch_shapes=[pltpu.VMEM((2, AREA, 128), f32)],
        compiler_params=pltpu.CompilerParams(vmem_limit_bytes=63 * 2**20),
        cost_estimate=pl.CostEstimate(flops=10**9, transcendentals=0, bytes_accessed=3 * 2**20),
    )(home, *rest)


def share_sums(place_ref, got_ref, router_ref, gain_ref):
    total = got_ref[0].astype(f32)
    for source in range(1, PEERS):
        total = total + got_ref[source].astype(f32)
    total = total * factor
    router_ref[...] = total[:PEERS, :EXPERTS]
    gain = total[PEERS : PEERS + 1, :32]
    for k in range(1, 4):
        gain = jnp.where((place_ref[0] >> 1) == k, total[PEERS : PEERS + 1, k * 32 : k * 32 + 32], gain)
    gain_ref[...] = gain


def run_share_sums(place, got):
    return call(
        share_sums,
        (shape((PEERS, EXPERTS), f32), shape((1, PEERS), f32)),
        [SMEM, VMEM],
        [],
        (place, got),
        10**6,
        1,
    )


def body(
    forward_input,
    queries,
    new_keys,
    new_values,
    cache_keys,
    cache_values,
    context_lengths,
    norm_gain,
    router,
    gate_weight,
    up_weight,
    down_weight,
    forward_ids,
    backward_input,
    backward_ids,
    output_grad,
):
    near_y, core = lax.axis_index("y") & 1, lax.axis_index("core")
    zh = (lax.axis_index("zh") + 4 * near_y + 2 * core).astype(jnp.int32).reshape(1)
    gain = norm_gain
    table = router[0].T
    weights = (gate_weight[0, 0], up_weight[0, 0], down_weight[0, 0])
    back_x, back_g = backward_input[0], output_grad[0]
    ids_b, ids_f = backward_ids[0].T, forward_ids[0].T
    ids_far = swapped(jnp.concatenate([ids_b, ids_f], axis=0))
    x_far = swapped(back_x)
    g_far = swapped(back_g)
    resid = run_attend(
        context_lengths,
        forward_input[0],
        queries[0],
        cache_keys[0],
        new_keys[0],
        cache_values[0],
        new_values[0],
    )
    resid_far = swapped(resid)
    sent_1, normed_b, hot_b, probs_b, mix_f = run_near_pack(
        zh, ids_b, ids_f, back_x, back_g, resid, gain, table
    )
    got_1 = spread_out(sent_1)
    sent_3, normed_c, hot_c, probs_c = run_far_pack(zh, ids_far[:4], x_far, g_far, gain, table)
    sent_2, mix_h = run_ahead_pack(zh, ids_far[4:], resid_far, gain, table)
    sent_2, _ = lax.optimization_barrier((sent_2, got_1))
    got_2 = spread_out(sent_2)
    sent_3, got_2 = lax.optimization_barrier((sent_3, got_2))
    got_3 = spread_out(sent_3)
    back_b, small_b = run_near_experts(got_1, *weights)
    made = run_ahead_experts(got_1, got_2, *weights)
    made, got_3 = lax.optimization_barrier((made, got_3))
    home_f = spread_out(made)
    back_c = run_far_experts(got_3, small_b, *weights)
    back_c, home_f = lax.optimization_barrier((back_c, home_f))
    home_c = spread_out(back_c)
    own_h = run_ahead_end(ahead_far, 1, home_f, mix_h)
    moved_h = moved(own_h, False, 1)
    own_f = run_ahead_end(ahead_near, 0, home_f, mix_f, resid)
    moved_f = moved(own_f, True, 1)
    back_b, home_c = lax.optimization_barrier((back_b, home_c))
    home_d = spread_out(back_b)
    note = run_behind_note(zh, home_c, hot_b, hot_c)
    far_note = swapped(note)
    own_c, gains_c = run_behind_far(zh, home_c, hot_c, probs_c, x_far, gain)
    moved_c = moved(own_c, False, -1)
    logit_b, parts = run_behind_logits(zh, note, far_note, probs_b, probs_c, normed_b, normed_c)
    own_b, mine, theirs = run_behind_near(
        zh, home_d, hot_b, probs_b, logit_b, gains_c, back_x, back_g, gain, table
    )
    theirs = swapped(theirs)
    moved_b = moved(own_b, True, -1)
    shares = run_share_parts(parts, mine, theirs)
    got_s = spread_out(shares)
    router_grad, gain_grad = run_share_sums(zh, got_s)
    forward_output = (moved_f.astype(f32) + moved_h.astype(f32)).astype(bf16)
    input_grad = (moved_b.astype(f32) + moved_c.astype(f32)).astype(bf16)
    return forward_output[None], input_grad[None], router_grad[None], gain_grad


def solution(mesh):
    grid = Mesh(mesh.devices.reshape(4, 4, 2, 4, 2), ("pipe", "x", "zh", "y", "core"))
    rows = P("pipe", ALL, None)
    placed = (
        rows,
        rows,
        rows,
        rows,
        rows,
        rows,
        P("pipe", ALL),
        P("pipe", None),
        P("pipe", None, None),
        P("pipe", ALL, None, None),
        P("pipe", ALL, None, None),
        P("pipe", ALL, None, None),
        rows,
        rows,
        rows,
        rows,
    )
    return jax.shard_map(
        body,
        mesh=grid,
        in_specs=placed,
        out_specs=(rows, rows, rows, P("pipe", ALL)),
        check_vma=False,
    )
```

```python
import jax
import jax.numpy as jnp
from jax import lax
from jax.experimental import pallas as pl
from jax.experimental.pallas import tpu as pltpu
from jax.sharding import Mesh, PartitionSpec as P


HEADS = 16
KV_HEADS = 2
HEAD_DIM = 128
D = 2048
FF = 768
EXPERTS = 64
MOST = 9
TOK = 128
PEERS = 32
SLOTS = PEERS * MOST
ROWS = MOST * 8
AREA = SLOTS * 8
XY = ("x", "y", "core")
ALL = ("x", "zh", "y", "core")

epsilon = 1e-06
far_below = -1e30
factor = 8192 ** (-0.5)
bf16 = jnp.bfloat16
f32 = jnp.float32
ACROSS = (((1,), (1,)), ((), ()))
DOWN = (((0,), (0,)), ((), ()))
VMEM = pl.BlockSpec(memory_space=pltpu.VMEM)
SMEM = pl.BlockSpec(memory_space=pltpu.SMEM)
HBM = pl.BlockSpec(memory_space=pltpu.HBM)


def spread_out(x):
    return lax.all_to_all(x, XY, 0, 0, tiled=True)


def swapped(x):
    return lax.ppermute(x, "zh", [(0, 1), (1, 0)])


def moved(x, same, step):
    pairs = []
    for pipe in range(4):
        for zh in range(2):
            to = ((pipe + step) % 4) * 2 + (zh if same else 1 - zh)
            pairs.append((pipe * 2 + zh, to))
    return lax.ppermute(x, ("pipe", "zh"), pairs)


def shape(dims, dtype=bf16):
    return jax.ShapeDtypeStruct(dims, dtype)


def call(kernel, outs, ins, scratch, args, flops, mib):
    return pl.pallas_call(
        kernel,
        out_shape=outs,
        in_specs=ins,
        out_specs=tuple(VMEM for _ in outs),
        scratch_shapes=scratch,
        compiler_params=pltpu.CompilerParams(vmem_limit_bytes=63 * 2**20),
        cost_estimate=pl.CostEstimate(
            flops=flops, transcendentals=0, bytes_accessed=mib * 2**20
        ),
    )(*args)


def dot(a, b, dims=None):
    if dims is None:
        return jnp.dot(a, b, preferred_element_type=f32)
    return lax.dot_general(a, b, dims, preferred_element_type=f32)


def iota(dims, dim):
    return lax.broadcasted_iota(jnp.int32, dims, dim)


def marks(cond):
    return cond.astype(f32).astype(bf16)


def unit_rows(x):
    wide = x.astype(f32)
    inv_rms = lax.rsqrt(jnp.mean(wide * wide, axis=-1, keepdims=True) + epsilon)
    return inv_rms, wide * inv_rms


def hits(ids):
    expert = iota((EXPERTS, ids.shape[1]), 0)
    hit = ids[0:1, :] == expert
    for k in range(1, 4):
        hit = hit | (ids[k : k + 1, :] == expert)
    return hit


def choice(normed, table, hit):
    logits = jnp.where(hit, dot(table, normed, ACROSS), far_below)
    lifted = jnp.where(hit, jnp.exp(logits - jnp.max(logits, axis=0, keepdims=True)), 0.0)
    return lifted / jnp.sum(lifted, axis=0, keepdims=True)


def ranked(hit):
    tokens = hit.shape[1]
    earlier, later = iota((tokens, tokens), 0), iota((tokens, tokens), 1)
    before = marks((earlier < later) & (earlier // TOK == later // TOK))
    hit = hit.astype(f32)
    return (hit * (dot(hit.astype(bf16), before) + 1.0)).astype(bf16)


def picks(peer, zh):
    owner = (peer // 8) * 16 + zh * 8 + peer % 8
    return marks(owner == iota(peer.shape, 1))


def each_peer(step):
    def turn(d, carry):
        step(d, pl.ds(pl.multiple_of(d * ROWS, 8), ROWS))
        return carry

    lax.fori_loop(0, PEERS, turn, 0)


def area_rows(d, area):
    return pl.ds(pl.multiple_of(d * ROWS + area * AREA, 8), ROWS)


LANES = (pl.ds(0, 128), pl.ds(128, 128))


def put_rows(wide_ref, j, rows, start=0):
    for lane in range(rows.shape[1] // 128):
        wide_ref[lane, pl.ds(start + j, rows.shape[0], stride=8), :] = rows[
            :, lane * 128 : lane * 128 + 128
        ]


def get_rows(wide_ref, j, count, start=0):
    return jnp.concatenate(
        [
            wide_ref[lane, pl.ds(start + j, count, stride=8), :].astype(bf16)
            for lane in range(wide_ref.shape[0])
        ],
        axis=1,
    )


def routed(ids, x, zh, gain, table):
    hit = hits(ids)
    _, unit = unit_rows(x)
    normed = (unit * gain).astype(bf16)
    probs = choice(normed, table, hit)
    pick = picks(iota((SLOTS, EXPERTS), 0) // MOST, zh)
    slot = (iota((SLOTS, TOK), 0) % MOST + 1).astype(f32)
    return normed, probs, pick, marks(dot(pick, ranked(hit)) == slot)


def mixed_by(onehot, pick, probs):
    return onehot * dot(pick, probs.astype(bf16)).astype(bf16)


def loop(count, step):
    def turn(i, carry):
        step(i)
        return carry

    lax.fori_loop(0, count, turn, 0)


def columns(j, width):
    return pl.ds(pl.multiple_of(j * width, width), width)


def fill_looped(wide_ref, area, onehot_ref, rows_ref):
    def step(j):
        put_rows(wide_ref, j, dot(onehot_ref[...], rows_ref[:, columns(j, 256)]), area * AREA)

    loop(8, step)


def fill(wide_ref, area, onehot, rows_ref):
    for j in range(8):
        put_rows(wide_ref, j, dot(onehot, rows_ref[:, pl.ds(j * 256, 256)]), area * AREA)


def give(wide_ref, sent_ref, areas):
    def step(d, rows):
        for area in range(areas):
            for lane in range(2):
                sent_ref[d, pl.ds(area * ROWS, ROWS), LANES[lane]] = wide_ref[lane, area_rows(d, area), :].astype(bf16)

    each_peer(step)


def near_pack(
    zh_ref, ids_ref, ahead_ids_ref, x_ref, g_ref, resid_ref, gain_ref, table_ref,
    sent_ref, normed_ref, onehot_ref, probs_ref, mix_ref, wide_ref, rows_ref
):
    zh, gain, table = zh_ref[0], gain_ref[...], table_ref[...]
    normed_ref[...], probs_ref[...], _, onehot_ref[...] = routed(ids_ref[...], x_ref[...], zh, gain, table)
    fill(wide_ref, 0, onehot_ref[...], normed_ref)
    fill(wide_ref, 1, onehot_ref[...], g_ref)
    rows_ref[...], probs, pick, onehot = routed(ahead_ids_ref[...], resid_ref[...], zh, gain, table)
    mix_ref[...] = mixed_by(onehot, pick, probs)
    fill(wide_ref, 2, onehot, rows_ref)
    give(wide_ref, sent_ref, 3)


def run_near_pack(*args):
    return call(
        near_pack,
        (
            shape((PEERS, 3 * ROWS, 256)),
            shape((TOK, D)),
            shape((SLOTS, TOK)),
            shape((EXPERTS, TOK), f32),
            shape((SLOTS, TOK)),
        ),
        [SMEM] + [VMEM] * 7,
        [pltpu.VMEM((2, 3 * AREA, 128), f32), pltpu.VMEM((TOK, D), bf16)],
        args,
        2 * 10**9,
        8,
    )


def far_pack(
    zh_ref, ids_ref, x_ref, g_ref, gain_ref, table_ref, sent_ref, normed_ref, onehot_ref, probs_ref, wide_ref
):
    normed_ref[...], probs_ref[...], _, onehot_ref[...] = routed(
        ids_ref[...], x_ref[...], zh_ref[0], gain_ref[...], table_ref[...]
    )
    fill(wide_ref, 0, onehot_ref[...], normed_ref)
    fill(wide_ref, 1, onehot_ref[...], g_ref)
    give(wide_ref, sent_ref, 2)


def run_far_pack(*args):
    return call(
        far_pack,
        (shape((PEERS, 2 * ROWS, 256)), shape((TOK, D)), shape((SLOTS, TOK)), shape((EXPERTS, TOK), f32)),
        [SMEM] + [VMEM] * 5,
        [pltpu.VMEM((2, 2 * AREA, 128), f32)],
        args,
        10**9,
        6,
    )


def ahead_pack(zh_ref, ids_ref, x_ref, gain_ref, table_ref, sent_ref, mix_ref, wide_ref, rows_ref, onehot_ref):
    rows_ref[...], probs, pick, onehot = routed(ids_ref[...], x_ref[...], zh_ref[0], gain_ref[...], table_ref[...])
    mix_ref[...] = mixed_by(onehot, pick, probs)
    onehot_ref[...] = onehot
    fill_looped(wide_ref, 0, onehot_ref, rows_ref)
    give(wide_ref, sent_ref, 1)


def run_ahead_pack(*args):
    return call(
        ahead_pack,
        (shape((PEERS, ROWS, 256)), shape((SLOTS, TOK))),
        [SMEM] + [VMEM] * 4,
        [pltpu.VMEM((2, AREA, 128), f32), pltpu.VMEM((TOK, D), bf16), pltpu.VMEM((SLOTS, TOK), bf16)],
        args,
        10**9,
        4,
    )


def fetched(pairs, sems):
    copies = [pltpu.make_async_copy(a, b, sems.at[i]) for i, (a, b) in enumerate(pairs)]
    for copy in copies:
        copy.start()
    return copies


def expert_slopes(gate_pre, up_pre, down_grad, gate_grad, up_grad):
    sig = 1.0 / (1.0 + jnp.exp(-gate_pre))
    act = gate_pre * sig
    hidden = (act * up_pre).astype(bf16).astype(f32)
    gate_grad[...] = (down_grad * up_pre * sig * (1.0 + gate_pre * (1.0 - sig))).astype(bf16)
    up_grad[...] = (down_grad * act).astype(bf16)
    return jnp.sum(hidden * down_grad, axis=-1, keepdims=True).astype(bf16).astype(f32)


def small_grads(grads, place):
    p, lane = iota((SLOTS, 128), 0), iota((SLOTS, 128), 1)
    gather = marks(iota((PEERS * 8, SLOTS), 1) // MOST == iota((PEERS * 8, SLOTS), 0) // 8)
    spread = jnp.where(lane == p % MOST + place * MOST, grads, 0.0)
    return dot(gather, spread.astype(bf16))


def behind_half(got_ref, weights, place, wide_ref, sems, gate_grad, up_grad):
    (gate_hbm, gate_ref), (up_hbm, up_ref), (down_hbm, down_ref) = weights
    copies = fetched(weights, sems)

    def take(d, rows):
        for lane in range(2):
            for kind in range(2):
                wide_ref[lane, area_rows(d, kind), :] = got_ref[d, pl.ds(kind * ROWS, ROWS), LANES[lane]].astype(f32)

    each_peer(take)
    copies[0].wait()
    copies[1].wait()
    gate_pre, up_pre = jnp.zeros((SLOTS, FF), f32), jnp.zeros((SLOTS, FF), f32)
    for j in range(4):
        rows = jnp.concatenate([get_rows(wide_ref, 2 * j + i, SLOTS) for i in range(2)], axis=1)
        gate_pre = gate_pre + dot(rows, gate_ref[pl.ds(j * 512, 512), :])
        up_pre = up_pre + dot(rows, up_ref[pl.ds(j * 512, 512), :])
    copies[2].wait()
    down_grad = jnp.zeros((SLOTS, FF), f32)
    for j in range(4):
        rows = jnp.concatenate([get_rows(wide_ref, 2 * j + i, SLOTS, AREA) for i in range(2)], axis=1)
        down_grad = down_grad + dot(rows, down_ref[:, pl.ds(j * 512, 512)], ACROSS)
    grads = expert_slopes(gate_pre, up_pre, down_grad, gate_grad, up_grad)
    for j in range(8):
        part = pl.ds(j * 256, 256)
        rows = dot(gate_grad[...], gate_ref[part, :], ACROSS) + dot(up_grad[...], up_ref[part, :], ACROSS)
        put_rows(wide_ref, j, rows)
    return small_grads(grads, place)


def near_experts(
    got_ref, gate_hbm, up_hbm, down_hbm, back_ref, small_ref, wide_ref, gate_ref, up_ref, down_ref, sems,
    gate_sum, up_sum, down_sum, gate_grad, up_grad
):
    copies = fetched(((gate_hbm, gate_ref), (up_hbm, up_ref), (down_hbm, down_ref)), sems)

    def take(d, rows):
        for lane in range(2):
            for kind in range(2):
                wide_ref[lane, area_rows(d, kind), :] = got_ref[d, pl.ds(kind * ROWS, ROWS), LANES[lane]].astype(f32)

    each_peer(take)
    for ref in (gate_sum, up_sum, down_sum):
        ref[...] = jnp.zeros((SLOTS, FF), f32)
    for copy in copies:
        copy.wait()

    def inward(j):
        rows = jnp.concatenate([get_rows(wide_ref, 2 * j + i, SLOTS) for i in range(2)], axis=1)
        gate_sum[...] += dot(rows, gate_ref[columns(j, 512), :])
        up_sum[...] += dot(rows, up_ref[columns(j, 512), :])
        rows = jnp.concatenate([get_rows(wide_ref, 2 * j + i, SLOTS, AREA) for i in range(2)], axis=1)
        down_sum[...] += dot(rows, down_ref[:, columns(j, 512)], ACROSS)

    loop(4, inward)
    grads = expert_slopes(gate_sum[...], up_sum[...], down_sum[...], gate_grad, up_grad)

    def outward(j):
        part = columns(j, 256)
        rows = dot(gate_grad[...], gate_ref[part, :], ACROSS) + dot(up_grad[...], up_ref[part, :], ACROSS)
        put_rows(wide_ref, j, rows)

    loop(8, outward)
    small_ref[...] = small_grads(grads, 0)

    def put(d, rows):
        for lane in range(2):
            back_ref[d, :, LANES[lane]] = wide_ref[lane, rows, :].astype(bf16)

    each_peer(put)


def far_experts(
    got_ref, near_ref, near_small_ref, gate_hbm, up_hbm, down_hbm, back_ref, wide_ref, gate_ref, up_ref, down_ref, sems,
    gate_grad, up_grad
):
    weights = ((gate_hbm, gate_ref), (up_hbm, up_ref), (down_hbm, down_ref))
    small = behind_half(got_ref, weights, 1, wide_ref, sems, gate_grad, up_grad) + near_small_ref[...]
    wide_ref[0, pl.ds(AREA, PEERS * 8), :] = small

    def put(d, rows):
        for lane in range(2):
            back_ref[d, pl.ds(0, ROWS), LANES[lane]] = near_ref[d, :, LANES[lane]]
            back_ref[d, pl.ds(ROWS, ROWS), LANES[lane]] = wide_ref[lane, rows, :].astype(bf16)
        extra = wide_ref[0, pl.ds(pl.multiple_of(AREA + d * 8, 8), 8), :].astype(bf16)
        back_ref[d, pl.ds(2 * ROWS, 8), LANES[0]] = extra
        back_ref[d, pl.ds(2 * ROWS, 8), LANES[1]] = extra

    each_peer(put)


GRADS = [pltpu.VMEM((SLOTS, FF), bf16)] * 2
WEIGHTS = [
    pltpu.VMEM((D, FF), bf16),
    pltpu.VMEM((D, FF), bf16),
    pltpu.VMEM((FF, D), bf16),
    pltpu.SemaphoreType.DMA((3,)),
]


def run_near_experts(*args):
    return call(
        near_experts,
        (shape((PEERS, ROWS, 256)), shape((PEERS * 8, 128), f32)),
        [VMEM] + [HBM] * 3,
        [pltpu.VMEM((2, 2 * AREA, 128), f32)] + WEIGHTS + [pltpu.VMEM((SLOTS, FF), f32)] * 3 + GRADS,
        args,
        5 * 10**9,
        13,
    )


def run_far_experts(*args):
    return call(
        far_experts,
        (shape((PEERS, 2 * ROWS + 8, 256)),),
        [VMEM] * 3 + [HBM] * 3,
        [pltpu.VMEM((2, 2 * AREA, 128), f32)] + WEIGHTS + GRADS,
        args,
        5 * 10**9,
        15,
    )[0]


def ahead_experts(
    near_ref, far_ref, gate_hbm, up_hbm, down_hbm, made_ref, wide_ref, gate_ref, up_ref, down_ref, sems,
    gate_sum, up_sum, hidden_ref
):
    copies = fetched(((gate_hbm, gate_ref), (up_hbm, up_ref), (down_hbm, down_ref)), sems)
    count = 2 * SLOTS

    def take(d, rows):
        for lane in range(2):
            wide_ref[lane, area_rows(d, 0), :] = near_ref[d, pl.ds(2 * ROWS, ROWS), LANES[lane]].astype(f32)
            wide_ref[lane, area_rows(d, 1), :] = far_ref[d, :, LANES[lane]].astype(f32)

    each_peer(take)
    copies[0].wait()
    copies[1].wait()
    gate_sum[...] = jnp.zeros((count, FF), f32)
    up_sum[...] = jnp.zeros((count, FF), f32)

    def inward(j):
        rows = jnp.concatenate([get_rows(wide_ref, 2 * j, count), get_rows(wide_ref, 2 * j + 1, count)], axis=1)
        gate_sum[...] += dot(rows, gate_ref[columns(j, 512), :])
        up_sum[...] += dot(rows, up_ref[columns(j, 512), :])

    loop(4, inward)
    gate_pre = gate_sum[...]
    hidden_ref[...] = (gate_pre / (1.0 + jnp.exp(-gate_pre)) * up_sum[...]).astype(bf16)
    copies[2].wait()

    def outward(j):
        put_rows(wide_ref, j, dot(hidden_ref[...], down_ref[:, columns(j, 256)]))

    loop(8, outward)

    def put(d, rows):
        for lane in range(2):
            for half in range(2):
                made_ref[d, pl.ds(half * ROWS, ROWS), LANES[lane]] = wide_ref[lane, area_rows(d, half), :].astype(bf16)

    each_peer(put)


def run_ahead_experts(*args):
    return call(
        ahead_experts,
        (shape((PEERS, 2 * ROWS, 256)),),
        [VMEM] * 2 + [HBM] * 3,
        [pltpu.VMEM((2, 2 * AREA, 128), f32)]
        + WEIGHTS
        + [pltpu.VMEM((2 * SLOTS, FF), f32), pltpu.VMEM((2 * SLOTS, FF), f32), pltpu.VMEM((2 * SLOTS, FF), bf16)],
        args,
        6 * 10**9,
        14,
    )[0]


def attend(length_ref, x_ref, q_ref, kc_ref, kn_ref, vc_ref, vn_ref, resid_ref):
    length = length_ref[0, 0]
    row, col = iota((TOK, 2 * TOK), 0), iota((TOK, 2 * TOK), 1)
    visible = ((col < TOK) & (col < length)) | ((col >= TOK) & (col - TOK <= row))
    for kv in range(KV_HEADS):
        part = pl.ds(kv * HEAD_DIM, HEAD_DIM)
        keys = jnp.concatenate([kc_ref[:, part], kn_ref[:, part]], axis=0)
        values = jnp.concatenate([vc_ref[:, part], vn_ref[:, part]], axis=0)
        for h in range(HEADS // KV_HEADS):
            cols = pl.ds((kv * (HEADS // KV_HEADS) + h) * HEAD_DIM, HEAD_DIM)
            scores = dot(q_ref[:, cols], keys, ACROSS) * HEAD_DIM ** (-0.5)
            scores = jnp.where(visible, scores, far_below)
            lifted = jnp.exp(scores - jnp.max(scores, axis=-1, keepdims=True))
            weights = (lifted * (1.0 / jnp.sum(lifted, axis=-1, keepdims=True))).astype(bf16)
            mixed = dot(weights, values).astype(bf16)
            resid_ref[:, cols] = (x_ref[:, cols].astype(f32) + mixed.astype(f32)).astype(bf16)


def run_attend(length, x, q, kc, kn, vc, vn):
    return call(
        attend,
        (shape((TOK, D)),),
        [SMEM] + [VMEM] * 6,
        [],
        (length, x, q, kc, kn, vc, vn),
        3 * 10**9,
        8,
    )[0]


def through_norm(sums, gain, inv, unit):
    scaled = sums * gain
    return inv * (scaled - unit * jnp.mean(scaled * unit, axis=-1, keepdims=True))


def behind_note(zh_ref, home_ref, near_hot_ref, far_hot_ref, note_ref):
    pick = picks(iota((SLOTS, EXPERTS), 0) // MOST, zh_ref[0]).astype(f32)
    small = jnp.concatenate([home_ref[d].astype(f32) for d in range(PEERS)], axis=0)[:, :128].astype(bf16)
    share = marks(iota((SLOTS, PEERS * 8), 0) // MOST * 8 == iota((SLOTS, PEERS * 8), 1))
    small = dot(share, small)
    p, lane = iota((SLOTS, 128), 0) % MOST, iota((SLOTS, 128), 1)
    for half, hot in enumerate((near_hot_ref, far_hot_ref)):
        grads = jnp.sum(jnp.where(lane == p + half * MOST, small, 0.0), axis=-1, keepdims=True)
        note_ref[:, pl.ds(half * TOK, TOK)] = dot((pick * grads).astype(bf16), hot[...], DOWN)


def whole(a):
    return pl.BlockSpec(a.shape, lambda i, n=a.ndim: (0,) * n)


def run_behind_note(zh, home, near_hot, far_hot):
    tail = pl.BlockSpec((PEERS, 8, 256), lambda i: (0, 2 * ROWS // 8, 0))
    return pl.pallas_call(
        behind_note,
        grid=(1,),
        out_shape=shape((EXPERTS, 2 * TOK), f32),
        in_specs=[SMEM, tail, whole(near_hot), whole(far_hot)],
        out_specs=pl.BlockSpec((EXPERTS, 2 * TOK), lambda i: (0, 0)),
        compiler_params=pltpu.CompilerParams(vmem_limit_bytes=63 * 2**20),
        cost_estimate=pl.CostEstimate(flops=10**7, transcendentals=0, bytes_accessed=2**18),
    )(zh, home, near_hot, far_hot)


def behind_sums(
    zh_ref, home_ref, near_hot_ref, far_hot_ref, near_probs_ref, far_probs_ref, near_x_ref, far_x_ref, gain_ref,
    sums_ref, sent_ref, theirs_ref, mine_ref, wide_ref, line_ref, mix_ref
):
    zh = zh_ref[0]

    def take(d, rows):
        for half in range(2):
            for lane in range(2):
                wide_ref[lane, area_rows(d, half), :] = home_ref[d, pl.ds(half * ROWS, ROWS), LANES[lane]].astype(f32)

    each_peer(take)
    pick = picks(iota((SLOTS, EXPERTS), 0) // MOST, zh)
    mix_ref[0] = mixed_by(near_hot_ref[...], pick, near_probs_ref[...])
    mix_ref[1] = mixed_by(far_hot_ref[...], pick, far_probs_ref[...])

    for j in range(8):
        cols = pl.ds(j * 256, 256)
        sums_ref[:, cols] = dot(mix_ref[0], get_rows(wide_ref, j, SLOTS), DOWN)
        line_ref[:, cols] = dot(mix_ref[1], get_rows(wide_ref, j, SLOTS, AREA), DOWN)
    inv, unit = unit_rows(far_x_ref[...])
    sums = line_ref[...]
    sent_ref[...] = through_norm(sums, gain_ref[...], inv, unit).astype(bf16)
    total = jnp.sum(sums * unit, axis=0, keepdims=True)
    _, unit = unit_rows(near_x_ref[...])
    total = total + jnp.sum(sums_ref[...] * unit, axis=0, keepdims=True)
    theirs_ref[...] = jnp.zeros((8, 256), f32)
    mine_ref[...] = jnp.zeros((8, 256), f32)
    for x in range(4):
        first, second = total[:, x * 512 : x * 512 + 256], total[:, x * 512 + 256 : x * 512 + 512]
        mine_ref[pl.ds(x, 1), :] = jnp.where(zh == 0, first, second)
        theirs_ref[pl.ds(x, 1), :] = jnp.where(zh == 0, second, first)


def run_behind_sums(*args):
    return call(
        behind_sums,
        (shape((TOK, D), f32), shape((TOK, D)), shape((8, 256), f32), shape((8, 256), f32)),
        [SMEM] + [VMEM] * 8,
        [
            pltpu.VMEM((2, 2 * AREA, 128), f32),
            pltpu.VMEM((TOK, D), f32),
            pltpu.VMEM((2, SLOTS, TOK), bf16),
        ],
        args,
        10**9,
        6,
    )


def behind_end(
    near_note_ref, far_note_ref, sums_ref, near_probs_ref, far_probs_ref, x_ref, g_ref, gain_ref, table_ref,
    sent_ref, near_logit_ref, far_logit_ref
):
    near_tok, far_tok = pl.ds(0, TOK), pl.ds(TOK, TOK)

    def logit_grads(probs, grads):
        return (probs * (grads - jnp.sum(probs * grads, axis=0, keepdims=True))).astype(bf16)

    near_logit_ref[...] = logit_grads(near_probs_ref[...], near_note_ref[:, near_tok] + far_note_ref[:, far_tok])
    far_logit_ref[...] = logit_grads(far_probs_ref[...], near_note_ref[:, far_tok] + far_note_ref[:, near_tok])
    inv, unit = unit_rows(x_ref[...])
    sums = sums_ref[...] + dot(near_logit_ref[...], table_ref[...], DOWN)
    sent_ref[...] = (g_ref[...].astype(f32) + through_norm(sums, gain_ref[...], inv, unit)).astype(bf16)


def run_behind_end(*args):
    return call(
        behind_end,
        (shape((TOK, D)), shape((EXPERTS, TOK)), shape((EXPERTS, TOK))),
        [VMEM] * 9,
        [],
        args,
        10**9,
        4,
    )


def share_parts(
    zh_ref, near_logit_ref, far_logit_ref, mine_ref, theirs_ref, near_normed_ref, far_normed_ref, near_x_ref,
    far_x_ref, table_ref, shares_ref
):
    zh = zh_ref[0]
    near_logit, far_logit = near_logit_ref[...], far_logit_ref[...]
    _, near_unit = unit_rows(near_x_ref[...])
    _, far_unit = unit_rows(far_x_ref[...])
    near_term, far_term = dot(near_logit, table_ref[...], DOWN), dot(far_logit, table_ref[...], DOWN)
    total = jnp.sum(near_term * near_unit + far_term * far_unit, axis=0, keepdims=True)
    row = iota((128 - EXPERTS, 256), 0)
    for x in range(4):
        first, second = total[:, x * 512 : x * 512 + 256], total[:, x * 512 + 256 : x * 512 + 512]
        gains = jnp.where(zh == 0, first, second) + mine_ref[pl.ds(x, 1), :] + theirs_ref[pl.ds(x, 1), :]
        cols = pl.ds(pl.multiple_of(x * 512 + zh * 256, 256), 256)
        part = dot(near_logit, near_normed_ref[:, cols]) + dot(far_logit, far_normed_ref[:, cols])
        both = jnp.concatenate([part, jnp.where(row == 0, gains, 0.0)], axis=0)
        shares_ref[pl.ds(x * 256, 256), :] = both.T.astype(bf16)


def run_share_parts(*args):
    return call(share_parts, (shape((D // 2, 128)),), [SMEM] + [VMEM] * 9, [], args, 10**9, 3)[0]


def ahead_sums(home_ref, mix_ref, wide_ref):
    def take(d, rows):
        for lane in range(2):
            wide_ref[lane, rows, :] = home_ref[d, :, LANES[lane]].astype(f32)

    each_peer(take)
    for j in range(8):
        yield pl.ds(j * 256, 256), dot(mix_ref[...], get_rows(wide_ref, j, SLOTS), DOWN)


def ahead_far(home_ref, mix_ref, out_ref, wide_ref):
    for cols, sums in ahead_sums(home_ref, mix_ref, wide_ref):
        out_ref[:, cols] = sums.astype(bf16)


def ahead_near(home_ref, mix_ref, resid_ref, out_ref, wide_ref):
    for cols, sums in ahead_sums(home_ref, mix_ref, wide_ref):
        out_ref[:, cols] = (resid_ref[:, cols].astype(f32) + sums).astype(bf16)


def run_ahead_end(kernel, half, home, *rest):
    return pl.pallas_call(
        kernel,
        grid=(1,),
        out_shape=shape((TOK, D)),
        in_specs=[pl.BlockSpec((PEERS, ROWS, 256), lambda i: (0, half, 0))] + [whole(a) for a in rest],
        out_specs=pl.BlockSpec((TOK, D), lambda i: (0, 0)),
        scratch_shapes=[pltpu.VMEM((2, AREA, 128), f32)],
        compiler_params=pltpu.CompilerParams(vmem_limit_bytes=63 * 2**20),
        cost_estimate=pl.CostEstimate(flops=10**9, transcendentals=0, bytes_accessed=3 * 2**20),
    )(home, *rest)


def share_sums(got_ref, router_ref, gain_ref):
    total = got_ref[0].astype(f32)
    for source in range(1, PEERS):
        total = total + got_ref[source].astype(f32)
    total = total * factor
    router_ref[...] = total[:, :EXPERTS]
    gain_ref[...] = total.T[EXPERTS : EXPERTS + 1, :]


def run_share_sums(got):
    return call(
        share_sums, (shape((PEERS, EXPERTS), f32), shape((1, PEERS), f32)), [VMEM], [], (got,), 10**6, 1
    )


def body(
    forward_input,
    queries,
    new_keys,
    new_values,
    cache_keys,
    cache_values,
    context_lengths,
    norm_gain,
    router,
    gate_weight,
    up_weight,
    down_weight,
    forward_ids,
    backward_input,
    backward_ids,
    output_grad,
):
    zh = lax.axis_index("zh").astype(jnp.int32).reshape(1)
    gain = norm_gain
    table = router[0].T
    weights = (gate_weight[0, 0], up_weight[0, 0], down_weight[0, 0])
    back_x, back_g = backward_input[0], output_grad[0]
    ids_b, ids_f = backward_ids[0].T, forward_ids[0].T
    ids_far = swapped(jnp.concatenate([ids_b, ids_f], axis=0))
    x_far = swapped(back_x)
    g_far = swapped(back_g)
    resid = run_attend(
        context_lengths,
        forward_input[0],
        queries[0],
        cache_keys[0],
        new_keys[0],
        cache_values[0],
        new_values[0],
    )
    resid_far = swapped(resid)
    sent_1, normed_b, hot_b, probs_b, mix_f = run_near_pack(
        zh, ids_b, ids_f, back_x, back_g, resid, gain, table
    )
    got_1 = spread_out(sent_1)
    sent_2, normed_c, hot_c, probs_c = run_far_pack(zh, ids_far[:4], x_far, g_far, gain, table)
    sent_2, _ = lax.optimization_barrier((sent_2, got_1))
    got_2 = spread_out(sent_2)
    sent_3, mix_h = run_ahead_pack(zh, ids_far[4:], resid_far, gain, table)
    sent_3, got_2 = lax.optimization_barrier((sent_3, got_2))
    got_3 = spread_out(sent_3)
    back_b, small_b = run_near_experts(got_1, *weights)
    back = run_far_experts(got_2, back_b, small_b, *weights)
    back, got_3 = lax.optimization_barrier((back, got_3))
    home_b = spread_out(back)
    made = run_ahead_experts(got_1, got_3, *weights)
    made, home_b = lax.optimization_barrier((made, home_b))
    home_f = spread_out(made)
    note = run_behind_note(zh, home_b, hot_b, hot_c)
    far_note = swapped(note)
    sums_b, own_c, theirs, mine = run_behind_sums(
        zh, home_b, hot_b, hot_c, probs_b, probs_c, back_x, x_far, gain
    )
    moved_c = moved(own_c, False, -1)
    own_b, logit_b, logit_c = run_behind_end(
        note, far_note, sums_b, probs_b, probs_c, back_x, back_g, gain, table
    )
    moved_b = moved(own_b, True, -1)
    own_h = run_ahead_end(ahead_far, 1, home_f, mix_h)
    moved_h = moved(own_h, False, 1)
    theirs = swapped(theirs)
    shares = run_share_parts(
        zh, logit_b, logit_c, mine, theirs, normed_b, normed_c, back_x, x_far, table
    )
    own_f = run_ahead_end(ahead_near, 0, home_f, mix_f, resid)
    moved_f = moved(own_f, True, 1)
    shares, own_f = lax.optimization_barrier((shares, own_f))
    got_s = spread_out(shares.reshape(PEERS, PEERS, 128))
    router_grad, gain_grad = run_share_sums(got_s)
    input_grad = (moved_b.astype(f32) + moved_c.astype(f32)).astype(bf16)
    forward_output = (moved_f.astype(f32) + moved_h.astype(f32)).astype(bf16)
    return forward_output[None], input_grad[None], router_grad[None], gain_grad


def solution(mesh):
    grid = Mesh(mesh.devices.reshape(4, 4, 2, 4, 2), ("pipe", "x", "zh", "y", "core"))
    rows = P("pipe", ALL, None)
    placed = (
        rows,
        rows,
        rows,
        rows,
        rows,
        rows,
        P("pipe", ALL),
        P("pipe", None),
        P("pipe", None, None),
        P("pipe", ALL, None, None),
        P("pipe", ALL, None, None),
        P("pipe", ALL, None, None),
        rows,
        rows,
        rows,
        rows,
    )
    return jax.shard_map(
        body,
        mesh=grid,
        in_specs=placed,
        out_specs=(rows, rows, rows, P("pipe", ALL)),
        check_vma=False,
    )
```

```python
import jax
import jax.numpy as jnp
from jax import lax
from jax.experimental import pallas as pl
from jax.experimental.pallas import tpu as pltpu
from jax.sharding import Mesh, PartitionSpec as P


HEADS = 16
KV_HEADS = 2
HEAD_DIM = 128
D = 2048
FF = 768
EXPERTS = 64
MOST = 9
TOK = 128
PEERS = 32
SLOTS = PEERS * MOST
ROWS = MOST * 8
AREA = SLOTS * 8
XY = ("x", "y", "core")
ALL = ("x", "zh", "y", "core")

epsilon = 1e-06
far_below = -1e30
factor = 8192 ** (-0.5)
bf16 = jnp.bfloat16
f32 = jnp.float32
ACROSS = (((1,), (1,)), ((), ()))
DOWN = (((0,), (0,)), ((), ()))
VMEM = pl.BlockSpec(memory_space=pltpu.VMEM)
SMEM = pl.BlockSpec(memory_space=pltpu.SMEM)
HBM = pl.BlockSpec(memory_space=pltpu.HBM)


def spread_out(x):
    return lax.all_to_all(x, XY, 0, 0, tiled=True)


def swapped(x):
    return lax.ppermute(x, "zh", [(0, 1), (1, 0)])


def moved(x, same, step):
    pairs = []
    for pipe in range(4):
        for zh in range(2):
            to = ((pipe + step) % 4) * 2 + (zh if same else 1 - zh)
            pairs.append((pipe * 2 + zh, to))
    return lax.ppermute(x, ("pipe", "zh"), pairs)


def shape(dims, dtype=bf16):
    return jax.ShapeDtypeStruct(dims, dtype)


def call(kernel, outs, ins, scratch, args, flops, mib):
    return pl.pallas_call(
        kernel,
        out_shape=outs,
        in_specs=ins,
        out_specs=tuple(VMEM for _ in outs),
        scratch_shapes=scratch,
        compiler_params=pltpu.CompilerParams(vmem_limit_bytes=63 * 2**20),
        cost_estimate=pl.CostEstimate(
            flops=flops, transcendentals=0, bytes_accessed=mib * 2**20
        ),
    )(*args)


def dot(a, b, dims=None):
    if dims is None:
        return jnp.dot(a, b, preferred_element_type=f32)
    return lax.dot_general(a, b, dims, preferred_element_type=f32)


def iota(dims, dim):
    return lax.broadcasted_iota(jnp.int32, dims, dim)


def marks(cond):
    return cond.astype(f32).astype(bf16)


def unit_rows(x):
    wide = x.astype(f32)
    inv_rms = lax.rsqrt(jnp.mean(wide * wide, axis=-1, keepdims=True) + epsilon)
    return inv_rms, wide * inv_rms


def hits(ids):
    expert = iota((EXPERTS, ids.shape[1]), 0)
    hit = ids[0:1, :] == expert
    for k in range(1, 4):
        hit = hit | (ids[k : k + 1, :] == expert)
    return hit


def choice(normed, table, hit):
    logits = jnp.where(hit, dot(table, normed, ACROSS), far_below)
    lifted = jnp.where(hit, jnp.exp(logits - jnp.max(logits, axis=0, keepdims=True)), 0.0)
    return lifted / jnp.sum(lifted, axis=0, keepdims=True)


def ranked(hit):
    tokens = hit.shape[1]
    earlier, later = iota((tokens, tokens), 0), iota((tokens, tokens), 1)
    before = marks((earlier < later) & (earlier // TOK == later // TOK))
    hit = hit.astype(f32)
    return (hit * (dot(hit.astype(bf16), before) + 1.0)).astype(bf16)


def picks(peer, zh):
    owner = (peer // 8) * 16 + zh * 8 + peer % 8
    return marks(owner == iota(peer.shape, 1))


def each_peer(step):
    def turn(d, carry):
        step(d, pl.ds(pl.multiple_of(d * ROWS, 8), ROWS))
        return carry

    lax.fori_loop(0, PEERS, turn, 0)


def area_rows(d, area):
    return pl.ds(pl.multiple_of(d * ROWS + area * AREA, 8), ROWS)


LANES = (pl.ds(0, 128), pl.ds(128, 128))


def put_rows(wide_ref, j, rows, start=0):
    for lane in range(rows.shape[1] // 128):
        wide_ref[lane, pl.ds(start + j, rows.shape[0], stride=8), :] = rows[
            :, lane * 128 : lane * 128 + 128
        ]


def get_rows(wide_ref, j, count, start=0):
    return jnp.concatenate(
        [
            wide_ref[lane, pl.ds(start + j, count, stride=8), :].astype(bf16)
            for lane in range(wide_ref.shape[0])
        ],
        axis=1,
    )


def routed(ids, x, zh, gain, table):
    hit = hits(ids)
    _, unit = unit_rows(x)
    normed = (unit * gain).astype(bf16)
    probs = choice(normed, table, hit)
    pick = picks(iota((SLOTS, EXPERTS), 0) // MOST, zh)
    slot = (iota((SLOTS, TOK), 0) % MOST + 1).astype(f32)
    return normed, probs, pick, marks(dot(pick, ranked(hit)) == slot)


def mixed_by(onehot, pick, probs):
    return onehot * dot(pick, probs.astype(bf16)).astype(bf16)


def loop(count, step):
    def turn(i, carry):
        step(i)
        return carry

    lax.fori_loop(0, count, turn, 0)


def columns(j, width):
    return pl.ds(pl.multiple_of(j * width, width), width)


def fill_looped(wide_ref, area, onehot_ref, rows_ref):
    def step(j):
        put_rows(wide_ref, j, dot(onehot_ref[...], rows_ref[:, columns(j, 256)]), area * AREA)

    loop(8, step)


def fill(wide_ref, area, onehot, rows_ref):
    for j in range(8):
        put_rows(wide_ref, j, dot(onehot, rows_ref[:, pl.ds(j * 256, 256)]), area * AREA)


def give(wide_ref, sent_ref, areas):
    def step(d, rows):
        for area in range(areas):
            for lane in range(2):
                sent_ref[d, pl.ds(area * ROWS, ROWS), LANES[lane]] = wide_ref[lane, area_rows(d, area), :].astype(bf16)

    each_peer(step)


def near_pack(
    zh_ref, ids_ref, ahead_ids_ref, x_ref, g_ref, resid_ref, gain_ref, table_ref,
    sent_ref, normed_ref, onehot_ref, probs_ref, mix_ref, wide_ref, rows_ref
):
    zh, gain, table = zh_ref[0], gain_ref[...], table_ref[...]
    normed_ref[...], probs_ref[...], _, onehot_ref[...] = routed(ids_ref[...], x_ref[...], zh, gain, table)
    fill(wide_ref, 0, onehot_ref[...], normed_ref)
    fill(wide_ref, 1, onehot_ref[...], g_ref)
    rows_ref[...], probs, pick, onehot = routed(ahead_ids_ref[...], resid_ref[...], zh, gain, table)
    mix_ref[...] = mixed_by(onehot, pick, probs)
    fill(wide_ref, 2, onehot, rows_ref)
    give(wide_ref, sent_ref, 3)


def run_near_pack(*args):
    return call(
        near_pack,
        (
            shape((PEERS, 3 * ROWS, 256)),
            shape((TOK, D)),
            shape((SLOTS, TOK)),
            shape((EXPERTS, TOK), f32),
            shape((SLOTS, TOK)),
        ),
        [SMEM] + [VMEM] * 7,
        [pltpu.VMEM((2, 3 * AREA, 128), f32), pltpu.VMEM((TOK, D), bf16)],
        args,
        2 * 10**9,
        8,
    )


def far_pack(
    zh_ref, ids_ref, x_ref, g_ref, gain_ref, table_ref, sent_ref, normed_ref, onehot_ref, probs_ref, wide_ref
):
    normed_ref[...], probs_ref[...], _, onehot_ref[...] = routed(
        ids_ref[...], x_ref[...], zh_ref[0], gain_ref[...], table_ref[...]
    )
    fill(wide_ref, 0, onehot_ref[...], normed_ref)
    fill(wide_ref, 1, onehot_ref[...], g_ref)
    give(wide_ref, sent_ref, 2)


def run_far_pack(*args):
    return call(
        far_pack,
        (shape((PEERS, 2 * ROWS, 256)), shape((TOK, D)), shape((SLOTS, TOK)), shape((EXPERTS, TOK), f32)),
        [SMEM] + [VMEM] * 5,
        [pltpu.VMEM((2, 2 * AREA, 128), f32)],
        args,
        10**9,
        6,
    )


def ahead_pack(zh_ref, ids_ref, x_ref, gain_ref, table_ref, sent_ref, mix_ref, wide_ref, rows_ref, onehot_ref):
    rows_ref[...], probs, pick, onehot = routed(ids_ref[...], x_ref[...], zh_ref[0], gain_ref[...], table_ref[...])
    mix_ref[...] = mixed_by(onehot, pick, probs)
    onehot_ref[...] = onehot
    fill_looped(wide_ref, 0, onehot_ref, rows_ref)
    give(wide_ref, sent_ref, 1)


def run_ahead_pack(*args):
    return call(
        ahead_pack,
        (shape((PEERS, ROWS, 256)), shape((SLOTS, TOK))),
        [SMEM] + [VMEM] * 4,
        [pltpu.VMEM((2, AREA, 128), f32), pltpu.VMEM((TOK, D), bf16), pltpu.VMEM((SLOTS, TOK), bf16)],
        args,
        10**9,
        4,
    )


def fetched(pairs, sems):
    copies = [pltpu.make_async_copy(a, b, sems.at[i]) for i, (a, b) in enumerate(pairs)]
    for copy in copies:
        copy.start()
    return copies


def expert_slopes(gate_pre, up_pre, down_grad, gate_grad, up_grad):
    sig = 1.0 / (1.0 + jnp.exp(-gate_pre))
    act = gate_pre * sig
    hidden = (act * up_pre).astype(bf16).astype(f32)
    gate_grad[...] = (down_grad * up_pre * sig * (1.0 + gate_pre * (1.0 - sig))).astype(bf16)
    up_grad[...] = (down_grad * act).astype(bf16)
    return jnp.sum(hidden * down_grad, axis=-1, keepdims=True).astype(bf16).astype(f32)


def small_grads(grads, place):
    p, lane = iota((SLOTS, 128), 0), iota((SLOTS, 128), 1)
    gather = marks(iota((PEERS * 8, SLOTS), 1) // MOST == iota((PEERS * 8, SLOTS), 0) // 8)
    spread = jnp.where(lane == p % MOST + place * MOST, grads, 0.0)
    return dot(gather, spread.astype(bf16))


def behind_half(got_ref, weights, place, wide_ref, sems, gate_grad, up_grad):
    (gate_hbm, gate_ref), (up_hbm, up_ref), (down_hbm, down_ref) = weights
    copies = fetched(weights, sems)

    def take(d, rows):
        for lane in range(2):
            for kind in range(2):
                wide_ref[lane, area_rows(d, kind), :] = got_ref[d, pl.ds(kind * ROWS, ROWS), LANES[lane]].astype(f32)

    each_peer(take)
    copies[0].wait()
    copies[1].wait()
    gate_pre, up_pre = jnp.zeros((SLOTS, FF), f32), jnp.zeros((SLOTS, FF), f32)
    for j in range(4):
        rows = jnp.concatenate([get_rows(wide_ref, 2 * j + i, SLOTS) for i in range(2)], axis=1)
        gate_pre = gate_pre + dot(rows, gate_ref[pl.ds(j * 512, 512), :])
        up_pre = up_pre + dot(rows, up_ref[pl.ds(j * 512, 512), :])
    copies[2].wait()
    down_grad = jnp.zeros((SLOTS, FF), f32)
    for j in range(4):
        rows = jnp.concatenate([get_rows(wide_ref, 2 * j + i, SLOTS, AREA) for i in range(2)], axis=1)
        down_grad = down_grad + dot(rows, down_ref[:, pl.ds(j * 512, 512)], ACROSS)
    grads = expert_slopes(gate_pre, up_pre, down_grad, gate_grad, up_grad)
    for j in range(8):
        part = pl.ds(j * 256, 256)
        rows = dot(gate_grad[...], gate_ref[part, :], ACROSS) + dot(up_grad[...], up_ref[part, :], ACROSS)
        put_rows(wide_ref, j, rows)
    return small_grads(grads, place)


def near_experts(
    got_ref, gate_hbm, up_hbm, down_hbm, back_ref, small_ref, wide_ref, gate_ref, up_ref, down_ref, sems,
    gate_sum, up_sum, down_sum, gate_grad, up_grad
):
    copies = fetched(((gate_hbm, gate_ref), (up_hbm, up_ref), (down_hbm, down_ref)), sems)

    def take(d, rows):
        for lane in range(2):
            for kind in range(2):
                wide_ref[lane, area_rows(d, kind), :] = got_ref[d, pl.ds(kind * ROWS, ROWS), LANES[lane]].astype(f32)

    each_peer(take)
    for ref in (gate_sum, up_sum, down_sum):
        ref[...] = jnp.zeros((SLOTS, FF), f32)
    for copy in copies:
        copy.wait()

    def inward(j):
        rows = jnp.concatenate([get_rows(wide_ref, 2 * j + i, SLOTS) for i in range(2)], axis=1)
        gate_sum[...] += dot(rows, gate_ref[columns(j, 512), :])
        up_sum[...] += dot(rows, up_ref[columns(j, 512), :])
        rows = jnp.concatenate([get_rows(wide_ref, 2 * j + i, SLOTS, AREA) for i in range(2)], axis=1)
        down_sum[...] += dot(rows, down_ref[:, columns(j, 512)], ACROSS)

    loop(4, inward)
    grads = expert_slopes(gate_sum[...], up_sum[...], down_sum[...], gate_grad, up_grad)

    def outward(j):
        part = columns(j, 256)
        rows = dot(gate_grad[...], gate_ref[part, :], ACROSS) + dot(up_grad[...], up_ref[part, :], ACROSS)
        put_rows(wide_ref, j, rows)

    loop(8, outward)
    small_ref[...] = small_grads(grads, 0)

    def put(d, rows):
        for lane in range(2):
            back_ref[d, :, LANES[lane]] = wide_ref[lane, rows, :].astype(bf16)

    each_peer(put)


def far_experts(
    got_ref, near_ref, near_small_ref, gate_hbm, up_hbm, down_hbm, back_ref, wide_ref, gate_ref, up_ref, down_ref, sems,
    gate_grad, up_grad
):
    weights = ((gate_hbm, gate_ref), (up_hbm, up_ref), (down_hbm, down_ref))
    small = behind_half(got_ref, weights, 1, wide_ref, sems, gate_grad, up_grad) + near_small_ref[...]
    wide_ref[0, pl.ds(AREA, PEERS * 8), :] = small

    def put(d, rows):
        for lane in range(2):
            back_ref[d, pl.ds(0, ROWS), LANES[lane]] = near_ref[d, :, LANES[lane]]
            back_ref[d, pl.ds(ROWS, ROWS), LANES[lane]] = wide_ref[lane, rows, :].astype(bf16)
        extra = wide_ref[0, pl.ds(pl.multiple_of(AREA + d * 8, 8), 8), :].astype(bf16)
        back_ref[d, pl.ds(2 * ROWS, 8), LANES[0]] = extra
        back_ref[d, pl.ds(2 * ROWS, 8), LANES[1]] = extra

    each_peer(put)


GRADS = [pltpu.VMEM((SLOTS, FF), bf16)] * 2
WEIGHTS = [
    pltpu.VMEM((D, FF), bf16),
    pltpu.VMEM((D, FF), bf16),
    pltpu.VMEM((FF, D), bf16),
    pltpu.SemaphoreType.DMA((3,)),
]


def run_near_experts(*args):
    return call(
        near_experts,
        (shape((PEERS, ROWS, 256)), shape((PEERS * 8, 128), f32)),
        [VMEM] + [HBM] * 3,
        [pltpu.VMEM((2, 2 * AREA, 128), f32)] + WEIGHTS + [pltpu.VMEM((SLOTS, FF), f32)] * 3 + GRADS,
        args,
        5 * 10**9,
        13,
    )


def run_far_experts(*args):
    return call(
        far_experts,
        (shape((PEERS, 2 * ROWS + 8, 256)),),
        [VMEM] * 3 + [HBM] * 3,
        [pltpu.VMEM((2, 2 * AREA, 128), f32)] + WEIGHTS + GRADS,
        args,
        5 * 10**9,
        15,
    )[0]


def ahead_experts(
    near_ref, far_ref, gate_hbm, up_hbm, down_hbm, first_ref, second_ref, wide_ref, gate_ref, up_ref, down_ref, sems,
    gate_sum, up_sum, hidden_ref
):
    copies = fetched(((gate_hbm, gate_ref), (up_hbm, up_ref), (down_hbm, down_ref)), sems)
    count = 2 * SLOTS

    def take(d, rows):
        for lane in range(2):
            wide_ref[lane, area_rows(d, 0), :] = near_ref[d, pl.ds(2 * ROWS, ROWS), LANES[lane]].astype(f32)
            wide_ref[lane, area_rows(d, 1), :] = far_ref[d, :, LANES[lane]].astype(f32)

    each_peer(take)
    copies[0].wait()
    copies[1].wait()
    gate_sum[...] = jnp.zeros((count, FF), f32)
    up_sum[...] = jnp.zeros((count, FF), f32)

    def inward(j):
        rows = jnp.concatenate([get_rows(wide_ref, 2 * j, count), get_rows(wide_ref, 2 * j + 1, count)], axis=1)
        gate_sum[...] += dot(rows, gate_ref[columns(j, 512), :])
        up_sum[...] += dot(rows, up_ref[columns(j, 512), :])

    loop(4, inward)
    gate_pre = gate_sum[...]
    hidden_ref[...] = (gate_pre / (1.0 + jnp.exp(-gate_pre)) * up_sum[...]).astype(bf16)
    copies[2].wait()

    def outward(c):
        for part in range(2):
            made = dot(hidden_ref[...], down_ref[:, columns(part * 4 + c, 256)])
            for i in range(2):
                wide_ref[part, pl.ds(2 * c + i, count, stride=8), :] = made[:, i * 128 : i * 128 + 128]

    loop(4, outward)

    def put(d, rows):
        for half in range(2):
            first_ref[d, pl.ds(half * ROWS, ROWS), :] = wide_ref[0, area_rows(d, half), :].astype(bf16)
            second_ref[d, pl.ds(half * ROWS, ROWS), :] = wide_ref[1, area_rows(d, half), :].astype(bf16)

    each_peer(put)


def run_ahead_experts(*args):
    return call(
        ahead_experts,
        (shape((PEERS, 2 * ROWS, 128)), shape((PEERS, 2 * ROWS, 128))),
        [VMEM] * 2 + [HBM] * 3,
        [pltpu.VMEM((2, 2 * AREA, 128), f32)]
        + WEIGHTS
        + [pltpu.VMEM((2 * SLOTS, FF), f32), pltpu.VMEM((2 * SLOTS, FF), f32), pltpu.VMEM((2 * SLOTS, FF), bf16)],
        args,
        6 * 10**9,
        14,
    )


def attend(length_ref, x_ref, q_ref, kc_ref, kn_ref, vc_ref, vn_ref, resid_ref):
    length = length_ref[0, 0]
    row, col = iota((TOK, 2 * TOK), 0), iota((TOK, 2 * TOK), 1)
    visible = ((col < TOK) & (col < length)) | ((col >= TOK) & (col - TOK <= row))
    for kv in range(KV_HEADS):
        part = pl.ds(kv * HEAD_DIM, HEAD_DIM)
        keys = jnp.concatenate([kc_ref[:, part], kn_ref[:, part]], axis=0)
        values = jnp.concatenate([vc_ref[:, part], vn_ref[:, part]], axis=0)
        for h in range(HEADS // KV_HEADS):
            cols = pl.ds((kv * (HEADS // KV_HEADS) + h) * HEAD_DIM, HEAD_DIM)
            scores = dot(q_ref[:, cols], keys, ACROSS) * HEAD_DIM ** (-0.5)
            scores = jnp.where(visible, scores, far_below)
            lifted = jnp.exp(scores - jnp.max(scores, axis=-1, keepdims=True))
            weights = (lifted * (1.0 / jnp.sum(lifted, axis=-1, keepdims=True))).astype(bf16)
            mixed = dot(weights, values).astype(bf16)
            resid_ref[:, cols] = (x_ref[:, cols].astype(f32) + mixed.astype(f32)).astype(bf16)


def run_attend(length, x, q, kc, kn, vc, vn):
    return call(
        attend,
        (shape((TOK, D)),),
        [SMEM] + [VMEM] * 6,
        [],
        (length, x, q, kc, kn, vc, vn),
        3 * 10**9,
        8,
    )[0]


def through_norm(sums, gain, inv, unit):
    scaled = sums * gain
    return inv * (scaled - unit * jnp.mean(scaled * unit, axis=-1, keepdims=True))


def behind_note(zh_ref, home_ref, near_hot_ref, far_hot_ref, note_ref):
    pick = picks(iota((SLOTS, EXPERTS), 0) // MOST, zh_ref[0]).astype(f32)
    small = jnp.concatenate([home_ref[d].astype(f32) for d in range(PEERS)], axis=0)[:, :128].astype(bf16)
    share = marks(iota((SLOTS, PEERS * 8), 0) // MOST * 8 == iota((SLOTS, PEERS * 8), 1))
    small = dot(share, small)
    p, lane = iota((SLOTS, 128), 0) % MOST, iota((SLOTS, 128), 1)
    for half, hot in enumerate((near_hot_ref, far_hot_ref)):
        grads = jnp.sum(jnp.where(lane == p + half * MOST, small, 0.0), axis=-1, keepdims=True)
        note_ref[:, pl.ds(half * TOK, TOK)] = dot((pick * grads).astype(bf16), hot[...], DOWN)


def whole(a):
    return pl.BlockSpec(a.shape, lambda i, n=a.ndim: (0,) * n)


def run_behind_note(zh, home, near_hot, far_hot):
    tail = pl.BlockSpec((PEERS, 8, 256), lambda i: (0, 2 * ROWS // 8, 0))
    return pl.pallas_call(
        behind_note,
        grid=(1,),
        out_shape=shape((EXPERTS, 2 * TOK), f32),
        in_specs=[SMEM, tail, whole(near_hot), whole(far_hot)],
        out_specs=pl.BlockSpec((EXPERTS, 2 * TOK), lambda i: (0, 0)),
        compiler_params=pltpu.CompilerParams(vmem_limit_bytes=63 * 2**20),
        cost_estimate=pl.CostEstimate(flops=10**7, transcendentals=0, bytes_accessed=2**18),
    )(zh, home, near_hot, far_hot)


def behind_sums(
    zh_ref, home_ref, near_hot_ref, far_hot_ref, near_probs_ref, far_probs_ref, near_x_ref, far_x_ref, gain_ref,
    sums_ref, sent_ref, theirs_ref, mine_ref, wide_ref, line_ref, mix_ref
):
    zh = zh_ref[0]

    def take(d, rows):
        for half in range(2):
            for lane in range(2):
                wide_ref[lane, area_rows(d, half), :] = home_ref[d, pl.ds(half * ROWS, ROWS), LANES[lane]].astype(f32)

    each_peer(take)
    pick = picks(iota((SLOTS, EXPERTS), 0) // MOST, zh)
    mix_ref[0] = mixed_by(near_hot_ref[...], pick, near_probs_ref[...])
    mix_ref[1] = mixed_by(far_hot_ref[...], pick, far_probs_ref[...])

    for j in range(8):
        cols = pl.ds(j * 256, 256)
        sums_ref[:, cols] = dot(mix_ref[0], get_rows(wide_ref, j, SLOTS), DOWN)
        line_ref[:, cols] = dot(mix_ref[1], get_rows(wide_ref, j, SLOTS, AREA), DOWN)
    inv, unit = unit_rows(far_x_ref[...])
    sums = line_ref[...]
    sent_ref[...] = through_norm(sums, gain_ref[...], inv, unit).astype(bf16)
    total = jnp.sum(sums * unit, axis=0, keepdims=True)
    _, unit = unit_rows(near_x_ref[...])
    total = total + jnp.sum(sums_ref[...] * unit, axis=0, keepdims=True)
    theirs_ref[...] = jnp.zeros((8, 256), f32)
    mine_ref[...] = jnp.zeros((8, 256), f32)
    for x in range(4):
        first, second = total[:, x * 512 : x * 512 + 256], total[:, x * 512 + 256 : x * 512 + 512]
        mine_ref[pl.ds(x, 1), :] = jnp.where(zh == 0, first, second)
        theirs_ref[pl.ds(x, 1), :] = jnp.where(zh == 0, second, first)


def run_behind_sums(*args):
    return call(
        behind_sums,
        (shape((TOK, D), f32), shape((TOK, D)), shape((8, 256), f32), shape((8, 256), f32)),
        [SMEM] + [VMEM] * 8,
        [
            pltpu.VMEM((2, 2 * AREA, 128), f32),
            pltpu.VMEM((TOK, D), f32),
            pltpu.VMEM((2, SLOTS, TOK), bf16),
        ],
        args,
        10**9,
        6,
    )


def behind_end(
    near_note_ref, far_note_ref, sums_ref, near_probs_ref, far_probs_ref, x_ref, g_ref, gain_ref, table_ref,
    sent_ref, near_logit_ref, far_logit_ref
):
    near_tok, far_tok = pl.ds(0, TOK), pl.ds(TOK, TOK)

    def logit_grads(probs, grads):
        return (probs * (grads - jnp.sum(probs * grads, axis=0, keepdims=True))).astype(bf16)

    near_logit_ref[...] = logit_grads(near_probs_ref[...], near_note_ref[:, near_tok] + far_note_ref[:, far_tok])
    far_logit_ref[...] = logit_grads(far_probs_ref[...], near_note_ref[:, far_tok] + far_note_ref[:, near_tok])
    inv, unit = unit_rows(x_ref[...])
    sums = sums_ref[...] + dot(near_logit_ref[...], table_ref[...], DOWN)
    sent_ref[...] = (g_ref[...].astype(f32) + through_norm(sums, gain_ref[...], inv, unit)).astype(bf16)


def run_behind_end(*args):
    return call(
        behind_end,
        (shape((TOK, D)), shape((EXPERTS, TOK)), shape((EXPERTS, TOK))),
        [VMEM] * 9,
        [],
        args,
        10**9,
        4,
    )


def share_parts(
    zh_ref, near_logit_ref, far_logit_ref, mine_ref, theirs_ref, near_normed_ref, far_normed_ref, near_x_ref,
    far_x_ref, table_ref, shares_ref
):
    zh = zh_ref[0]
    near_logit, far_logit = near_logit_ref[...], far_logit_ref[...]
    _, near_unit = unit_rows(near_x_ref[...])
    _, far_unit = unit_rows(far_x_ref[...])
    near_term, far_term = dot(near_logit, table_ref[...], DOWN), dot(far_logit, table_ref[...], DOWN)
    total = jnp.sum(near_term * near_unit + far_term * far_unit, axis=0, keepdims=True)
    row = iota((128 - EXPERTS, 256), 0)
    for x in range(4):
        first, second = total[:, x * 512 : x * 512 + 256], total[:, x * 512 + 256 : x * 512 + 512]
        gains = jnp.where(zh == 0, first, second) + mine_ref[pl.ds(x, 1), :] + theirs_ref[pl.ds(x, 1), :]
        cols = pl.ds(pl.multiple_of(x * 512 + zh * 256, 256), 256)
        part = dot(near_logit, near_normed_ref[:, cols]) + dot(far_logit, far_normed_ref[:, cols])
        both = jnp.concatenate([part, jnp.where(row == 0, gains, 0.0)], axis=0)
        shares_ref[pl.ds(x * 256, 256), :] = both.T.astype(bf16)


def run_share_parts(*args):
    return call(share_parts, (shape((D // 2, 128)),), [SMEM] + [VMEM] * 9, [], args, 10**9, 3)[0]


def ahead_end(home_ref, near_mix_ref, far_mix_ref, resid_ref, near_ref, far_ref, wide_ref):
    def take(d, rows):
        for half in range(2):
            wide_ref[0, area_rows(d, half), :] = home_ref[d, pl.ds(half * ROWS, ROWS), :].astype(f32)

    each_peer(take)
    for c in range(4):
        cols = pl.ds(c * 256, 256)
        for half, (mix_ref, out_ref) in enumerate(((near_mix_ref, near_ref), (far_mix_ref, far_ref))):
            rows = jnp.concatenate([get_rows(wide_ref, 2 * c + i, SLOTS, half * AREA) for i in range(2)], axis=1)
            sums = dot(mix_ref[...], rows, DOWN)
            if half == 0:
                sums = sums + resid_ref[:, cols].astype(f32)
            out_ref[:, cols] = sums.astype(bf16)


def run_ahead_end(home, near_mix, far_mix, resid, part):
    columns = pl.BlockSpec((TOK, D // 2), lambda i: (0, part))
    whole = [pl.BlockSpec(a.shape, lambda i, n=a.ndim: (0,) * n) for a in (home, near_mix, far_mix)]
    half = pl.BlockSpec((TOK, D // 2), lambda i: (0, 0))
    return pl.pallas_call(
        ahead_end,
        grid=(1,),
        out_shape=(shape((TOK, D // 2)), shape((TOK, D // 2))),
        in_specs=whole + [columns],
        out_specs=(half, half),
        scratch_shapes=[pltpu.VMEM((1, 2 * AREA, 128), f32)],
        compiler_params=pltpu.CompilerParams(vmem_limit_bytes=63 * 2**20),
        cost_estimate=pl.CostEstimate(flops=10**9, transcendentals=0, bytes_accessed=3 * 2**20),
    )(home, near_mix, far_mix, resid)


def final_add(a_ref, b_ref, c_ref, d_ref, out_ref):
    half = D // 2
    out_ref[:, pl.ds(0, half)] = (a_ref[...].astype(f32) + b_ref[...].astype(f32)).astype(bf16)
    out_ref[:, pl.ds(half, half)] = (c_ref[...].astype(f32) + d_ref[...].astype(f32)).astype(bf16)


def run_final_add(*args):
    return call(final_add, (shape((TOK, D)),), [VMEM] * 4, [], args, 10**6, 2)[0]


def share_sums(got_ref, router_ref, gain_ref):
    total = got_ref[0].astype(f32)
    for source in range(1, PEERS):
        total = total + got_ref[source].astype(f32)
    total = total * factor
    router_ref[...] = total[:, :EXPERTS]
    gain_ref[...] = total.T[EXPERTS : EXPERTS + 1, :]


def run_share_sums(got):
    return call(
        share_sums, (shape((PEERS, EXPERTS), f32), shape((1, PEERS), f32)), [VMEM], [], (got,), 10**6, 1
    )


def body(
    forward_input,
    queries,
    new_keys,
    new_values,
    cache_keys,
    cache_values,
    context_lengths,
    norm_gain,
    router,
    gate_weight,
    up_weight,
    down_weight,
    forward_ids,
    backward_input,
    backward_ids,
    output_grad,
):
    zh = lax.axis_index("zh").astype(jnp.int32).reshape(1)
    gain = norm_gain
    table = router[0].T
    weights = (gate_weight[0, 0], up_weight[0, 0], down_weight[0, 0])
    back_x, back_g = backward_input[0], output_grad[0]
    ids_b, ids_f = backward_ids[0].T, forward_ids[0].T
    ids_far = swapped(jnp.concatenate([ids_b, ids_f], axis=0))
    x_far = swapped(back_x)
    g_far = swapped(back_g)
    resid = run_attend(
        context_lengths,
        forward_input[0],
        queries[0],
        cache_keys[0],
        new_keys[0],
        cache_values[0],
        new_values[0],
    )
    resid_far = swapped(resid)
    sent_1, normed_b, hot_b, probs_b, mix_f = run_near_pack(
        zh, ids_b, ids_f, back_x, back_g, resid, gain, table
    )
    got_1 = spread_out(sent_1)
    sent_2, normed_c, hot_c, probs_c = run_far_pack(zh, ids_far[:4], x_far, g_far, gain, table)
    sent_2, _ = lax.optimization_barrier((sent_2, got_1))
    got_2 = spread_out(sent_2)
    sent_3, mix_h = run_ahead_pack(zh, ids_far[4:], resid_far, gain, table)
    sent_3, got_2 = lax.optimization_barrier((sent_3, got_2))
    got_3 = spread_out(sent_3)
    back_b, small_b = run_near_experts(got_1, *weights)
    back = run_far_experts(got_2, back_b, small_b, *weights)
    back, got_3 = lax.optimization_barrier((back, got_3))
    home_b = spread_out(back)
    made_1, made_2 = run_ahead_experts(got_1, got_3, *weights)
    made_1, home_b = lax.optimization_barrier((made_1, home_b))
    home_1 = spread_out(made_1)
    made_2, home_1 = lax.optimization_barrier((made_2, home_1))
    home_2 = spread_out(made_2)
    note = run_behind_note(zh, home_b, hot_b, hot_c)
    far_note = swapped(note)
    sums_b, own_c, theirs, mine = run_behind_sums(
        zh, home_b, hot_b, hot_c, probs_b, probs_c, back_x, x_far, gain
    )
    moved_c = moved(own_c, False, -1)
    own_b, logit_b, logit_c = run_behind_end(
        note, far_note, sums_b, probs_b, probs_c, back_x, back_g, gain, table
    )
    moved_b = moved(own_b, True, -1)
    own_f1, own_h1 = run_ahead_end(home_1, mix_f, mix_h, resid, 0)
    moved_h1 = moved(own_h1, False, 1)
    moved_f1 = moved(own_f1, True, 1)
    theirs = swapped(theirs)
    shares = run_share_parts(
        zh, logit_b, logit_c, mine, theirs, normed_b, normed_c, back_x, x_far, table
    )
    own_f2, own_h2 = run_ahead_end(home_2, mix_f, mix_h, resid, 1)
    moved_h2 = moved(own_h2, False, 1)
    moved_f2 = moved(own_f2, True, 1)
    shares, own_f2 = lax.optimization_barrier((shares, own_f2))
    got_s = spread_out(shares.reshape(PEERS, PEERS, 128))
    router_grad, gain_grad = run_share_sums(got_s)
    input_grad = (moved_b.astype(f32) + moved_c.astype(f32)).astype(bf16)
    forward_output = run_final_add(moved_f1, moved_h1, moved_f2, moved_h2)
    return forward_output[None], input_grad[None], router_grad[None], gain_grad


def solution(mesh):
    grid = Mesh(mesh.devices.reshape(4, 4, 2, 4, 2), ("pipe", "x", "zh", "y", "core"))
    rows = P("pipe", ALL, None)
    placed = (
        rows,
        rows,
        rows,
        rows,
        rows,
        rows,
        P("pipe", ALL),
        P("pipe", None),
        P("pipe", None, None),
        P("pipe", ALL, None, None),
        P("pipe", ALL, None, None),
        P("pipe", ALL, None, None),
        rows,
        rows,
        rows,
        rows,
    )
    return jax.shard_map(
        body,
        mesh=grid,
        in_specs=placed,
        out_specs=(rows, rows, rows, P("pipe", ALL)),
        check_vma=False,
    )
```
